32 devices in a mesh: fsdp: 4 (over z), ctx: 2 (over x), tp: 4 (over y, core).
Axes of the slice: x: 2, y: 2, z: 4, core: 2. Of those that a mesh axis runs over, the one named last changes fastest.
Arguments:
- layer_in: bfloat16 [16384, 768], P(('fsdp', 'ctx')), may hold values from -6 to 6
- cotangent: bfloat16 [16384, 768], P(('fsdp', 'ctx')), may hold values from -6 to 6
- lengths: int32 [4], P('fsdp'), may hold values from 1024 to 4096, as said below
- rand_blocks: int32 [4, 64, 3], P('fsdp', 'ctx'), may hold values from 2 to 63, as said below
- w_query: bfloat16 [768, 768], P('fsdp', 'tp'), may hold values from -0.21875 to 0.21875
- b_query: bfloat16 [768], P(('tp', 'fsdp')), may hold values from -0.625 to 0.625
- w_key: bfloat16 [768, 768], P('fsdp', 'tp'), may hold values from -0.21875 to 0.21875
- w_value: bfloat16 [768, 768], P('fsdp', 'tp'), may hold values from -0.21875 to 0.21875
- b_value: bfloat16 [768], P(('tp', 'fsdp')), may hold values from -0.3125 to 0.3125
- w_proj: bfloat16 [768, 768], P('tp', 'fsdp'), may hold values from -1.5 to 1.5
- b_proj: bfloat16 [768], P('fsdp'), may hold values from -0.625 to 0.625
- gain_one: bfloat16 [768], P('fsdp'), may hold values from 0.5 to 1.5
- shift_one: bfloat16 [768], P('fsdp'), may hold values from -0.625 to 0.625
- w_in: bfloat16 [768, 3072], P('fsdp', 'tp'), may hold values from -0.21875 to 0.21875
- b_in: bfloat16 [3072], P(('tp', 'fsdp')), may hold values from -0.625 to 0.625
- w_out: bfloat16 [3072, 768], P('tp', 'fsdp'), may hold values from -0.109375 to 0.109375
- b_out: bfloat16 [768], P('fsdp'), may hold values from -0.625 to 0.625
- gain_two: bfloat16 [768], P('fsdp'), may hold values from 0.5 to 1.5
- shift_two: bfloat16 [768], P('fsdp'), may hold values from -0.625 to 0.625
Outputs:
- layer_out: bfloat16 [16384, 768], P(('fsdp', 'ctx'))
- grad_input: bfloat16 [16384, 768], P(('fsdp', 'ctx'))
- dw_query: float32 [768, 768], P('fsdp', 'tp')
- db_query: float32 [768], P(('tp', 'fsdp'))
- dw_key: float32 [768, 768], P('fsdp', 'tp')
- dw_value: float32 [768, 768], P('fsdp', 'tp')
- db_value: float32 [768], P(('tp', 'fsdp'))
- dw_proj: float32 [768, 768], P('tp', 'fsdp')
- db_proj: float32 [768], P('fsdp')
- dgain_one: float32 [768], P('fsdp')
- dshift_one: float32 [768], P('fsdp')
- dw_in: float32 [768, 3072], P('fsdp', 'tp')
- db_in: float32 [3072], P(('tp', 'fsdp'))
- dw_out: float32 [3072, 768], P('tp', 'fsdp')
- db_out: float32 [768], P('fsdp')
- dgain_two: float32 [768], P('fsdp')
- dshift_two: float32 [768], P('fsdp')
The draws below stay inside these ranges and needn't reach their ends.
Inputs may be any that keep to these rules, and one draw needn't show every extreme that they name: `lengths`: some sequence has 4096 live tokens and some has 1024. For sequence s and query block i, rand_blocks[s, i, :] are 3 different block numbers, none under 2 and none within one of i. Rows i < 2 are drawn alike and not read.
All inputs are finite; a program needn't handle non-finite values.
Results may differ from the reference program's by a relative error of at most 0.02.
Values may be sent and summed in bfloat16 or wider, within the bound.
No kernel may reach another device: no remote copies, remote signals or barrier semaphores. Data moves between devices by JAX's collectives and lax.ppermute only.
A program may use at most 320 MiB of HBM per device.

```python
import math
import jax
import jax.numpy as jnp
from jax import lax

D = 768
HEADS = 12
HEAD_DIM = 64
FF = 3072
BLK = 64
GLOBAL_BLOCKS = 2
RANDOM_BLOCKS = 3
SEQ = 4096
NB = 64
SEQS = 4
TOKENS = 16384


def draw_lengths(key, part):
    low_len = SEQ // 4
    drawn = jax.random.randint(key, (SEQS,), low_len, SEQ + 1, dtype=jnp.int32)
    picked = jax.random.permutation(jax.random.fold_in(key, 7), SEQS)
    drawn = drawn.at[picked[0]].set(SEQ)
    drawn = drawn.at[picked[1]].set(low_len)
    return drawn.astype(jnp.int32)


def draw_rand_blocks(key, part):
    drawn = jax.random.randint(key, (SEQS, NB, NB), 0, 1 << 20, dtype=jnp.int32)
    columns = jnp.arange(NB, dtype=jnp.int32)
    scores = drawn * NB + columns[None, None, :]
    blocked = (columns[None, :] < GLOBAL_BLOCKS) | (jnp.abs(columns[:, None] - columns[None, :]) <= 1)
    scores = jnp.where(blocked[None, :, :], -1, scores)
    picked = lax.top_k(scores, RANDOM_BLOCKS)[1]
    return picked.astype(jnp.int32)


def level_of(key, extent, cuts, smallest, top_value):
    factor_of, own = 1.0, jax.random.fold_in(key, 6)
    for position, parts in cuts:
        steps = jnp.exp(jax.random.uniform(jax.random.fold_in(own, position), (parts,), jnp.float32, smallest / len(cuts), top_value / len(cuts)))
        factor_of = factor_of * jnp.repeat(steps, extent[position] // parts).reshape([-1 if axis == position else 1 for axis in range(len(extent))])
    return factor_of


def scatter_about(key, dims, width, reach, split=(), kind=jnp.bfloat16):
    level = level_of(key, dims, split, -0.22, 0.18) if split else 1.0
    values = jax.random.normal(key, dims, jnp.float32) * width * level
    return jnp.minimum(jnp.maximum(values, -reach), reach).astype(kind)


def setup_inputs(seed: int = 0) -> dict:
    streams_of = jax.random.split(jax.random.key(seed), 20)
    return {
        "layer_in": scatter_about(streams_of[0], (TOKENS, D), 1.0, 6.0, ((0, 8),)),
        "cotangent": scatter_about(streams_of[1], (TOKENS, D), 1.0, 6.0, ((0, 8),)),
        "lengths": draw_lengths(jax.random.fold_in(streams_of[19], 71), 0),
        "rand_blocks": draw_rand_blocks(jax.random.fold_in(streams_of[19], 71), 0),
        "w_query": scatter_about(streams_of[4], (D, D), D ** -0.5, 0.21875, ((0, 4), (1, 4))),
        "b_query": scatter_about(streams_of[5], (D,), 0.1, 0.625, ((0, 16),)),
        "w_key": scatter_about(streams_of[6], (D, D), D ** -0.5, 0.21875, ((0, 4), (1, 4))),
        "w_value": scatter_about(streams_of[7], (D, D), D ** -0.5, 0.21875, ((0, 4), (1, 4))),
        "b_value": scatter_about(streams_of[8], (D,), 0.05, 0.3125, ((0, 16),)),
        "w_proj": scatter_about(streams_of[9], (D, D), 16 ** -0.5, 1.5, ((0, 4), (1, 4))),
        "b_proj": scatter_about(streams_of[10], (D,), 0.1, 0.625, ((0, 4),)),
        "gain_one": jnp.clip(1.0 + 0.1 * jax.random.normal(streams_of[11], (D,), jnp.float32), 0.5, 1.5).astype(jnp.bfloat16),
        "shift_one": scatter_about(streams_of[12], (D,), 0.1, 0.625, ((0, 4),)),
        "w_in": scatter_about(streams_of[13], (D, FF), D ** -0.5, 0.21875, ((0, 4), (1, 4))),
        "b_in": scatter_about(streams_of[14], (FF,), 0.1, 0.625, ((0, 16),)),
        "w_out": scatter_about(streams_of[15], (FF, D), FF ** -0.5, 0.109375, ((0, 4), (1, 4))),
        "b_out": scatter_about(streams_of[16], (D,), 0.1, 0.625, ((0, 4),)),
        "gain_two": jnp.clip(1.0 + 0.1 * jax.random.normal(streams_of[17], (D,), jnp.float32), 0.5, 1.5).astype(jnp.bfloat16),
        "shift_two": scatter_about(streams_of[18], (D,), 0.1, 0.625, ((0, 4),)),
    }


EPSILON = 1e-05
MASKED = -1e+30
HIGHEST = lax.Precision.HIGHEST

@jax.custom_vjp
def low(v):
    return lax.optimization_barrier(v.astype(jnp.bfloat16)).astype(jnp.float32)

@jax.custom_vjp
def low_back(v):
    return v

def low_keep(v):
    return (low(v), None)

def low_pass(kept, grad):
    return (grad,)

def back_keep(v):
    return (v, None)

def back_low(kept, grad):
    return (low(grad),)
low.defvjp(low_keep, low_pass)
low_back.defvjp(back_keep, back_low)

def product(left_op, right_op):
    return jnp.dot(left_op, right_op, precision=HIGHEST, preferred_element_type=jnp.float32)

def layer_norm(values, gain_vec, shift_vec):
    center = lax.optimization_barrier(jnp.mean(values, axis=-1, keepdims=True))
    offset = values - center
    spread = lax.optimization_barrier(jnp.mean(offset * offset, axis=-1, keepdims=True))
    return offset * lax.rsqrt(spread + EPSILON) * gain_vec + shift_vec

def group_attend(queries, key_rows, values_in, allowed):
    factor = 1.0 / math.sqrt(HEAD_DIM)
    scores = jnp.einsum('qhd,khd->hqk', queries, key_rows, precision=HIGHEST) * factor
    scores = low_back(scores)
    scores = jnp.where(allowed[None, :, :], scores, MASKED)
    weights = jax.nn.softmax(scores, axis=-1)
    return jnp.einsum('hqk,khd->qhd', low(weights), values_in, precision=HIGHEST)

def attend_sequence(operands):
    queries, key_rows, values_in, picked, length = operands
    per_group = 8 if NB % 8 == 0 else 1
    groups_total = NB // per_group
    key_live = jnp.arange(SEQ, dtype=jnp.int32) < length
    columns = jnp.arange(NB, dtype=jnp.int32)
    attend = jax.checkpoint(group_attend)

    def one_group(pieces):
        rows_q, rand_rows, first_block = pieces
        row_blocks = first_block + jnp.arange(per_group, dtype=jnp.int32)
        near_band = jnp.abs(row_blocks[:, None] - columns[None, :]) <= 1
        global_band = (row_blocks[:, None] < GLOBAL_BLOCKS) | (columns[None, :] < GLOBAL_BLOCKS)
        chosen = jnp.any(rand_rows[:, :, None] == columns[None, None, :], axis=1)
        blocks_ok = near_band | global_band | chosen
        allowed = jnp.repeat(jnp.repeat(blocks_ok, BLK, axis=0), BLK, axis=1) & key_live[None, :]
        return attend(rows_q, key_rows, values_in, allowed)
    grouped = queries.reshape(groups_total, per_group * BLK, HEADS, HEAD_DIM)
    rand_grouped = picked.reshape(groups_total, per_group, RANDOM_BLOCKS)
    starts = jnp.arange(groups_total, dtype=jnp.int32) * per_group
    attended = lax.map(one_group, (grouped, rand_grouped, starts))
    return attended.reshape(SEQ, HEADS, HEAD_DIM)

def reference(layer_in, cotangent, lengths, rand_blocks, w_query, b_query, w_key, w_value, b_value, w_proj, b_proj, gain_one, shift_one, w_in, b_in, w_out, b_out, gain_two, shift_two):
    positions = jnp.arange(SEQ, dtype=jnp.int32)
    row_live = (positions[None, :] < lengths[:, None]).reshape(TOKENS, 1).astype(jnp.float32)

    def forward(inputs, wq_float, bq_float, wk_float, wv_float, bv_float, wp_float, bp_float, g1_float, s1_float, wi_float, bi_float, wo_float, bo_float, g2_float, s2_float):
        queries = low_back(low(product(inputs, wq_float) + bq_float))
        key_all = low_back(low(product(inputs, wk_float)))
        value_all = low_back(low(product(inputs, wv_float) + bv_float))
        shaped = (queries.reshape(SEQS, SEQ, HEADS, HEAD_DIM), key_all.reshape(SEQS, SEQ, HEADS, HEAD_DIM), value_all.reshape(SEQS, SEQ, HEADS, HEAD_DIM), rand_blocks, lengths)
        attended = lax.map(attend_sequence, shaped).reshape(TOKENS, D)
        heads_out = low_back(low(attended))
        branch = low_back(product(heads_out, wp_float) + bp_float)
        hidden = layer_norm(inputs + branch, g1_float, s1_float)
        hidden_low = low(hidden)
        pre_act = low_back(product(hidden_low, wi_float) + bi_float)
        act_low = low(jax.nn.gelu(pre_act, approximate=False))
        mlp_out = low_back(product(act_low, wo_float) + bo_float)
        return layer_norm(hidden + mlp_out, g2_float, s2_float) * row_live
    floats = (layer_in.astype(jnp.float32), w_query.astype(jnp.float32), b_query.astype(jnp.float32), w_key.astype(jnp.float32), w_value.astype(jnp.float32), b_value.astype(jnp.float32), w_proj.astype(jnp.float32), b_proj.astype(jnp.float32), gain_one.astype(jnp.float32), shift_one.astype(jnp.float32), w_in.astype(jnp.float32), b_in.astype(jnp.float32), w_out.astype(jnp.float32), b_out.astype(jnp.float32), gain_two.astype(jnp.float32), shift_two.astype(jnp.float32))
    result, pullback = jax.vjp(forward, *floats)
    grads = pullback(cotangent.astype(jnp.float32))
    return (result.astype(jnp.bfloat16), grads[0].astype(jnp.bfloat16), grads[1], grads[2], grads[3], grads[4], grads[5], grads[6], grads[7], grads[8], grads[9], grads[10], grads[11], grads[12], grads[13], grads[14], grads[15])
```

```python
import functools

import math

import jax
import jax.numpy as jnp
from jax import lax
from jax.experimental import pallas as pl
from jax.experimental.pallas import tpu as pltpu
from jax.sharding import PartitionSpec as P

BLK = 64
PAIR = 2
MASKED = -1e30
CHUNK = 512
f32, bf16 = jnp.float32, jnp.bfloat16


def nt(a, b):
    return lax.dot_general(a, b, (((1,), (1,)), ((), ())), preferred_element_type=f32)


def tn(a, b):
    return lax.dot_general(a, b, (((0,), (0,)), ((), ())), preferred_element_type=f32)


def nn(a, b):
    return jnp.dot(a, b, preferred_element_type=f32)


def head_masks(places):
    group = lax.broadcasted_iota(jnp.int32, (1, 256), 1) // 64
    return [(group == place).astype(bf16) for place in places]


def spread(rows, masks):
    return jnp.concatenate([rows * m for m in masks], axis=0)


def fold(stacked, masks):
    n = stacked.shape[0] // 3
    out = stacked[0:n] * masks[0].astype(f32)
    for h in (1, 2):
        out = out + stacked[h * n : (h + 1) * n] * masks[h].astype(f32)
    return out


def tile_starts(i, b, rand_ref, seq):
    near = jnp.clip((i - 1) * BLK, 0, seq - 3 * BLK)
    near = pl.multiple_of(near, BLK)
    rand = [pl.multiple_of(rand_ref[3 * b + r] * BLK, BLK) for r in range(3)]
    return near, rand


def gather_tiles(kv_ref, near, rand):
    parts = [kv_ref[pl.ds(near, 3 * BLK), :]]
    parts += [kv_ref[pl.ds(r, BLK), :] for r in rand]
    parts += [kv_ref[0 : 2 * BLK, :]]
    return jnp.concatenate(parts, axis=0)


def tile_live(i, near, rand, length):
    out = []
    for j in range(3):
        blk = near // BLK + j
        ok = jnp.abs(blk - i) <= 1
        out.append(jnp.where(ok, length - blk * BLK, 0))
    out += [length - r for r in rand]
    for g in range(2):
        out.append(jnp.where(jnp.abs(i - g) > 1, length - g * BLK, 0))
    return out


def fwd_kernel(seq, meta_ref, rand_ref, q_ref, kv_ref, o_ref):
    step = pl.program_id(0)
    steps = pl.num_programs(0)
    first = meta_ref[0] + PAIR * lax.rem(step + meta_ref[3] // PAIR, steps)
    length = meta_ref[2]
    block0 = meta_ref[1] + first
    kmask = head_masks((0, 1, 2))
    vmask = head_masks((2, 3, 1))

    def sparse(u):
        i = block0 + u
        near, rand = tile_starts(i, first + u, rand_ref, seq)
        tiles = gather_tiles(kv_ref, near, rand)
        live = tile_live(i, near, rand, length)
        lane = lax.broadcasted_iota(jnp.int32, (1, BLK), 1)
        bias = jnp.concatenate([jnp.where(lane < n, 0.0, MASKED) for n in live], axis=1)
        qs = spread(q_ref[u * BLK : (u + 1) * BLK, :], kmask)
        s = nt(qs, tiles[:, 0:256]) + bias
        top = jnp.max(s, axis=1, keepdims=True)
        p = jnp.exp(s - top)
        total = jnp.sum(p, axis=1, keepdims=True)
        mixed = nn(p.astype(bf16), tiles[:, 128:384]) / total
        o_ref[u * BLK : (u + 1) * BLK, :] = fold(mixed, vmask).astype(bf16)

    def dense():
        qs = jnp.concatenate(
            [spread(q_ref[u * BLK : (u + 1) * BLK, :], kmask) for u in range(PAIR)], axis=0
        )
        rows = qs.shape[0]
        lane = lax.broadcasted_iota(jnp.int32, (1, CHUNK), 1)

        def body(c, carry):
            top, total, mixed = carry
            start = pl.multiple_of(c * CHUNK, CHUNK)
            keys = kv_ref[pl.ds(start, CHUNK), :]
            s = nt(qs, keys[:, 0:256]) + jnp.where(lane + start < length, 0.0, MASKED)
            new = jnp.maximum(top, jnp.max(s, axis=1, keepdims=True))
            scale = jnp.exp(top - new)
            p = jnp.exp(s - new)
            total = total * scale + jnp.sum(p, axis=1, keepdims=True)
            mixed = mixed * scale + nn(p.astype(bf16), keys[:, 128:384])
            return new, total, mixed

        init = (
            jnp.full((rows, 1), MASKED, f32),
            jnp.zeros((rows, 1), f32),
            jnp.zeros((rows, 256), f32),
        )
        top, total, mixed = lax.fori_loop(0, seq // CHUNK, body, init)
        mixed = mixed / total
        half = rows // PAIR
        for u in range(PAIR):
            o_ref[u * BLK : (u + 1) * BLK, :] = fold(
                mixed[u * half : (u + 1) * half], vmask
            ).astype(bf16)

    @pl.when(block0 >= 2)
    def _():
        for u in range(PAIR):
            sparse(u)

    @pl.when(block0 < 2)
    def _():
        dense()


def attend(meta, rand, q, kv, rows):
    seq = kv.shape[0]
    steps = rows // (PAIR * BLK)
    spec = pltpu.PrefetchScalarGridSpec(
        num_scalar_prefetch=2,
        grid=(steps,),
        in_specs=[
            pl.BlockSpec((PAIR * BLK, 256), lambda g, m, r: (m[0] // PAIR + lax.rem(g + m[3] // PAIR, steps), 0)),
            pl.BlockSpec((seq, 384), lambda g, m, r: (0, 0), pipeline_mode=pl.Buffered(1)),
        ],
        out_specs=pl.BlockSpec((PAIR * BLK, 256), lambda g, m, r: (g, 0)),
    )
    return pl.pallas_call(
        functools.partial(fwd_kernel, seq),
        grid_spec=spec,
        out_shape=jax.ShapeDtypeStruct((rows, 256), bf16),
        compiler_params=pltpu.CompilerParams(vmem_limit_bytes=40 << 20),
        cost_estimate=pl.CostEstimate(
            flops=4 * rows * 3 * 512 * 256, bytes_accessed=seq * 768, transcendentals=rows * 3 * 512
        ),
        name="attend",
    )(meta, rand, q, kv)


def bwd_kernel(seq, last, meta_ref, rand_ref, q_ref, kv_ref, do_ref, *rest):
    if last:
        in_ref, dq_ref, out_ref, acc = rest
    else:
        dq_ref, out_ref = rest
        acc = out_ref
    step = pl.program_id(0)
    steps = pl.num_programs(0)
    first = meta_ref[0] + PAIR * lax.rem(step + meta_ref[3] // PAIR, steps)
    length = meta_ref[2]
    block0 = meta_ref[1] + first
    kmask = head_masks((0, 1, 2))
    vmask = head_masks((2, 3, 1))

    @pl.when(step == 0)
    def _():
        if last:
            pltpu.sync_copy(in_ref, acc)
        else:
            acc[...] = jnp.zeros_like(acc)

    def add_rows(start, count, wk, wv):
        rows = pl.ds(start, count)
        acc[rows, 0:128] += wk[:, 0:128]
        acc[rows, 128:256] += wk[:, 128:256] + wv[:, 0:128]
        acc[rows, 256:384] += wv[:, 128:256]

    def sparse(u):
        i = block0 + u
        near, rand = tile_starts(i, first + u, rand_ref, seq)
        tiles = gather_tiles(kv_ref, near, rand)
        live = tile_live(i, near, rand, length)
        row = lax.broadcasted_iota(jnp.int32, (BLK, 192), 0)
        qs = spread(q_ref[u * BLK : (u + 1) * BLK, :], kmask)
        gs = spread(do_ref[u * BLK : (u + 1) * BLK, :], vmask)
        s = nt(tiles[:, 0:256], qs)
        s = jnp.concatenate(
            [
                jnp.where(row < live[j], s[j * BLK : (j + 1) * BLK], MASKED)
                for j in range(8)
            ],
            axis=0,
        )
        top = jnp.max(s, axis=0, keepdims=True)
        p = jnp.exp(s - top)
        p = p * (1.0 / jnp.sum(p, axis=0, keepdims=True))
        dp = nt(tiles[:, 128:384], gs)
        inner = jnp.sum(p * dp, axis=0, keepdims=True)
        ds = (p * (dp - inner)).astype(bf16)
        wk = nn(ds, qs)
        wv = nn(p.astype(bf16), gs)
        add_rows(near, 192, wk[0:192], wv[0:192])
        for r in range(3):
            a = 192 + r * BLK
            add_rows(rand[r], BLK, wk[a : a + BLK], wv[a : a + BLK])
        add_rows(0, 128, wk[384:512], wv[384:512])
        dq = fold(tn(ds, tiles[:, 0:256]), kmask) * 0.125
        dq_ref[u * BLK : (u + 1) * BLK, :] = dq.astype(bf16)

    def dense():
        qs = jnp.concatenate(
            [spread(q_ref[u * BLK : (u + 1) * BLK, :], kmask) for u in range(PAIR)], axis=0
        )
        gs = jnp.concatenate(
            [spread(do_ref[u * BLK : (u + 1) * BLK, :], vmask) for u in range(PAIR)], axis=0
        )
        cols = qs.shape[0]
        row = lax.broadcasted_iota(jnp.int32, (CHUNK, cols), 0)

        def scores(c):
            start = pl.multiple_of(c * CHUNK, CHUNK)
            keys = kv_ref[pl.ds(start, CHUNK), :]
            s = jnp.where(row < length - start, nt(keys[:, 0:256], qs), MASKED)
            return start, keys, s, nt(keys[:, 128:384], gs)

        def stats(c, carry):
            top, total, inner = carry
            _, _, s, dp = scores(c)
            new = jnp.maximum(top, jnp.max(s, axis=0, keepdims=True))
            scale = jnp.exp(top - new)
            p = jnp.exp(s - new)
            total = total * scale + jnp.sum(p, axis=0, keepdims=True)
            inner = inner * scale + jnp.sum(p * dp, axis=0, keepdims=True)
            return new, total, inner

        init = (
            jnp.full((1, cols), MASKED, f32),
            jnp.zeros((1, cols), f32),
            jnp.zeros((1, cols), f32),
        )
        top, total, inner = lax.fori_loop(0, seq // CHUNK, stats, init)
        inverse = 1.0 / total
        inner = inner * inverse

        def back(c, dq):
            start, keys, s, dp = scores(c)
            p = jnp.exp(s - top) * inverse
            ds = (p * (dp - inner)).astype(bf16)
            add_rows(start, CHUNK, nn(ds, qs), nn(p.astype(bf16), gs))
            return dq + tn(ds, keys[:, 0:256])

        dq = lax.fori_loop(0, seq // CHUNK, back, jnp.zeros((cols, 256), f32))
        half = cols // PAIR
        for u in range(PAIR):
            dq_ref[u * BLK : (u + 1) * BLK, :] = (
                fold(dq[u * half : (u + 1) * half], kmask) * 0.125
            ).astype(bf16)

    @pl.when(block0 >= 2)
    def _():
        for u in range(PAIR):
            sparse(u)

    @pl.when(block0 < 2)
    def _():
        dense()

    if last:

        @pl.when(step == pl.num_programs(0) - 1)
        def _():
            out_ref[...] = acc[...].astype(bf16)


def attend_back(meta, rand, q, kv, grad, carried):
    seq = kv.shape[0]
    rows = grad.shape[0]
    steps = rows // (PAIR * BLK)
    last = carried is not None
    whole = pl.BlockSpec((seq, 384), lambda g, m, r: (0, 0), pipeline_mode=pl.Buffered(1))
    spec = pltpu.PrefetchScalarGridSpec(
        num_scalar_prefetch=2,
        grid=(steps,),
        in_specs=[
            pl.BlockSpec((PAIR * BLK, 256), lambda g, m, r: (m[0] // PAIR + lax.rem(g + m[3] // PAIR, steps), 0)),
            whole,
            pl.BlockSpec((PAIR * BLK, 256), lambda g, m, r: (g, 0)),
        ]
        + ([pl.BlockSpec(memory_space=pl.ANY)] if last else []),
        out_specs=[pl.BlockSpec((PAIR * BLK, 256), lambda g, m, r: (g, 0)), whole],
        scratch_shapes=[pltpu.VMEM((seq, 384), f32)] if last else [],
    )
    return pl.pallas_call(
        functools.partial(bwd_kernel, seq, last),
        grid_spec=spec,
        out_shape=[
            jax.ShapeDtypeStruct((rows, 256), bf16),
            jax.ShapeDtypeStruct((seq, 384), bf16 if last else f32),
        ],
        compiler_params=pltpu.CompilerParams(vmem_limit_bytes=60 << 20),
        cost_estimate=pl.CostEstimate(
            flops=10 * rows * 3 * 512 * 256, bytes_accessed=seq * 384 * 8, transcendentals=rows * 3 * 512
        ),
        name="attend_back",
    )(meta, rand, q, kv, grad, *([carried] if last else []))


EPSILON = 1e-05
FSDP, CTX, TP = "fsdp", "ctx", "tp"


def core_swap(value):
    return lax.ppermute(value, TP, [(0, 1), (1, 0), (2, 3), (3, 2)])


def y_swap(value):
    return lax.ppermute(value, TP, [(0, 2), (2, 0), (1, 3), (3, 1)])


def x_swap(value):
    return lax.ppermute(value, CTX, [(0, 1), (1, 0)])


def rows_at(array, start, count):
    return lax.dynamic_slice_in_dim(array, start, count, axis=0)


def put_rows(pieces, starts, total):
    out = jnp.zeros((total,) + pieces[0].shape[1:], pieces[0].dtype)
    for piece, start in zip(pieces, starts):
        out = lax.dynamic_update_slice_in_dim(out, piece, start, axis=0)
    return out


def norm_forward(resid_in, gain_vec, shift_vec):
    center = jnp.mean(resid_in, axis=-1, keepdims=True)
    offset = resid_in - center
    spread_sq = jnp.mean(offset * offset, axis=-1, keepdims=True)
    inverse = lax.rsqrt(spread_sq + EPSILON)
    normed = offset * inverse
    return (normed * gain_vec + shift_vec, normed, inverse)


def norm_backward(grad_out, normed, inverse, gain_vec):
    grad_normed = grad_out * gain_vec
    first_mean = jnp.mean(grad_normed, axis=-1, keepdims=True)
    second_mean = jnp.mean(grad_normed * normed, axis=-1, keepdims=True)
    grad_in = inverse * (grad_normed - first_mean - normed * second_mean)
    return (grad_in, jnp.sum(grad_out * normed, axis=0), jnp.sum(grad_out, axis=0))


def gelu_pair(pre):
    cdf = 0.5 * lax.erfc(pre * -math.sqrt(0.5))
    density = jnp.exp(-0.5 * pre * pre) * (1.0 / math.sqrt(2.0 * math.pi))
    return (pre * cdf).astype(bf16), (cdf + pre * density).astype(bf16)


def z_gather(piece):
    count = lax.axis_size(FSDP)
    me = lax.axis_index(FSDP)
    rows = piece.shape[0]
    pieces, starts = [piece], [me * rows]
    for shift in range(1, count):
        pieces.append(lax.ppermute(piece, FSDP, [(i, (i + shift) % count) for i in range(count)]))
        starts.append(lax.rem(me - shift + count, count) * rows)
    return put_rows(pieces, starts, count * rows)


def on_device(
    layer_in,
    cotangent,
    lengths,
    rand_blocks,
    w_query,
    b_query,
    w_key,
    w_value,
    b_value,
    w_proj,
    b_proj,
    gain_one,
    shift_one,
    w_in,
    b_in,
    w_out,
    b_out,
    gain_two,
    shift_two,
):
    tokens, width = layer_in.shape
    ctx_count = lax.axis_size(CTX)
    fsdp_count = lax.axis_size(FSDP)
    ctx = lax.axis_index(CTX)
    tp = lax.axis_index(TP)
    y, c = tp // 2, tp % 2
    seq = tokens * ctx_count
    half, quarter = tokens // 2, tokens // 4
    shard = w_query.shape[0]
    hidden_units = w_in.shape[1]
    order = [2 * y + 1 - c, 2 * y + c, 2 * (1 - y) + 1 - c, 2 * (1 - y) + c]

    def kv_columns(key_cols, value_cols):
        return jnp.concatenate([key_cols, value_cols[:, 128:192], value_cols[:, 0:128]], axis=1)

    attn_rows = jnp.concatenate([w_query, kv_columns(w_key, w_value)], axis=1)
    bias_rows = jnp.zeros((16, attn_rows.shape[1]), bf16)
    bias_rows = bias_rows.at[0, 0 : b_query.shape[0]].set(b_query)
    bias_rows = bias_rows.at[1, 0 : b_value.shape[0]].set(b_value)
    attn_all = z_gather(jnp.concatenate([attn_rows, bias_rows], axis=0))
    attn_all = attn_all.reshape(fsdp_count, shard + 16, attn_rows.shape[1])
    attn_w = attn_all[:, 0:shard].reshape(width, attn_rows.shape[1])
    bq = attn_all[:, shard, 0 : b_query.shape[0]].reshape(1, 192).astype(f32)
    bv = attn_all[:, shard + 1, 0 : b_value.shape[0]].reshape(1, 192).astype(f32)
    wq = jnp.concatenate([attn_w[:, 0:192], jnp.zeros((width, 64), bf16)], axis=1)
    wkv = attn_w[:, 192:576]
    bq = jnp.concatenate([bq, jnp.zeros((1, 64), f32)], axis=1)
    bkv = jnp.concatenate([jnp.zeros((1, 192), f32), bv[:, 128:192], bv[:, 0:128]], axis=1)

    proj_t = w_proj.T
    proj_t = jnp.concatenate([proj_t[:, 128:192], proj_t[:, 0:128]], axis=1)
    vec = jnp.concatenate([b_in, b_proj, gain_one, shift_one, b_out, gain_two, shift_two])
    in_cols = hidden_units + 192
    vec_rows = jnp.zeros((16 * in_cols,), bf16).at[0 : vec.shape[0]].set(vec).reshape(16, in_cols)
    in_pack = jnp.concatenate([jnp.concatenate([w_in, proj_t], axis=1), vec_rows], axis=0)
    in_mine = lax.all_gather(in_pack, FSDP, axis=0, tiled=False)
    in_theirs = y_swap(in_mine)
    out_mine = lax.all_gather(w_out.T, FSDP, axis=0, tiled=True)
    out_theirs = y_swap(out_mine)

    def unpack(pack):
        w = pack[:, 0:shard].reshape(width, in_cols)
        p = jnp.concatenate([jnp.zeros((width, 64), bf16), w[:, hidden_units:]], axis=1)
        return w[:, 0:hidden_units], p, pack[:, shard:].reshape(fsdp_count, 16 * in_cols)

    win_mine, wp_mine, vec_mine = unpack(in_mine)
    win_theirs, wp_theirs, vec_theirs = unpack(in_theirs)

    def vector(v, index):
        return v[:, index * 192 : index * 192 + vec.shape[0] // 7].reshape(1, -1).astype(f32)

    n_vec = vec.shape[0] // 7

    def vectors(v):
        return [v[:, k * n_vec : (k + 1) * n_vec].reshape(1, -1).astype(f32) for k in range(7)]

    bin_mine, bp, g1, s1, bo, g2, s2 = vectors(vec_mine)
    bin_theirs = vectors(vec_theirs)[0]

    if ctx_count == 2:
        chunks = 2
        size = half // chunks
        got = [x_swap(rows_at(layer_in, c * half + k * size, size)) for k in range(chunks)]
        got2 = [core_swap(g) for g in got]
        base = (1 - ctx) * tokens
        x_all = put_rows(
            [layer_in] + got + got2,
            [ctx * tokens]
            + [base + c * half + k * size for k in range(chunks)]
            + [base + (1 - c) * half + k * size for k in range(chunks)],
            seq,
        )
    else:
        x_all = lax.all_gather(layer_in, CTX, axis=0, tiled=True)
    q_all = (nn(layer_in, wq) + bq).astype(bf16) * jnp.asarray(0.125, bf16)
    kv_all = (nn(x_all, wkv) + bkv).astype(bf16)
    blocks = tokens // BLK
    rand = rand_blocks.reshape(-1)
    live = lengths[0]

    def meta(half_index):
        return jnp.stack([half_index * (blocks // 2), ctx * blocks, live, (1 - c) * (blocks // 4)]).astype(
            jnp.int32
        )

    o_send = attend(meta(1 - y), rand, q_all, kv_all, half)
    o_got = y_swap(o_send)
    o_keep = attend(meta(y), rand, q_all, kv_all, half)

    def branch_of(rows):
        return nt(o_keep[rows], wp_mine) + nt(o_got[rows], wp_theirs)

    peer, own = slice(0, quarter), slice(quarter, half)
    x_own = rows_at(layer_in, tp * quarter, quarter).astype(f32)
    branch = branch_of(own) + core_swap(branch_of(peer).astype(bf16)).astype(f32)
    hidden, normed_one, inverse_one = norm_forward(x_own + branch + bp, g1, s1)
    hid_own = hidden.astype(bf16)
    hid = jnp.concatenate([core_swap(hid_own), hid_own], axis=0)

    act_m, slope_m = gelu_pair(nn(hid, win_mine) + bin_mine)
    act_t, slope_t = gelu_pair(nn(hid, win_theirs) + bin_theirs)

    def mlp_of(rows):
        return nt(act_m[rows], out_mine) + nt(act_t[rows], out_theirs)

    mlp = mlp_of(own) + core_swap(mlp_of(peer).astype(bf16)).astype(f32)
    result, normed_two, inverse_two = norm_forward(hidden + mlp + bo, g2, s2)
    position = ctx * tokens + tp * quarter + jnp.arange(quarter, dtype=jnp.int32)
    row_live = (position < live).astype(f32)[:, None]
    out_own = (result * row_live).astype(bf16)
    out_other = y_swap(out_own)
    outs = [core_swap(out_own), out_own, core_swap(out_other), out_other]
    layer_out = put_rows(outs, [k * quarter for k in order], tokens)

    grad_result = rows_at(cotangent, tp * quarter, quarter).astype(f32) * row_live
    grad_two, dg2, ds2 = norm_backward(grad_result, normed_two, inverse_two, g2)
    gm_own = grad_two.astype(bf16)
    db_out = jnp.sum(gm_own, axis=0, dtype=f32)
    gm = jnp.concatenate([core_swap(gm_own), gm_own], axis=0)
    gp_m = (nn(gm, out_mine) * slope_m.astype(f32)).astype(bf16)
    gp_t = (nn(gm, out_theirs) * slope_t.astype(f32)).astype(bf16)

    def gh_of(rows):
        return nt(gp_m[rows], win_mine) + nt(gp_t[rows], win_theirs)

    grad_hidden = grad_two + gh_of(own) + core_swap(gh_of(peer).astype(bf16)).astype(f32)
    grad_one, dg1, ds1 = norm_backward(grad_hidden, normed_one, inverse_one, g1)
    gb_own = grad_one.astype(bf16)
    db_proj = jnp.sum(gb_own, axis=0, dtype=f32)
    gb = jnp.concatenate([core_swap(gb_own), gb_own], axis=0)
    go_got = y_swap(nn(gb, wp_theirs).astype(bf16))
    go_keep = nn(gb, wp_mine).astype(bf16)

    dwo_t = tn(gm, act_t).astype(bf16)
    dwi_t = tn(hid, gp_t).astype(bf16)
    dwp_t = tn(gb, o_got).astype(bf16)
    dbi_t = jnp.sum(gp_t, axis=0, dtype=f32)
    dwo_t, dwi_t, dwp_t, dbi_t, go_got = lax.optimization_barrier((dwo_t, dwi_t, dwp_t, dbi_t, go_got))
    dwo = (tn(gm, act_m) + y_swap(dwo_t).astype(f32)).astype(bf16)
    dwi = (tn(hid, gp_m) + y_swap(dwi_t).astype(f32)).astype(bf16)
    dwp = (tn(gb, o_keep) + y_swap(dwp_t).astype(f32)).astype(bf16)
    dbi = jnp.sum(gp_m, axis=0, dtype=f32) + y_swap(dbi_t)
    vecs = jnp.stack([db_out, dg2, ds2, dg1, ds1, db_proj, jnp.zeros_like(ds1), jnp.zeros_like(ds1)])
    vecs = vecs + core_swap(vecs)
    vecs = vecs + y_swap(vecs)

    def z_reduce(value):
        return lax.psum_scatter(value, FSDP, scatter_dimension=0, tiled=True)

    def x_reduce(value):
        if ctx_count == 2:
            return value.astype(f32) + x_swap(value).astype(f32)
        return lax.psum(value, CTX).astype(f32)

    dwo_mine = x_reduce(z_reduce(dwo)).T
    dwi_mine = x_reduce(z_reduce(dwi))

    dq_keep, carried = attend_back(meta(y), rand, q_all, kv_all, go_keep, None)
    dq_got, dkv = attend_back(meta(1 - y), rand, q_all, kv_all, go_got, carried)
    dqs = [dq_keep[peer], dq_keep[own], dq_got[peer], dq_got[own]]
    if ctx_count == 2:
        mine = [rows_at(dkv, ctx * tokens + k * quarter, quarter) for k in order]
        theirs = [rows_at(dkv, (1 - ctx) * tokens + k * quarter, quarter) for k in order]
        got = {}
        for k in (0, 2, 1, 3):
            got[k] = x_swap(theirs[k])
        gkv = [(mine[k].astype(f32) + got[k].astype(f32)).astype(bf16) for k in range(4)]
    else:
        summed = lax.psum_scatter(dkv, CTX, scatter_dimension=0, tiled=True)
        gkv = [rows_at(summed, k * quarter, quarter) for k in order]

    def back_of(k):
        return nt(dqs[k], wq) + nt(gkv[k], wkv)

    sent = [core_swap(back_of(k).astype(bf16)) for k in (0, 2)]
    first = (back_of(1) + grad_one + sent[0].astype(f32)).astype(bf16)
    second = (back_of(3) + sent[1].astype(f32)).astype(bf16)
    first_sum = (first.astype(f32) + y_swap(second).astype(f32)).astype(bf16)
    second_sum = (second.astype(f32) + y_swap(first).astype(f32)).astype(bf16)
    gis = [core_swap(first_sum), first_sum, core_swap(second_sum), second_sum]
    grad_input = put_rows(gis, [k * quarter for k in order], tokens)

    x_dev = jnp.concatenate([rows_at(layer_in, k * quarter, quarter) for k in order], axis=0)
    dq_dev = jnp.concatenate([dq_keep, dq_got], axis=0)
    dwq = tn(x_dev, dq_dev)[:, 0:192].astype(bf16)
    dwkv = tn(x_all, dkv).astype(bf16)
    dbq = jnp.sum(dq_dev, axis=0, dtype=f32)[0:192]
    dbv = jnp.sum(dkv[:, 192:384], axis=0, dtype=f32)
    dbv = jnp.concatenate([dbv[64:192], dbv[0:64]])
    big = jnp.concatenate([dwq, dwkv, dwp[:, 64:256]], axis=1).reshape(fsdp_count, shard, 768)
    flat = jnp.concatenate(
        [vecs[k].reshape(fsdp_count, -1) for k in range(6)]
        + [dbi.reshape(fsdp_count, -1), dbq.reshape(fsdp_count, -1), dbv.reshape(fsdp_count, -1)],
        axis=1,
    ).astype(bf16)
    tail = jnp.zeros((fsdp_count, 16 * 768), bf16).at[:, 0 : flat.shape[1]].set(flat)
    both = jnp.concatenate([big, tail.reshape(fsdp_count, 16, 768)], axis=1)
    both = x_reduce(z_reduce(both.reshape(fsdp_count * (shard + 16), 768)))
    dwq = both[0:shard, 0:192]
    dwk = both[0:shard, 192:384]
    dwv = jnp.concatenate([both[0:shard, 448:576], both[0:shard, 384:448]], axis=1)
    dwp = both[0:shard, 576:768]
    dwp = jnp.concatenate([dwp[:, 64:192], dwp[:, 0:64]], axis=1).T
    small = both[shard:].reshape(-1)
    cuts = [0]
    for size in [shard] * 6 + [dbi.shape[0] // fsdp_count, 192 // fsdp_count, 192 // fsdp_count]:
        cuts.append(cuts[-1] + size)
    db_out, dg2, ds2, dg1, ds1, db_proj, db_in, db_query, db_value = [
        small[a:b] for a, b in zip(cuts[:-1], cuts[1:])
    ]
    return (
        layer_out,
        grad_input,
        dwq,
        db_query,
        dwk,
        dwv,
        db_value,
        dwp,
        db_proj,
        dg1,
        ds1,
        dwi_mine,
        db_in,
        dwo_mine,
        db_out,
        dg2,
        ds2,
    )


def solution(mesh):
    rows = P((FSDP, CTX), None)
    vector, unit = P(FSDP), P((TP, FSDP))
    column, row = P(FSDP, TP), P(TP, FSDP)
    return jax.shard_map(
        on_device,
        mesh=mesh,
        in_specs=(
            rows, rows, vector, P(FSDP, CTX, None), column, unit, column, column, unit, row,
            vector, vector, vector, column, unit, row, vector, vector, vector,
        ),
        out_specs=(
            rows, rows, column, unit, column, column, unit, row, vector, vector, vector,
            column, unit, row, vector, vector, vector,
        ),
        check_vma=False,
    )
```

```python
import functools
import math

import jax
import jax.numpy as jnp
from jax import lax
from jax.experimental import pallas as pl
from jax.experimental.pallas import tpu as pltpu
from jax.sharding import PartitionSpec as P

BLK = 64
PAIR = 2
MASKED = -1e30
CHUNK = 512
EPSILON = 1e-05
FSDP, CTX, TP = "fsdp", "ctx", "tp"
f32, bf16 = jnp.float32, jnp.bfloat16
ANY = pl.BlockSpec(memory_space=pl.ANY)


VM = pl.BlockSpec(memory_space=pltpu.VMEM)
HBM = pl.BlockSpec(memory_space=pltpu.HBM)
MIB = 1 << 20
LIGHT = pl.CostEstimate(flops=0, bytes_accessed=0, transcendentals=0)
SPACES = {"h": pltpu.HBM, "v": pltpu.VMEM}


def call(kernel, out_shape, ins="", outs="", **options):
    spec = options.get("grid_spec")
    tables = spec.num_scalar_prefetch if spec is not None else 0

    def letter(text, k):
        return text[min(k, len(text) - 1)] if text else "h"

    many = isinstance(out_shape, (list, tuple))
    shapes = list(out_shape) if many else [out_shape]
    shapes = [
        v if letter(outs, k) == "-" else SPACES[letter(outs, k)](v.shape, v.dtype)
        for k, v in enumerate(shapes)
    ]
    run = pl.pallas_call(kernel, out_shape=shapes if many else shapes[0], **options)

    def apply(*args):
        placed = [
            v if letter(ins, k) == "-" else pltpu.with_memory_space_constraint(v, SPACES[letter(ins, k)])
            for k, v in enumerate(args[tables:])
        ]
        return run(*args[0:tables], *placed)

    return apply


def nt(a, b):
    return lax.dot_general(a, b, (((1,), (1,)), ((), ())), preferred_element_type=f32)


def tn(a, b):
    return lax.dot_general(a, b, (((0,), (0,)), ((), ())), preferred_element_type=f32)


def nn(a, b):
    return jnp.dot(a, b, preferred_element_type=f32)


def place_kernel(count, starts_ref, *refs):
    for k in range(count):

        @pl.when(pl.program_id(0) == k)
        def _():
            refs[count][...] = refs[k][...]


def place(pieces, slots, total):
    count = len(pieces)
    rows, width = pieces[0].shape
    return call(
        functools.partial(place_kernel, count),
        grid_spec=pltpu.PrefetchScalarGridSpec(
            num_scalar_prefetch=1,
            grid=(count,),
            in_specs=[whole_block(p) for p in pieces],
            out_specs=pl.BlockSpec((rows, width), lambda g, s: (s[g], 0)),
        ),
        out_shape=jax.ShapeDtypeStruct((total, width), pieces[0].dtype),
        compiler_params=pltpu.CompilerParams(vmem_limit_bytes=8 * MIB),
        cost_estimate=LIGHT,
        name="place",
    )(jnp.stack(slots).astype(jnp.int32), *pieces)


def collect_kernel(count, slots_ref, x_ref, *refs):
    step = pl.program_id(0)

    @pl.when(step < 4)
    def _():
        refs[count][...] = x_ref[...]

    rows = x_ref.shape[0]
    parts = [(ref, at) for at in range(0, 2 * rows, rows) for ref in refs[:count]]
    for k, (ref, at) in enumerate(parts):

        @pl.when(step == 4 + k)
        def _():
            refs[count][...] = ref[at : at + rows, :]


def collect(x, slots, others):
    count = len(others)
    rows, width = x.shape[0] // 4, x.shape[1]
    steps = 4 + sum(v.shape[0] // rows for v in others)
    return call(
        functools.partial(collect_kernel, count),
        grid_spec=pltpu.PrefetchScalarGridSpec(
            num_scalar_prefetch=1,
            grid=(steps,),
            in_specs=[pl.BlockSpec((rows, width), lambda g, s: (s[jnp.minimum(g, 3)], 0))]
            + [whole_block(v) for v in others],
            out_specs=pl.BlockSpec((rows, width), lambda g, s: (g, 0)),
        ),
        out_shape=jax.ShapeDtypeStruct((steps * rows, width), x.dtype),
        compiler_params=pltpu.CompilerParams(vmem_limit_bytes=8 * MIB),
        cost_estimate=LIGHT,
        name="collect",
    )(jnp.stack(slots).astype(jnp.int32), x, *others)


def load_all(pairs, sems):
    copies = [pltpu.make_async_copy(src, dst, sems.at[k]) for k, (src, dst) in enumerate(pairs)]
    for copy in copies:
        copy.start()
    for copy in copies:
        copy.wait()


def open_kernel(count, slots_ref, x_ref, *refs):
    srcs, (a_ref, half_ref), bufs, sems = refs[0:5], refs[5:7], refs[7:12], refs[12]
    size = half_ref.shape[0] // count
    pairs = []
    for k in range(count):
        start = pl.multiple_of(slots_ref[k] * size, 64)
        pairs.append((x_ref.at[pl.ds(start, size)], half_ref.at[pl.ds(k * size, size)]))
    load_all(list(zip(srcs, bufs)) + pairs, sems)
    wq_ref, wk_ref, wv_ref, bq_ref, bv_ref = bufs
    rows = wq_ref.shape[0]
    bias = bq_ref.shape[1]
    a_ref[0:rows, 0:192] = wq_ref[...]
    a_ref[0:rows, 192:384] = wk_ref[...]
    a_ref[0:rows, 384:448] = wv_ref[:, 128:192]
    a_ref[0:rows, 448:576] = wv_ref[:, 0:128]
    a_ref[rows : rows + 16, :] = jnp.zeros((16, 576), bf16)
    a_ref[rows : rows + 1, 0:bias] = bq_ref[...]
    a_ref[rows + 1 : rows + 2, 0:bias] = bv_ref[...]


def whole_block(value):
    zeros = (0,) * value.ndim
    return pl.BlockSpec(value.shape, lambda *_: zeros, pipeline_mode=pl.Buffered(1))


def open_call(x, slots, size, wq, wk, wv, bq, bv):
    count = len(slots)
    rows, width = wq.shape[0], x.shape[1]
    srcs = [wq, wk, wv, bq[None], bv[None]]
    return call(
        functools.partial(open_kernel, count),
        grid_spec=pltpu.PrefetchScalarGridSpec(
            num_scalar_prefetch=1,
            grid=(1,),
            in_specs=[HBM] * 6,
            out_specs=[
                pl.BlockSpec((rows + 16, 576), lambda g, s: (0, 0)),
                pl.BlockSpec((count * size, width), lambda g, s: (0, 0)),
            ],
            scratch_shapes=[pltpu.VMEM(v.shape, bf16) for v in srcs]
            + [pltpu.SemaphoreType.DMA((5 + count,))],
        ),
        out_shape=[
            jax.ShapeDtypeStruct((rows + 16, 576), bf16),
            jax.ShapeDtypeStruct((count * size, width), bf16),
        ],
        compiler_params=pltpu.CompilerParams(vmem_limit_bytes=8 * MIB),
        cost_estimate=LIGHT,
        name="open",
    )(jnp.stack(slots).astype(jnp.int32), x, *srcs)


def pack_kernel(win_ref, wp_ref, vec_ref, d_ref, proj, vecs, sems):
    rows, units = win_ref.shape
    load_all(
        [(wp_ref, proj), (vec_ref, vecs), (win_ref, d_ref.at[pl.ds(0, rows), pl.ds(0, units)])], sems
    )
    turned = proj[...].T
    d_ref[0:rows, units : units + 64] = turned[:, 128:192]
    d_ref[0:rows, units + 64 : units + 192] = turned[:, 0:128]
    d_ref[rows : rows + 16, :] = jnp.zeros((16, d_ref.shape[1]), bf16)
    d_ref[rows : rows + vecs.shape[0], 0 : vecs.shape[1]] = vecs[...]


def pack_call(w_in, w_proj, vecs):
    rows, units = w_in.shape
    vecs = jnp.stack(vecs)
    return call(
        pack_kernel,
        grid=(1,),
        in_specs=[HBM] * 3,
        out_specs=pl.BlockSpec((rows + 16, units + 192), lambda g: (0, 0)),
        out_shape=jax.ShapeDtypeStruct((rows + 16, units + 192), bf16),
        scratch_shapes=[
            pltpu.VMEM(w_proj.shape, bf16),
            pltpu.VMEM(vecs.shape, bf16),
            pltpu.SemaphoreType.DMA((3,)),
        ],
        compiler_params=pltpu.CompilerParams(vmem_limit_bytes=6 * MIB),
        cost_estimate=LIGHT,
        name="pack",
    )(w_in, w_proj, vecs)


def head_masks(places):
    group = lax.broadcasted_iota(jnp.int32, (1, 256), 1) // 64
    return [(group == place).astype(bf16) for place in places]


def spread(rows, masks):
    return jnp.concatenate([rows * m for m in masks], axis=0)


def fold(stacked, masks):
    n = stacked.shape[0] // 3
    out = stacked[0:n] * masks[0].astype(f32)
    for h in (1, 2):
        out = out + stacked[h * n : (h + 1) * n] * masks[h].astype(f32)
    return out


def tile_starts(i, b, rand_ref, seq):
    near = jnp.clip((i - 1) * BLK, 0, seq - 3 * BLK)
    near = pl.multiple_of(near, BLK)
    rand = [pl.multiple_of(rand_ref[3 * b + r] * BLK, BLK) for r in range(3)]
    return near, rand


def gather_tiles(kv, near, rand):
    parts = [kv[pl.ds(near, 3 * BLK), :]]
    parts += [kv[pl.ds(r, BLK), :] for r in rand]
    parts += [kv[0 : 2 * BLK, :]]
    return jnp.concatenate(parts, axis=0)


def tile_live(i, near, rand, length):
    out = []
    for j in range(3):
        blk = near // BLK + j
        out.append(jnp.where(jnp.abs(blk - i) <= 1, length - blk * BLK, 0))
    out += [length - r for r in rand]
    for g in range(2):
        out.append(jnp.where(jnp.abs(i - g) > 1, length - g * BLK, 0))
    return out


def load_pieces(size, starts_ref, pieces, kv, sems):
    copies = []
    for piece in pieces:
        for at in range(0, piece.shape[0], size):
            k = len(copies)
            start = pl.multiple_of(starts_ref[k], 64)
            copies.append(
                pltpu.make_async_copy(
                    piece.at[pl.ds(at, size)], kv.at[pl.ds(start, size)], sems.at[k]
                )
            )
    for copy in copies:
        copy.start()
    for copy in copies:
        copy.wait()


def step_block(meta_ref):
    steps = pl.num_programs(0)
    first = meta_ref[0] + PAIR * lax.rem(pl.program_id(0) + meta_ref[3] // PAIR, steps)
    return first, meta_ref[1] + first, meta_ref[2]


def fwd_kernel(count, chunks, meta_ref, rand_ref, starts_ref, q_ref, *rest):
    pieces = rest[:count]
    o_ref, kv, sems = rest[count:]
    seq = kv.shape[0]
    first, block0, length = step_block(meta_ref)
    kmask = head_masks((0, 1, 2))
    vmask = head_masks((2, 3, 1))

    @pl.when(pl.program_id(0) == 0)
    def _():
        load_pieces(seq // chunks, starts_ref, pieces, kv, sems)

    def sparse(u):
        i = block0 + u
        near, rand = tile_starts(i, first + u, rand_ref, seq)
        tiles = gather_tiles(kv, near, rand)
        live = tile_live(i, near, rand, length)
        lane = lax.broadcasted_iota(jnp.int32, (1, BLK), 1)
        bias = jnp.concatenate([jnp.where(lane < n, 0.0, MASKED) for n in live], axis=1)
        qs = spread(q_ref[u * BLK : (u + 1) * BLK, :], kmask)
        s = nt(qs, tiles[:, 0:256]) + bias
        top = jnp.max(s, axis=1, keepdims=True)
        p = jnp.exp(s - top)
        total = jnp.sum(p, axis=1, keepdims=True)
        mixed = nn(p.astype(bf16), tiles[:, 128:384]) / total
        o_ref[u * BLK : (u + 1) * BLK, :] = fold(mixed, vmask).astype(bf16)

    def dense():
        qs = jnp.concatenate(
            [spread(q_ref[u * BLK : (u + 1) * BLK, :], kmask) for u in range(PAIR)], axis=0
        )
        rows = qs.shape[0]
        lane = lax.broadcasted_iota(jnp.int32, (1, CHUNK), 1)

        def body(c, carry):
            top, total, mixed = carry
            start = pl.multiple_of(c * CHUNK, CHUNK)
            keys = kv[pl.ds(start, CHUNK), :]
            s = nt(qs, keys[:, 0:256]) + jnp.where(lane + start < length, 0.0, MASKED)
            new = jnp.maximum(top, jnp.max(s, axis=1, keepdims=True))
            scale = jnp.exp(top - new)
            p = jnp.exp(s - new)
            total = total * scale + jnp.sum(p, axis=1, keepdims=True)
            mixed = mixed * scale + nn(p.astype(bf16), keys[:, 128:384])
            return new, total, mixed

        init = (
            jnp.full((rows, 1), MASKED, f32),
            jnp.zeros((rows, 1), f32),
            jnp.zeros((rows, 256), f32),
        )
        top, total, mixed = lax.fori_loop(0, seq // CHUNK, body, init)
        mixed = mixed / total
        half = rows // PAIR
        for u in range(PAIR):
            o_ref[u * BLK : (u + 1) * BLK, :] = fold(
                mixed[u * half : (u + 1) * half], vmask
            ).astype(bf16)

    @pl.when(block0 >= 2)
    def _():
        for u in range(PAIR):
            sparse(u)

    @pl.when(block0 < 2)
    def _():
        dense()


def q_spec(steps):
    return pl.BlockSpec(
        (PAIR * BLK, 256), lambda g, m, r, s: (m[0] // PAIR + lax.rem(g + m[3] // PAIR, steps), 0)
    )


def attend(meta, rand, starts, q, pieces, seq, rows, chunks):
    steps = rows // (PAIR * BLK)
    count = len(pieces)
    return call(
        functools.partial(fwd_kernel, count, chunks),
        grid_spec=pltpu.PrefetchScalarGridSpec(
            num_scalar_prefetch=3,
            grid=(steps,),
            in_specs=[q_spec(steps)] + [ANY] * count,
            out_specs=pl.BlockSpec((PAIR * BLK, 256), lambda g, m, r, s: (g, 0)),
            scratch_shapes=[pltpu.VMEM((seq, 384), bf16), pltpu.SemaphoreType.DMA((chunks,))],
        ),
        out_shape=jax.ShapeDtypeStruct((rows, 256), bf16),
        compiler_params=pltpu.CompilerParams(vmem_limit_bytes=seq * 768 + 8 * MIB),
        cost_estimate=LIGHT,
        name="attend",
    )(meta, rand, starts, q, *pieces)


def bwd_kernel(count, last, chunks, n_send, meta_ref, rand_ref, starts_ref, q_ref, do_ref, *rest):
    pieces, rest = rest[:count], rest[count:]
    if last:
        in_ref, _, dq_ref, all_ref = rest[:4]
        sends, (kv, acc, sems) = rest[4 : 4 + n_send], rest[-3:]
    else:
        dq_ref, out_ref, kv, acc, sems = rest
    seq = kv.shape[0]
    first, block0, length = step_block(meta_ref)
    kmask = head_masks((0, 1, 2))
    vmask = head_masks((2, 3, 1))

    @pl.when(pl.program_id(0) == 0)
    def _():
        if last:
            carry = pltpu.make_async_copy(in_ref, acc, sems.at[chunks])
            carry.start()
        else:
            acc[...] = jnp.zeros_like(acc)
        load_pieces(seq // chunks, starts_ref, pieces, kv, sems)
        if last:
            carry.wait()

    def add_rows(start, n, wk, wv):
        rows = pl.ds(start, n)
        acc[rows, 0:128] += wk[:, 0:128]
        acc[rows, 128:256] += wk[:, 128:256] + wv[:, 0:128]
        acc[rows, 256:384] += wv[:, 128:256]

    def sparse(u):
        i = block0 + u
        near, rand = tile_starts(i, first + u, rand_ref, seq)
        tiles = gather_tiles(kv, near, rand)
        live = tile_live(i, near, rand, length)
        row = lax.broadcasted_iota(jnp.int32, (BLK, 192), 0)
        qs = spread(q_ref[u * BLK : (u + 1) * BLK, :], kmask)
        gs = spread(do_ref[u * BLK : (u + 1) * BLK, :], vmask)
        s = nt(tiles[:, 0:256], qs)
        s = jnp.concatenate(
            [jnp.where(row < live[j], s[j * BLK : (j + 1) * BLK], MASKED) for j in range(8)],
            axis=0,
        )
        top = jnp.max(s, axis=0, keepdims=True)
        p = jnp.exp(s - top)
        p = p * (1.0 / jnp.sum(p, axis=0, keepdims=True))
        dp = nt(tiles[:, 128:384], gs)
        inner = jnp.sum(p * dp, axis=0, keepdims=True)
        ds = (p * (dp - inner)).astype(bf16)
        wk = nn(ds, qs)
        wv = nn(p.astype(bf16), gs)
        add_rows(near, 192, wk[0:192], wv[0:192])
        for r in range(3):
            a = 192 + r * BLK
            add_rows(rand[r], BLK, wk[a : a + BLK], wv[a : a + BLK])
        add_rows(0, 128, wk[384:512], wv[384:512])
        dq = fold(tn(ds, tiles[:, 0:256]), kmask) * 0.125
        dq_ref[u * BLK : (u + 1) * BLK, :] = dq.astype(bf16)

    def dense():
        qs = jnp.concatenate(
            [spread(q_ref[u * BLK : (u + 1) * BLK, :], kmask) for u in range(PAIR)], axis=0
        )
        gs = jnp.concatenate(
            [spread(do_ref[u * BLK : (u + 1) * BLK, :], vmask) for u in range(PAIR)], axis=0
        )
        cols = qs.shape[0]
        row = lax.broadcasted_iota(jnp.int32, (CHUNK, cols), 0)

        def scores(c):
            start = pl.multiple_of(c * CHUNK, CHUNK)
            keys = kv[pl.ds(start, CHUNK), :]
            s = jnp.where(row < length - start, nt(keys[:, 0:256], qs), MASKED)
            return start, keys, s, nt(keys[:, 128:384], gs)

        def stats(c, carry):
            top, total, inner = carry
            _, _, s, dp = scores(c)
            new = jnp.maximum(top, jnp.max(s, axis=0, keepdims=True))
            scale = jnp.exp(top - new)
            p = jnp.exp(s - new)
            total = total * scale + jnp.sum(p, axis=0, keepdims=True)
            inner = inner * scale + jnp.sum(p * dp, axis=0, keepdims=True)
            return new, total, inner

        init = (
            jnp.full((1, cols), MASKED, f32),
            jnp.zeros((1, cols), f32),
            jnp.zeros((1, cols), f32),
        )
        top, total, inner = lax.fori_loop(0, seq // CHUNK, stats, init)
        inverse = 1.0 / total
        inner = inner * inverse

        def back(c, dq):
            start, keys, s, dp = scores(c)
            p = jnp.exp(s - top) * inverse
            ds = (p * (dp - inner)).astype(bf16)
            add_rows(start, CHUNK, nn(ds, qs), nn(p.astype(bf16), gs))
            return dq + tn(ds, keys[:, 0:256])

        dq = lax.fori_loop(0, seq // CHUNK, back, jnp.zeros((cols, 256), f32))
        half = cols // PAIR
        for u in range(PAIR):
            dq_ref[u * BLK : (u + 1) * BLK, :] = (
                fold(dq[u * half : (u + 1) * half], kmask) * 0.125
            ).astype(bf16)

    @pl.when(block0 >= 2)
    def _():
        for u in range(PAIR):
            sparse(u)

    @pl.when(block0 < 2)
    def _():
        dense()

    @pl.when(pl.program_id(0) == pl.num_programs(0) - 1)
    def _():
        if not last:
            pltpu.sync_copy(acc, out_ref)
        else:
            size = seq // chunks

            def emit(k):
                start = pl.multiple_of(starts_ref[chunks + k], 64)
                return acc[pl.ds(start, size), :].astype(bf16)

            for k in range(chunks):
                piece = emit(k)
                all_ref[k * size : (k + 1) * size, :] = piece
                if n_send and k >= chunks - 4:
                    j = k - chunks + 4
                    dst, at = sends[j // 2], j % 2
                    dst[at * size : (at + 1) * size, :] = piece


def attend_back(meta, rand, starts, q, grad, pieces, seq, carried, chunks, n_send, tokens):
    rows = tokens // 2
    steps = rows // (PAIR * BLK)
    count = len(pieces)
    last = carried is not None
    dq_block = (lambda g, m, r, s: (g + steps, 0)) if last else (lambda g, m, r, s: (g, 0))
    out_specs = [pl.BlockSpec((PAIR * BLK, 256), dq_block)]
    out_shape = [jax.ShapeDtypeStruct((tokens, 256), bf16)]
    if last:
        out_specs += [pl.BlockSpec((seq, 384), lambda g, m, r, s: (0, 0), pipeline_mode=pl.Buffered(1))]
        sizes = [2] * n_send
        out_specs += [
            pl.BlockSpec((n * seq // chunks, 384), lambda g, m, r, s: (0, 0), pipeline_mode=pl.Buffered(1))
            for n in sizes
        ]
        out_shape += [jax.ShapeDtypeStruct((seq, 384), bf16)]
        out_shape += [jax.ShapeDtypeStruct((n * seq // chunks, 384), bf16) for n in sizes]
    else:
        out_specs += [ANY]
        out_shape += [jax.ShapeDtypeStruct((seq, 384), f32)]
    return call(
        functools.partial(bwd_kernel, count, last, chunks, n_send),
        grid_spec=pltpu.PrefetchScalarGridSpec(
            num_scalar_prefetch=3,
            grid=(steps,),
            in_specs=[q_spec(steps), pl.BlockSpec((PAIR * BLK, 256), lambda g, m, r, s: (g, 0))]
            + [ANY] * (count + (2 if last else 0)),
            out_specs=out_specs,
            scratch_shapes=[
                pltpu.VMEM((seq, 384), bf16),
                pltpu.VMEM((seq, 384), f32),
                pltpu.SemaphoreType.DMA((chunks + 1,)),
            ],
        ),
        out_shape=out_shape,
        input_output_aliases={3 + 2 + count + 1: 0} if last else {},
        compiler_params=pltpu.CompilerParams(vmem_limit_bytes=seq * (4608 if last else 2304) + 10 * MIB),
        cost_estimate=LIGHT,
        name="attend_back",
    )(meta, rand, starts, q, grad, *pieces, *(carried if last else ()))


def split_kernel(count, cuts, length, starts_ref, *refs):
    pieces, outs = refs[:count], refs[count:]
    rows = pieces[0].shape[0] - 16
    for (low, high, at), out in zip(cuts, outs):
        width = out.shape[1]
        for k, piece in enumerate(pieces):
            start = pl.multiple_of(starts_ref[k] * rows, 32)
            part = piece[0:rows, low:high]
            if at:
                part = jnp.concatenate([jnp.zeros((rows, at), bf16), part], axis=1)
            if at + high - low < width:
                part = jnp.concatenate(
                    [part, jnp.zeros((rows, width - at - high + low), bf16)], axis=1
                )
            out[pl.ds(start, rows), :] = part
    vectors = [piece[rows : rows + 16, 0:length].astype(f32) for piece in pieces]
    for slot in range(count):
        value = jnp.zeros((16, length), f32)
        for k in range(count):
            value = jnp.where(starts_ref[k] == slot, vectors[k], value)
        outs[-1][:, slot * length : (slot + 1) * length] = value


def split_call(pieces, places, cuts, widths, length):
    count = len(pieces)
    rows = pieces[0].shape[0]
    outs = [jax.ShapeDtypeStruct((count * (rows - 16), w), bf16) for w in widths]
    outs += [jax.ShapeDtypeStruct((16, count * length), f32)]
    return call(
        functools.partial(split_kernel, count, cuts, length),
        grid_spec=pltpu.PrefetchScalarGridSpec(
            num_scalar_prefetch=1,
            grid=(1,),
            in_specs=[whole_block(p) for p in pieces],
            out_specs=[whole_block(v) for v in outs],
        ),
        out_shape=outs,
        compiler_params=pltpu.CompilerParams(vmem_limit_bytes=14 * MIB),
        cost_estimate=LIGHT,
        name="split",
    )(places, *pieces)


def unpack_kernel(count, length, d_ref, out_ref, wi_ref, wp_ref, vec_ref, wo_ref, sem):
    copy = pltpu.make_async_copy(out_ref, wo_ref, sem)
    copy.start()
    units = wi_ref.shape[1]
    step = d_ref.shape[0] // count
    rows = step - 16
    for k in range(count):
        there, here = slice(k * step, k * step + rows), slice(k * rows, (k + 1) * rows)
        wi_ref[here, :] = d_ref[there, 0:units]
        wp_ref[here, 0:64] = jnp.zeros((rows, 64), bf16)
        wp_ref[here, 64:256] = d_ref[there, units : units + 192]
        vec_ref[:, k * length : (k + 1) * length] = d_ref[
            k * step + rows : (k + 1) * step, 0:length
        ].astype(f32)
    copy.wait()


def unpack_call(count, length, d, out):
    rows, width = out.shape
    units = d.shape[1] - 192
    outs = [
        jax.ShapeDtypeStruct((rows, units), bf16),
        jax.ShapeDtypeStruct((rows, 256), bf16),
        jax.ShapeDtypeStruct((16, count * length), f32),
        jax.ShapeDtypeStruct((rows, width), bf16),
    ]
    return call(
        functools.partial(unpack_kernel, count, length),
        ins="h",
        outs="v",
        grid=(1,),
        in_specs=[whole_block(d), HBM],
        out_specs=[VM] * 4,
        out_shape=outs,
        scratch_shapes=[pltpu.SemaphoreType.DMA],
        compiler_params=pltpu.CompilerParams(vmem_limit_bytes=8 * MIB),
        cost_estimate=LIGHT,
        name="unpack",
    )(d, out)


TILE = 256


def proj_kernel(keep_ref, got_ref, wm_ref, wt_ref, peer_ref, own_ref):
    half = peer_ref.shape[0]
    for k, out in enumerate((peer_ref, own_ref)):
        rows = slice(k * half, (k + 1) * half)
        value = nt(keep_ref[rows, :], wm_ref[...]) + nt(got_ref[rows, :], wt_ref[...])
        out[...] = value.astype(out.dtype)


def in_vmem(kernel, out_shape, limit, name, aliases=None, outs="v", ins="v"):
    return lambda *args: call(
        kernel,
        ins=ins,
        outs=outs,
        in_specs=[VM] * len(args),
        out_specs=[VM] * len(out_shape),
        out_shape=out_shape,
        input_output_aliases=aliases or {},
        compiler_params=pltpu.CompilerParams(vmem_limit_bytes=limit * MIB),
        cost_estimate=LIGHT,
        name=name,
    )(*args)


def project(keep, got, wm, wt):
    rows, width = keep.shape[0] // 2, wm.shape[0]
    outs = [jax.ShapeDtypeStruct((rows, width), bf16), jax.ShapeDtypeStruct((rows, width), f32)]
    return in_vmem(proj_kernel, outs, 8, "project")(keep, got, wm, wt)


def stats(value):
    center = jnp.mean(value, axis=-1, keepdims=True)
    offset = value - center
    inverse = lax.rsqrt(jnp.mean(offset * offset, axis=-1, keepdims=True) + EPSILON)
    return offset * inverse, inverse


def fetch_two(slot_ref, src, dst, came, got, sems):
    start = pl.multiple_of(slot_ref[0] * dst.shape[0], 64)
    load_all([(src.at[pl.ds(start, dst.shape[0])], dst), (came, got)], sems)


def norm_one_kernel(
    slot_ref, x_ref, came_ref, part_ref, vec_ref, resid_ref, hidden_ref, low_ref, rows_ref, got_ref, sems
):
    fetch_two(slot_ref, x_ref, rows_ref, came_ref, got_ref, sems)
    for k in range(0, part_ref.shape[0], TILE):
        rows = slice(k, k + TILE)
        resid = rows_ref[rows, :].astype(f32) + (
            part_ref[rows, :] + got_ref[rows, :].astype(f32) + vec_ref[1:2, :]
        )
        resid_ref[rows, :] = resid
        normed, _ = stats(resid)
        hidden = normed * vec_ref[2:3, :] + vec_ref[3:4, :]
        hidden_ref[rows, :] = hidden
        low_ref[rows, :] = hidden.astype(bf16)


def norm_one(slot, x, part, got, vec):
    rows, width = part.shape
    return call(
        norm_one_kernel,
        ins="hhv",
        outs="v",
        grid_spec=pltpu.PrefetchScalarGridSpec(
            num_scalar_prefetch=1,
            grid=(1,),
            in_specs=[HBM, HBM, VM, VM],
            out_specs=[VM] * 3,
            scratch_shapes=[pltpu.VMEM((rows, width), bf16)] * 2 + [pltpu.SemaphoreType.DMA((2,))],
        ),
        out_shape=[jax.ShapeDtypeStruct((rows, width), t) for t in (f32, f32, bf16)],
        compiler_params=pltpu.CompilerParams(vmem_limit_bytes=8 * MIB),
        cost_estimate=LIGHT,
        name="norm_one",
    )(slot, x, got, part, vec)


def add_sums(total, low, error, normed):
    sums = [jnp.sum(v, axis=0, keepdims=True) for v in (low.astype(f32), error * normed, error)]
    return sums if total is None else [x + z for x, z in zip(total, sums)]


def ride(low_ref, sums_ref, total):
    sums = jnp.concatenate(total + [jnp.zeros((5, low_ref.shape[1]), f32)], axis=0)
    sums_ref[...] = sums
    rows = low_ref.shape[0] - 16
    low_ref[rows : rows + 16, :] = jnp.concatenate([sums, jnp.zeros_like(sums)], axis=0).astype(bf16)


def norm_two_kernel(
    slot_ref, cot_ref, came_ref, hidden_ref, part_ref, vec_ref,
    out_ref, low_ref, grad_ref, sums_ref, rows_ref, got_ref, sems,
):
    fetch_two(slot_ref, cot_ref, rows_ref, came_ref, got_ref, sems)
    gain = vec_ref[5:6, :]
    total = None
    for k in range(0, part_ref.shape[0], TILE):
        rows = slice(k, k + TILE)
        value = hidden_ref[rows, :] + (part_ref[rows, :] + got_ref[rows, :].astype(f32)) + vec_ref[4:5, :]
        normed, inverse = stats(value)
        position = slot_ref[1] + k + lax.broadcasted_iota(jnp.int32, (TILE, 1), 0)
        live = (position < slot_ref[2]).astype(f32)
        out_ref[rows, :] = ((normed * gain + vec_ref[6:7, :]) * live).astype(bf16)
        error = rows_ref[rows, :].astype(f32) * live
        inner = error * gain
        first = jnp.mean(inner, axis=-1, keepdims=True)
        second = jnp.mean(inner * normed, axis=-1, keepdims=True)
        grad = inverse * (inner - first - normed * second)
        grad_ref[rows, :] = grad
        low = grad.astype(bf16)
        low_ref[rows, :] = low
        total = add_sums(total, low, error, normed)
    ride(low_ref, sums_ref, total)


def norm_two(slot, cotangent, hidden, part, got, vec):
    rows, width = part.shape
    return call(
        norm_two_kernel,
        ins="hhv",
        outs="hvvv",
        grid_spec=pltpu.PrefetchScalarGridSpec(
            num_scalar_prefetch=1,
            grid=(1,),
            in_specs=[HBM] * 2 + [VM] * 3,
            out_specs=[pl.BlockSpec((rows, width), lambda g, s: (0, 0))] + [VM] * 3,
            scratch_shapes=[pltpu.VMEM((rows, width), bf16)] * 2 + [pltpu.SemaphoreType.DMA((2,))],
        ),
        out_shape=[
            jax.ShapeDtypeStruct((rows, width), bf16),
            jax.ShapeDtypeStruct((rows + 16, width), bf16),
            jax.ShapeDtypeStruct((rows, width), f32),
            jax.ShapeDtypeStruct((8, width), f32),
        ],
        compiler_params=pltpu.CompilerParams(vmem_limit_bytes=10 * MIB),
        cost_estimate=LIGHT,
        name="norm_two",
    )(slot, cotangent, got, hidden, part, vec)


def norm_one_back_kernel(resid_ref, two_ref, part_ref, got_ref, vec_ref, grad_ref, low_ref, sums_ref):
    total = None
    for k in range(0, part_ref.shape[0], TILE):
        rows = slice(k, k + TILE)
        normed, inverse = stats(resid_ref[rows, :])
        error = two_ref[rows, :] + (part_ref[rows, :] + got_ref[rows, :].astype(f32))
        inner = error * vec_ref[2:3, :]
        first = jnp.mean(inner, axis=-1, keepdims=True)
        second = jnp.mean(inner * normed, axis=-1, keepdims=True)
        grad = inverse * (inner - first - normed * second)
        grad_ref[rows, :] = grad
        low = grad.astype(bf16)
        low_ref[rows, :] = low
        total = add_sums(total, low, error, normed)
    ride(low_ref, sums_ref, total)


def norm_one_back(resid, two, part, got, vec):
    rows, width = part.shape
    outs = [
        jax.ShapeDtypeStruct((rows, width), f32),
        jax.ShapeDtypeStruct((rows + 16, width), bf16),
        jax.ShapeDtypeStruct((8, width), f32),
    ]
    return in_vmem(norm_one_back_kernel, outs, 10, "norm_one_back")(resid, two, part, got, vec)


ERFC = (
    -1.26551223, 1.00002368, 0.37409196, 0.09678418, -0.18628806,
    0.27886807, -1.13520398, 1.48851587, -0.82215223, 0.17087277,
)


def gelu_pair(pre):
    z = jnp.abs(pre) * math.sqrt(0.5)
    t = 1.0 / (1.0 + 0.5 * z)
    poly = jnp.full_like(t, ERFC[-1])
    for coefficient in ERFC[-2::-1]:
        poly = poly * t + coefficient
    square = -z * z
    tail = 0.5 * t * jnp.exp(square + poly)
    cdf = jnp.where(pre < 0, tail, 1.0 - tail)
    density = jnp.exp(square) * (1.0 / math.sqrt(2.0 * math.pi))
    return (pre * cdf).astype(bf16), (cdf + pre * density).astype(bf16)


def mlp_kernel(
    base, hid_ref, wim_ref, wit_ref, bm_ref, bt_ref, wom_ref, wot_ref, *rest
):
    act_ref, slope_ref, all_ref, part_ref = rest[-4:]
    units = wim_ref.shape[1]
    for k in range(0, part_ref.shape[0], TILE):
        rows, there = slice(k, k + TILE), slice(base + k, base + k + TILE)
        hid = hid_ref[rows, :]
        all_ref[there, :] = hid
        total = None
        for j, (wi, b, wo) in enumerate(((wim_ref, bm_ref, wom_ref), (wit_ref, bt_ref, wot_ref))):
            act, slope = gelu_pair(nn(hid, wi[...]) + b[0:1, :])
            act_ref[there, j * units : (j + 1) * units] = act
            slope_ref[there, j * units : (j + 1) * units] = slope
            value = nt(act, wo[...])
            total = value if total is None else total + value
        part_ref[rows, :] = total.astype(part_ref.dtype)


def mlp(hid, wi_m, wi_t, b_m, b_t, wo_m, wo_t, earlier, dtype):
    rows, width = hid.shape
    units = wi_m.shape[1]
    big = jax.ShapeDtypeStruct((2 * rows, 2 * units), bf16)
    outs = [big, big, jax.ShapeDtypeStruct((2 * rows, width), bf16), jax.ShapeDtypeStruct((rows, width), dtype)]
    second = earlier is not None
    kernel = functools.partial(mlp_kernel, rows if second else 0)
    aliases = {7 + k: k for k in range(3)} if second else {}
    args = (hid, wi_m, wi_t, b_m, b_t, wo_m, wo_t) + (tuple(earlier) if second else ())
    return in_vmem(kernel, outs, 14, "mlp", aliases)(*args)


def mlp_back_kernel(base, gm_ref, slope_ref, wim_ref, wit_ref, wom_ref, wot_ref, *rest):
    gp_ref, all_ref, part_ref, sums_ref = rest[-4:]
    units = wim_ref.shape[1]
    sums = [None, None]
    for k in range(0, part_ref.shape[0], TILE):
        rows, there = slice(k, k + TILE), slice(base + k, base + k + TILE)
        gm = gm_ref[rows, :]
        all_ref[there, :] = gm
        total = None
        for j, (wi, wo) in enumerate(((wim_ref, wom_ref), (wit_ref, wot_ref))):
            cols = slice(j * units, (j + 1) * units)
            gp = (nn(gm, wo[...]) * slope_ref[there, cols].astype(f32)).astype(bf16)
            gp_ref[there, cols] = gp
            column = jnp.sum(gp.astype(f32), axis=0, keepdims=True)
            sums[j] = column if sums[j] is None else sums[j] + column
            value = nt(gp, wi[...])
            total = value if total is None else total + value
        part_ref[rows, :] = total.astype(part_ref.dtype)
    sums_ref[...] = jnp.concatenate(sums + [jnp.zeros((6, units), f32)], axis=0)


def mlp_back(gm, slope, wi_m, wi_t, wo_m, wo_t, earlier, dtype):
    rows, width = gm.shape[0] - 16, gm.shape[1]
    units = wi_m.shape[1]
    outs = [
        jax.ShapeDtypeStruct((2 * rows, 2 * units), bf16),
        jax.ShapeDtypeStruct((2 * rows, width), bf16),
        jax.ShapeDtypeStruct((rows, width), dtype),
        jax.ShapeDtypeStruct((8, units), f32),
    ]
    second = earlier is not None
    kernel = functools.partial(mlp_back_kernel, rows if second else 0)
    aliases = {6 + k: k for k in range(2)} if second else {}
    args = (gm, slope, wi_m, wi_t, wo_m, wo_t) + (tuple(earlier) if second else ())
    return in_vmem(kernel, outs, 14, "mlp_back", aliases)(*args)


def heads_kernel(
    peer_ref, own_ref, wm_ref, wt_ref, two_ref, twop_ref, one_ref, dbi_a_ref, dbi_b_ref,
    send_ref, keep_ref, both_ref, vec_ref,
):
    half = peer_ref.shape[0] - 16
    for k, ref in enumerate((peer_ref, own_ref)):
        rows = slice(k * half, (k + 1) * half)
        grad = ref[0:half, :]
        both_ref[rows, :] = grad
        send_ref[rows, :] = nn(grad, wt_ref[...]).astype(bf16)
        keep_ref[rows, :] = nn(grad, wm_ref[...]).astype(bf16)
    two = two_ref[...] + twop_ref[half : half + 16, :].astype(f32)[0:8]
    one = one_ref[...] + peer_ref[half : half + 16, :].astype(f32)[0:8]
    dbi = dbi_a_ref[...] + dbi_b_ref[...]
    vec = jnp.concatenate([two[0:3], one[0:3], dbi[1:2], dbi[0:1]], axis=0)
    vec_ref[...] = vec
    width = vec.shape[1] // 3
    packed = jnp.concatenate([vec[:, k * width : (k + 1) * width] for k in range(3)], axis=0)
    packed = jnp.concatenate([packed, jnp.zeros((8, width), f32)], axis=0)
    send_ref[2 * half : 2 * half + 32, :] = packed.astype(bf16)


def heads_back(peer, own, wm, wt, two, gm_peer, one, dbi_a, dbi_b):
    rows, width = peer.shape[0] - 16, peer.shape[1]
    shapes = [(2 * rows + 32, 256), (2 * rows, 256), (2 * rows, width)]
    outs = [jax.ShapeDtypeStruct(v, bf16) for v in shapes] + [jax.ShapeDtypeStruct((8, width), f32)]
    return in_vmem(heads_kernel, outs, 8, "heads_back", outs="v-v-")(
        peer, own, wm, wt, two, gm_peer, one, dbi_a, dbi_b
    )


def input_kernel(count, dq_ref, mine_ref, *rest):
    got_ref = rest[0] if count else None
    wq_ref, wkv_ref = rest[count : count + 2]
    adds, out_ref = rest[count + 2 : -1], rest[-1]
    both = mine_ref[...]
    if count:
        both = (both.astype(f32) + got_ref[...].astype(f32)).astype(bf16)
    total = nt(dq_ref[...], wq_ref[...]) + nt(both, wkv_ref[...])
    for add in adds:
        total = total + add[...].astype(f32)
    out_ref[...] = total.astype(bf16)


def input_back(k, dq, mine, got, got_block, wq, wkv, adds):
    got = [] if got is None else [got]
    rows, width = dq.shape[0] // 4, wq.shape[0]
    out = jax.ShapeDtypeStruct((rows, width), bf16)
    return call(
        functools.partial(input_kernel, len(got)),
        grid=(1,),
        in_specs=[
            pl.BlockSpec((rows, 256), lambda g: (k, 0)),
            pl.BlockSpec((rows, 384), lambda g: (k, 0)),
        ]
        + [pl.BlockSpec((rows, 384), lambda g: (got_block, 0)) for _ in got]
        + [whole_block(v) for v in [wq, wkv] + adds],
        out_specs=whole_block(out),
        out_shape=out,
        compiler_params=pltpu.CompilerParams(vmem_limit_bytes=8 * MIB),
        cost_estimate=LIGHT,
        name="input_back",
    )(dq, mine, *got, wq, wkv, *adds)


def gather_kernel(dwq_ref, dwkv_ref, dwp_ref, got_ref, vec_ref, peer_ref, dq_ref, dkv_ref, table):
    count = (table.shape[0] - got_ref.shape[0]) // 16
    shard = got_ref.shape[0] // count
    dbq = jnp.sum(dq_ref[...].astype(f32), axis=0, keepdims=True)[:, 0:192]
    dbv = jnp.sum(dkv_ref[:, 128:384].astype(f32), axis=0, keepdims=True)
    dbv = jnp.concatenate([dbv[:, 128:256], dbv[:, 64:128]], axis=1)
    came = peer_ref[...].astype(f32)
    came = jnp.concatenate([came[8 * k : 8 * k + 8, :] for k in range(3)], axis=1)
    vectors = [vec_ref[k : k + 1, :] + came[k : k + 1, :] for k in (0, 1, 2, 4, 5, 3)]
    vectors += [vec_ref[7:8, :] + came[6:7, :], dbq, dbv]
    for j in range(count):
        rows = slice(j * shard, (j + 1) * shard)
        base = j * (shard + 16)
        main = slice(base, base + shard)
        table[main, 0:192] = dwq_ref[rows, 0:192].astype(bf16)
        table[main, 192:576] = dwkv_ref[rows, :].astype(bf16)
        table[main, 576:768] = (dwp_ref[rows, 64:256] + got_ref[rows, 64:256].astype(f32)).astype(bf16)
        parts = []
        for vector in vectors:
            n = vector.shape[1] // count
            parts.append(
                jnp.concatenate([vector[:, j * n : (j + 1) * n], jnp.zeros((1, 768 - n), f32)], axis=1)
            )
        parts.append(jnp.zeros((16 - len(parts), 768), f32))
        table[base + shard : base + shard + 16, :] = jnp.concatenate(parts, axis=0).astype(bf16)


def gather_small(count, dwq, dwkv, dwp, got, vec, peer, dq, dkv):
    rows = dwq.shape[0] + 16 * count
    out = jax.ShapeDtypeStruct((rows, 768), bf16)
    args = (dwq, dwkv, dwp, got, vec, peer, dq, dkv)
    return call(
        gather_kernel,
        ins="-",
        outs="h",
        grid=(1,),
        in_specs=[whole_block(v) for v in args[0:5]]
        + [pl.BlockSpec((32, 256), lambda g: (peer.shape[0] // 32 - 1, 0))]
        + [whole_block(v) for v in args[6:]],
        out_specs=whole_block(out),
        out_shape=out,
        compiler_params=pltpu.CompilerParams(vmem_limit_bytes=20 * MIB),
        cost_estimate=LIGHT,
        name="gather_small",
    )(*args)


def core_swap(value):
    return lax.ppermute(value, TP, [(0, 1), (1, 0), (2, 3), (3, 2)])


def y_swap(value):
    return lax.ppermute(value, TP, [(0, 2), (2, 0), (1, 3), (3, 1)])


def x_swap(value):
    return lax.ppermute(value, CTX, [(0, 1), (1, 0)])


def z_shift(value, shift):
    count = lax.axis_size(FSDP)
    return lax.ppermute(value, FSDP, [(i, (i + shift) % count) for i in range(count)])


def after(value, *others):
    return lax.optimization_barrier((value,) + others)[0]


def z_order():
    count = lax.axis_size(FSDP)
    return sorted(range(1, count), key=lambda s: min(s, count - s))


def z_gather(piece, gate=None):
    got = [piece]
    for k, shift in enumerate(z_order()):
        got.append(z_shift(piece if gate is None else after(piece, gate), shift))
    return got


def z_places():
    count = lax.axis_size(FSDP)
    me = lax.axis_index(FSDP)
    return [me] + [lax.rem(me - s + count, count) for s in z_order()]


def rows_at(array, start, count):
    return lax.dynamic_slice_in_dim(array, start, count, axis=0)


def on_device(
    layer_in,
    cotangent,
    lengths,
    rand_blocks,
    w_query,
    b_query,
    w_key,
    w_value,
    b_value,
    w_proj,
    b_proj,
    gain_one,
    shift_one,
    w_in,
    b_in,
    w_out,
    b_out,
    gain_two,
    shift_two,
):
    tokens, width = layer_in.shape
    ctx_count = lax.axis_size(CTX)
    fsdp_count = lax.axis_size(FSDP)
    ctx = lax.axis_index(CTX)
    tp = lax.axis_index(TP)
    y, c = tp // 2, tp % 2
    seq = tokens * ctx_count
    half, quarter = tokens // 2, tokens // 4
    shard = w_query.shape[0]
    units = w_in.shape[1]
    pair = ctx_count == 2
    order = [2 * y + 1 - c, 2 * y + c, 2 * (1 - y) + 1 - c, 2 * (1 - y) + c]
    own_rows, other_rows = ctx * tokens, (1 - ctx) * tokens
    places = jnp.stack(z_places()).astype(jnp.int32)

    first = open_call(
        layer_in, [order[1], order[3]], quarter, w_query, w_key, w_value, b_query, b_value
    )
    attn_piece, x_send = first
    x_got = x_swap(x_send) if pair else None
    attn_pieces = z_gather(attn_piece)
    vecs = [b_in, b_proj, gain_one, shift_one, b_out, gain_two, shift_two]
    in_piece = pack_call(w_in, w_proj, after(vecs, attn_piece))
    in_m = lax.all_gather(after(in_piece, *attn_pieces), FSDP, axis=0, tiled=True)
    out_m = lax.all_gather(after(w_out.T, in_piece), FSDP, axis=0, tiled=True)
    in_t = y_swap(in_m)

    wq, wkv, bias = split_call(
        attn_pieces, places, ((0, 192, 0), (192, 576, 0)), (256, 384), b_query.shape[0]
    )
    bq = jnp.concatenate([bias[0:1], jnp.zeros((1, 64), f32)], axis=1)
    bkv = jnp.concatenate([jnp.zeros((1, 192), f32), bias[1:2, 128:192], bias[1:2, 0:128]], axis=1)

    def kv_of(rows):
        return (nn(rows, wkv) + bkv).astype(bf16)

    q_all = (nn(layer_in, wq) + bq).astype(bf16) * jnp.asarray(0.125, bf16)
    if pair:
        x_got = after(x_got, wkv)
        kv_own = kv_of(layer_in)
        x_core = core_swap(x_got)
        kv_pieces = [kv_own, kv_of(x_got), kv_of(x_core)]
        kv_starts = [own_rows + k * quarter for k in range(4)]
        kv_starts += [other_rows + order[k] * quarter for k in (1, 3, 0, 2)]
    else:
        x_all = lax.all_gather(layer_in, CTX, axis=0, tiled=True)
        kv_pieces, kv_starts = [kv_of(x_all)], [k * quarter for k in range(seq // quarter)]
    blocks = tokens // BLK
    rand = rand_blocks.reshape(-1)
    live = lengths[0]

    def meta(half_index):
        values = [half_index * (blocks // 2), ctx * blocks, live, (1 - c) * (blocks // 4)]
        return jnp.stack(values).astype(jnp.int32)

    as_table = lambda values: jnp.stack([jnp.asarray(v, jnp.int32) for v in values])
    chunks = seq // quarter
    starts = as_table(kv_starts)
    kv_pieces[-1] = after(kv_pieces[-1], in_m)
    o_send = attend(meta(1 - y), rand, starts, q_all, kv_pieces, seq, half, chunks)
    o_got = y_swap(o_send)
    o_keep = attend(
        meta(y), rand, starts, after(q_all, o_send), kv_pieces, seq, half, chunks
    )
    o_keep, o_got, in_t, out_m = lax.optimization_barrier((o_keep, o_got, in_t, out_m))
    out_t = y_swap(out_m)
    x_order = collect(after(layer_in, out_m), order, [x_core, x_got] if pair else [])
    out_t = after(out_t, x_order)
    wi_m, wp_m, vec, wo_m = unpack_call(fsdp_count, b_in.shape[0], in_m, out_m)
    wi_t, wp_t, vec_t, wo_t = unpack_call(fsdp_count, b_in.shape[0], in_t, out_t)

    slot = jnp.stack([tp, ctx * tokens + tp * quarter, live]).astype(jnp.int32)
    part_peer, part_own = project(o_keep, o_got, wp_m, wp_t)
    resid, hidden, hid_own = norm_one(slot, layer_in, part_own, core_swap(part_peer), vec)
    hid_peer = core_swap(hid_own)

    weights = (wi_m, wi_t, vec, vec_t, wo_m, wo_t)
    outs = mlp(hid_peer, *weights, None, bf16)
    mlp_got = core_swap(outs[3])
    act, slope, hid, part_own = mlp(hid_own, *weights, outs[0:3], f32)
    out_own, gm_own, grad_two, sums_two = norm_two(slot, cotangent, hidden, part_own, mlp_got, vec)
    gm_peer = core_swap(gm_own)
    out_other = y_swap(out_own)
    weights = (wi_m, wi_t, wo_m, wo_t)
    outs = mlp_back(gm_peer, slope, *weights, None, bf16)
    gh_got, dbi_peer = core_swap(outs[2]), outs[3]
    gp, gm, gh_own, dbi_own = mlp_back(gm_own, slope, *weights, outs[0:2], f32)
    grad_one, gb_own, sums_one = norm_one_back(resid, grad_two, gh_own, gh_got, vec)
    go_send, go_keep, gb, vec_sum = heads_back(
        core_swap(gb_own), gb_own, wp_m, wp_t, sums_two, gm_peer, sums_one, dbi_peer, dbi_own
    )
    go_got = y_swap(go_send)

    def z_sum(value):
        return lax.psum_scatter(value, FSDP, scatter_dimension=0, tiled=True)

    def x_sum(value):
        value = value.astype(bf16)
        return value.astype(f32) + x_swap(value).astype(f32) if pair else lax.psum(value, CTX).astype(f32)

    dwo = z_sum(tn(gm, act).astype(bf16))
    dwi = z_sum(tn(hid, gp).astype(bf16))
    dwp_t = tn(gb, o_got).astype(bf16)

    if pair:
        chunk_rows = [own_rows + k * quarter for k in order] + [other_rows + k * quarter for k in order]
    else:
        chunk_rows = [k * quarter for k in range(chunks)]
    starts = as_table(kv_starts + chunk_rows)
    n_send = 2 if pair else 0
    go_keep = after(go_keep, dwp_t)
    carried = attend_back(
        meta(y), rand, starts, q_all, go_keep, kv_pieces, seq, None, chunks, n_send, tokens
    )
    go_got, dwo, *carried = lax.optimization_barrier((go_got, dwo, *carried))
    dwo_got = y_swap(dwo[:, units:])
    dwp_got = y_swap(after(dwp_t, carried[1]))
    outs = attend_back(
        meta(1 - y), rand, starts, q_all, go_got, kv_pieces, seq, (carried[1], carried[0]), chunks, n_send, tokens
    )
    outs, dwo_got, dwp_got = lax.optimization_barrier((outs, dwo_got, dwp_got))
    dq, dkv = outs[0], outs[1]
    dwp = tn(after(gb, dkv), o_keep)

    gate = dkv
    if pair:
        came = [x_swap(v) for v in outs[2:]]
        got = [came[0], came[0], came[1], came[1]]
        mine = dkv
        gate = came[1]
    else:
        got = [None] * 4
        mine = collect(lax.psum_scatter(dkv, CTX, scatter_dimension=0, tiled=True), order, [])

    def back_of(k, *adds):
        return input_back(k, dq, mine, got[k], k % 2, wq, wkv, list(adds))

    sent = [core_swap(back_of(k)) for k in (0, 2)]
    lead = back_of(1, grad_one, sent[0])
    rear = back_of(3, sent[1])
    lead_sum = (lead.astype(f32) + y_swap(rear).astype(f32)).astype(bf16)
    rear_sum = (rear.astype(f32) + y_swap(lead).astype(f32)).astype(bf16)
    out_own, out_other = after(out_own, gate), after(out_other, gate)
    layer_out = place(
        [core_swap(out_own), out_own, core_swap(out_other), out_other],
        order,
        tokens,
    )
    grad_input = place(
        [core_swap(lead_sum), lead_sum, core_swap(rear_sum), rear_sum],
        order,
        tokens,
    )

    x_late = after(x_order, dkv)
    dwq = tn(x_late[0:tokens], dq)
    dwkv = tn(x_late if pair else x_all, dkv)
    both = z_sum(gather_small(fsdp_count, dwq, dwkv, dwp, dwp_got, vec_sum, go_got, dq, dkv))
    dwo = x_sum(dwo[:, 0:units].astype(f32) + after(dwo_got, gate).astype(f32))
    dwi_got = y_swap(after(dwi, gate)[:, units:])
    dwi = x_sum(dwi[:, 0:units].astype(f32) + dwi_got.astype(f32))
    both = x_sum(both)
    dwq = both[0:shard, 0:192]
    dwk = both[0:shard, 192:384]
    dwv = jnp.concatenate([both[0:shard, 448:576], both[0:shard, 384:448]], axis=1)
    dwp = both[0:shard, 576:768]
    dwp = jnp.concatenate([dwp[:, 64:192], dwp[:, 0:64]], axis=1).T
    sizes = [shard] * 6 + [units // fsdp_count, 192 // fsdp_count, 192 // fsdp_count]
    db_out, dg2, ds2, dg1, ds1, db_proj, db_in, db_query, db_value = [
        both[shard + k, 0:size] for k, size in enumerate(sizes)
    ]

    return (
        layer_out,
        grad_input,
        dwq,
        db_query,
        dwk,
        dwv,
        db_value,
        dwp,
        db_proj,
        dg1,
        ds1,
        dwi,
        db_in,
        dwo.T,
        db_out,
        dg2,
        ds2,
    )


def solution(mesh):
    rows = P((FSDP, CTX), None)
    vector, unit = P(FSDP), P((TP, FSDP))
    column, row = P(FSDP, TP), P(TP, FSDP)
    return jax.shard_map(
        on_device,
        mesh=mesh,
        in_specs=(
            rows, rows, vector, P(FSDP, CTX, None), column, unit, column, column, unit, row,
            vector, vector, vector, column, unit, row, vector, vector, vector,
        ),
        out_specs=(
            rows, rows, column, unit, column, column, unit, row, vector, vector, vector,
            column, unit, row, vector, vector, vector,
        ),
        check_vma=False,
    )
```

```python
import functools
import math

import jax
import jax.numpy as jnp
from jax import lax
from jax.experimental import pallas as pl
from jax.experimental.pallas import tpu as pltpu
from jax.sharding import PartitionSpec as P

BLK = 64
PAIR = 2
MASKED = -1e30
CHUNK = 512
EPSILON = 1e-05
FSDP, CTX, TP = "fsdp", "ctx", "tp"
f32, bf16 = jnp.float32, jnp.bfloat16
ANY = pl.BlockSpec(memory_space=pl.ANY)


VM = pl.BlockSpec(memory_space=pltpu.VMEM)
HBM = pl.BlockSpec(memory_space=pltpu.HBM)
MIB = 1 << 20
LIGHT = pl.CostEstimate(flops=0, bytes_accessed=0, transcendentals=0)
SPACES = {"h": pltpu.HBM, "v": pltpu.VMEM}


def call(kernel, out_shape, ins="", outs="", **options):
    spec = options.get("grid_spec")
    tables = spec.num_scalar_prefetch if spec is not None else 0

    def letter(text, k):
        return text[min(k, len(text) - 1)] if text else "h"

    many = isinstance(out_shape, (list, tuple))
    shapes = list(out_shape) if many else [out_shape]
    shapes = [
        v if letter(outs, k) == "-" else SPACES[letter(outs, k)](v.shape, v.dtype)
        for k, v in enumerate(shapes)
    ]
    run = pl.pallas_call(kernel, out_shape=shapes if many else shapes[0], **options)

    def apply(*args):
        placed = [
            v if letter(ins, k) == "-" else pltpu.with_memory_space_constraint(v, SPACES[letter(ins, k)])
            for k, v in enumerate(args[tables:])
        ]
        return run(*args[0:tables], *placed)

    return apply


def nt(a, b):
    return lax.dot_general(a, b, (((1,), (1,)), ((), ())), preferred_element_type=f32)


def tn(a, b):
    return lax.dot_general(a, b, (((0,), (0,)), ((), ())), preferred_element_type=f32)


def nn(a, b):
    return jnp.dot(a, b, preferred_element_type=f32)


def place_kernel(count, slots_ref, *refs):
    for k in range(count):

        @pl.when(pl.program_id(0) == k)
        def _():
            refs[-1][...] = refs[k][...]


def place(pieces, slots, total, earlier=None):
    count = len(pieces)
    rows, width = pieces[0].shape
    more = [] if earlier is None else [earlier]
    return call(
        functools.partial(place_kernel, count),
        ins="-",
        outs="h",
        grid_spec=pltpu.PrefetchScalarGridSpec(
            num_scalar_prefetch=1,
            grid=(count,),
            in_specs=[whole_block(p) for p in pieces] + [ANY] * len(more),
            out_specs=pl.BlockSpec((rows, width), lambda g, s: (s[g], 0)),
        ),
        out_shape=jax.ShapeDtypeStruct((total, width), pieces[0].dtype),
        input_output_aliases={1 + count: 0} if more else {},
        compiler_params=pltpu.CompilerParams(vmem_limit_bytes=8 * MIB),
        cost_estimate=LIGHT,
        name="place",
    )(jnp.stack(slots).astype(jnp.int32), *pieces, *more)


def collect_kernel(count, slots_ref, x_ref, *refs):
    step = pl.program_id(0)

    @pl.when(step < 4)
    def _():
        refs[count][...] = x_ref[...]

    rows = x_ref.shape[0]
    parts = [(ref, at) for at in range(0, 2 * rows, rows) for ref in refs[:count]]
    for k, (ref, at) in enumerate(parts):

        @pl.when(step == 4 + k)
        def _():
            refs[count][...] = ref[at : at + rows, :]


def collect(x, slots, others):
    count = len(others)
    rows, width = x.shape[0] // 4, x.shape[1]
    steps = 4 + sum(v.shape[0] // rows for v in others)
    return call(
        functools.partial(collect_kernel, count),
        grid_spec=pltpu.PrefetchScalarGridSpec(
            num_scalar_prefetch=1,
            grid=(steps,),
            in_specs=[pl.BlockSpec((rows, width), lambda g, s: (s[jnp.minimum(g, 3)], 0))]
            + [whole_block(v) for v in others],
            out_specs=pl.BlockSpec((rows, width), lambda g, s: (g, 0)),
        ),
        out_shape=jax.ShapeDtypeStruct((steps * rows, width), x.dtype),
        compiler_params=pltpu.CompilerParams(vmem_limit_bytes=8 * MIB),
        cost_estimate=LIGHT,
        name="collect",
    )(jnp.stack(slots).astype(jnp.int32), x, *others)


def load_all(pairs, sems):
    copies = [pltpu.make_async_copy(src, dst, sems.at[k]) for k, (src, dst) in enumerate(pairs)]
    for copy in copies:
        copy.start()
    for copy in copies:
        copy.wait()


def open_kernel(count, slots_ref, x_ref, *refs):
    srcs, vecs = refs[0:4], refs[4:13]
    a_ref, half_ref, wq, wk, wv, wp, sems = refs[13:]
    size = half_ref.shape[0] // count
    pairs = []
    for k in range(count):
        start = pl.multiple_of(slots_ref[k] * size, 64)
        pairs.append((x_ref.at[pl.ds(start, size)], half_ref.at[pl.ds(k * size, size)]))
    load_all(list(zip(srcs, (wq, wk, wv, wp))) + pairs, sems)
    rows = wq.shape[0]
    a_ref[0:rows, 0:192] = wq[...]
    a_ref[0:rows, 192:384] = wk[...]
    a_ref[0:rows, 384:448] = wv[:, 128:192]
    a_ref[0:rows, 448:576] = wv[:, 0:128]
    turned_p = wp[...].T
    a_ref[0:rows, 576:640] = turned_p[:, 128:192]
    a_ref[0:rows, 640:768] = turned_p[:, 0:128]
    a_ref[rows : rows + 16, :] = jnp.zeros((16, 768), bf16)
    for k, vec in enumerate(vecs):
        n = vec.shape[0]
        a_ref[rows + k : rows + k + 1, 0:n] = vec[...].reshape(1, n)


def whole_block(value):
    zeros = (0,) * value.ndim
    return pl.BlockSpec(value.shape, lambda *_: zeros, pipeline_mode=pl.Buffered(1))


def open_call(x, slots, size, wq, wk, wv, wp, vecs):
    count = len(slots)
    rows, width = wq.shape[0], x.shape[1]
    srcs = [wq, wk, wv, wp]
    return call(
        functools.partial(open_kernel, count),
        grid_spec=pltpu.PrefetchScalarGridSpec(
            num_scalar_prefetch=1,
            grid=(1,),
            in_specs=[HBM] * 5 + [whole_block(v) for v in vecs],
            out_specs=[
                pl.BlockSpec((rows + 16, 768), lambda g, s: (0, 0)),
                pl.BlockSpec((count * size, width), lambda g, s: (0, 0)),
            ],
            scratch_shapes=[pltpu.VMEM(v.shape, bf16) for v in srcs]
            + [pltpu.SemaphoreType.DMA((4 + count,))],
        ),
        out_shape=[
            jax.ShapeDtypeStruct((rows + 16, 768), bf16),
            jax.ShapeDtypeStruct((count * size, width), bf16),
        ],
        compiler_params=pltpu.CompilerParams(vmem_limit_bytes=8 * MIB),
        cost_estimate=LIGHT,
        name="open",
    )(jnp.stack(slots).astype(jnp.int32), x, *srcs, *vecs)


def qkv_kernel(with_q, x_ref, wq_ref, wkv_ref, bias_ref, *outs):
    x = x_ref[...]
    zero = jnp.zeros((1, 64), f32)
    value_bias = bias_ref[1:2, :]
    bkv = jnp.concatenate([zero, zero, zero, value_bias[:, 128:192], value_bias[:, 0:128]], axis=1)
    outs[-1][...] = (nn(x, wkv_ref[...]) + bkv).astype(bf16)
    if with_q:
        bq = jnp.concatenate([bias_ref[0:1, :], zero], axis=1)
        outs[0][...] = (nn(x, wq_ref[...]) + bq).astype(bf16) * jnp.asarray(0.125, bf16)


def qkv(x, wq, wkv, bias, with_q):
    rows, width = x.shape
    tile = rows // 2 if rows <= 1024 else 512
    widths = [256, 384] if with_q else [384]
    return call(
        functools.partial(qkv_kernel, with_q),
        grid=(rows // tile,),
        in_specs=[pl.BlockSpec((tile, width), lambda g: (g, 0))]
        + [whole_block(v) for v in (wq, wkv, bias)],
        out_specs=[pl.BlockSpec((tile, w), lambda g: (g, 0)) for w in widths],
        out_shape=[jax.ShapeDtypeStruct((rows, w), bf16) for w in widths],
        compiler_params=pltpu.CompilerParams(vmem_limit_bytes=12 * MIB),
        cost_estimate=LIGHT,
        name="qkv",
    )(x, wq, wkv, bias)


def head_masks(places):
    group = lax.broadcasted_iota(jnp.int32, (1, 256), 1) // 64
    return [(group == place).astype(bf16) for place in places]


def spread(rows, masks):
    return jnp.concatenate([rows * m for m in masks], axis=0)


def fold(stacked, masks):
    n = stacked.shape[0] // 3
    out = stacked[0:n] * masks[0].astype(f32)
    for h in (1, 2):
        out = out + stacked[h * n : (h + 1) * n] * masks[h].astype(f32)
    return out


def tile_starts(i, b, rand_ref, seq):
    near = jnp.clip((i - 1) * BLK, 0, seq - 3 * BLK)
    near = pl.multiple_of(near, BLK)
    rand = [pl.multiple_of(rand_ref[3 * b + r] * BLK, BLK) for r in range(3)]
    return near, rand


def gather_tiles(kv, near, rand):
    parts = [kv[pl.ds(near, 3 * BLK), :]]
    parts += [kv[pl.ds(r, BLK), :] for r in rand]
    parts += [kv[0 : 2 * BLK, :]]
    return jnp.concatenate(parts, axis=0)


def tile_live(i, near, rand, length):
    out = []
    for j in range(3):
        blk = near // BLK + j
        out.append(jnp.where(jnp.abs(blk - i) <= 1, length - blk * BLK, 0))
    out += [length - r for r in rand]
    for g in range(2):
        out.append(jnp.where(jnp.abs(i - g) > 1, length - g * BLK, 0))
    return out


def load_pieces(size, starts_ref, pieces, kv, sems):
    copies = []
    for piece in pieces:
        for at in range(0, piece.shape[0], size):
            k = len(copies)
            start = pl.multiple_of(starts_ref[k], 64)
            copies.append(
                pltpu.make_async_copy(
                    piece.at[pl.ds(at, size)], kv.at[pl.ds(start, size)], sems.at[k]
                )
            )
    for copy in copies:
        copy.start()
    for copy in copies:
        copy.wait()


def step_block(meta_ref, step, steps):
    first = meta_ref[0] + PAIR * lax.rem(step + meta_ref[3] // PAIR, steps)
    return first, meta_ref[1] + first, meta_ref[2]


def turned(column):
    return jnp.broadcast_to(column, (column.shape[0], 128)).T[0:1, :]


def fwd_kernel(count, chunks, leads, meta_ref, rand_ref, starts_ref, q_ref, qd_ref, *rest):
    pieces, rest = rest[:count], rest[count:]
    if leads:
        o_ref, dense_ref, log_ref, kv, sems = rest
    else:
        dense_ref, o_ref, kv, sems = rest
    seq = kv.shape[0]
    step = pl.program_id(0) - (1 if leads else 0)
    steps = pl.num_programs(0) - (1 if leads else 0)
    first, block0, length = step_block(meta_ref, jnp.maximum(step, 0), steps)
    kmask = head_masks((0, 1, 2))
    vmask = head_masks((2, 3, 1))

    @pl.when(pl.program_id(0) == 0)
    def _():
        load_pieces(seq // chunks, starts_ref, pieces, kv, sems)

    def sparse(u):
        i = block0 + u
        near, rand = tile_starts(i, first + u, rand_ref, seq)
        tiles = gather_tiles(kv, near, rand)
        live = tile_live(i, near, rand, length)
        lane = lax.broadcasted_iota(jnp.int32, (1, BLK), 1)
        bias = jnp.concatenate([jnp.where(lane < n, 0.0, MASKED) for n in live], axis=1)
        qs = spread(q_ref[u * BLK : (u + 1) * BLK, :], kmask)
        s = nt(qs, tiles[:, 0:256]) + bias
        top = jnp.max(s, axis=1, keepdims=True)
        p = jnp.exp(s - top)
        total = jnp.sum(p, axis=1, keepdims=True)
        mixed = nn(p.astype(bf16), tiles[:, 128:384]) / total
        o_ref[u * BLK : (u + 1) * BLK, :] = fold(mixed, vmask).astype(bf16)

    def dense():
        qs = jnp.concatenate(
            [spread(qd_ref[u * BLK : (u + 1) * BLK, :], kmask) for u in range(PAIR)], axis=0
        )
        rows = qs.shape[0]
        lane = lax.broadcasted_iota(jnp.int32, (1, CHUNK), 1)

        def body(c, carry):
            top, total, mixed = carry
            start = pl.multiple_of(c * CHUNK, CHUNK)
            keys = kv[pl.ds(start, CHUNK), :]
            s = nt(qs, keys[:, 0:256]) + jnp.where(lane + start < length, 0.0, MASKED)
            new = jnp.maximum(top, jnp.max(s, axis=1, keepdims=True))
            scale = jnp.exp(top - new)
            p = jnp.exp(s - new)
            total = total * scale + jnp.sum(p, axis=1, keepdims=True)
            mixed = mixed * scale + nn(p.astype(bf16), keys[:, 128:384])
            return new, total, mixed

        init = (
            jnp.full((rows, 1), MASKED, f32),
            jnp.zeros((rows, 1), f32),
            jnp.zeros((rows, 256), f32),
        )
        top, total, mixed = lax.fori_loop(0, seq // CHUNK, body, init)
        mixed = mixed / total
        log_ref[...] = jnp.broadcast_to(turned(top + jnp.log(total)), log_ref.shape)
        half = rows // PAIR
        for u in range(PAIR):
            dense_ref[u * BLK : (u + 1) * BLK, :] = fold(
                mixed[u * half : (u + 1) * half], vmask
            ).astype(bf16)

    if leads:

        @pl.when((step < 0) & (meta_ref[1] == 0))
        def _():
            dense()

    @pl.when((step >= 0) & (block0 >= 2))
    def _():
        for u in range(PAIR):
            sparse(u)

    @pl.when((step >= 0) & (block0 < 2))
    def _():
        o_ref[...] = dense_ref[...]


def q_specs(steps, shift):
    def block(g, m, r, s):
        step = jnp.clip(g - shift, 0, steps - 1)
        return (m[0] // PAIR + lax.rem(step + m[3] // PAIR, steps), 0)

    fixed = pl.BlockSpec((PAIR * BLK, 256), lambda g, m, r, s: (0, 0))
    return [pl.BlockSpec((PAIR * BLK, 256), block), fixed]


def attend(meta, rand, starts, q, pieces, seq, rows, chunks, dense=None):
    steps = rows // (PAIR * BLK)
    count = len(pieces)
    leads = dense is None
    fixed = pl.BlockSpec((PAIR * BLK, 256), lambda g, m, r, s: (0, 0))
    out_specs = [
        pl.BlockSpec((PAIR * BLK, 256), lambda g, m, r, s: (jnp.maximum(g - (1 if leads else 0), 0), 0))
    ]
    out_shape = [jax.ShapeDtypeStruct((rows, 256), bf16)]
    if leads:
        out_specs += [fixed, pl.BlockSpec((8, 3 * PAIR * BLK), lambda g, m, r, s: (0, 0))]
        out_shape += [
            jax.ShapeDtypeStruct((PAIR * BLK, 256), bf16),
            jax.ShapeDtypeStruct((8, 3 * PAIR * BLK), f32),
        ]
    return call(
        functools.partial(fwd_kernel, count, chunks, leads),
        grid_spec=pltpu.PrefetchScalarGridSpec(
            num_scalar_prefetch=3,
            grid=(steps + (1 if leads else 0),),
            in_specs=q_specs(steps, 1 if leads else 0) + [ANY] * count + ([] if leads else [fixed]),
            out_specs=out_specs,
            scratch_shapes=[pltpu.VMEM((seq, 384), bf16), pltpu.SemaphoreType.DMA((chunks,))],
        ),
        out_shape=out_shape,
        compiler_params=pltpu.CompilerParams(vmem_limit_bytes=seq * 768 + 8 * MIB),
        cost_estimate=LIGHT,
        name="attend",
    )(meta, rand, starts, q, q, *pieces, *([] if leads else [dense]))


def bwd_kernel(count, last, chunks, n_send, meta_ref, rand_ref, starts_ref, q_ref, qd_ref, do_ref, *rest):
    pieces, rest = rest[:count], rest[count:]
    if last:
        in_ref, before_ref, x_ref, own_ref, came_ref, od_ref, log_ref, dq_ref, all_ref, dw_ref = rest[:10]
        sends, (kv, acc, sems, dqs, xs) = rest[10 : 10 + n_send], rest[-5:]
    else:
        dq_ref, out_ref, kv, acc, sems = rest
    seq = kv.shape[0]
    step = pl.program_id(0)
    steps = pl.num_programs(0) - (1 if last else 0)
    first, block0, length = step_block(meta_ref, jnp.minimum(step, steps - 1), steps)
    kmask = head_masks((0, 1, 2))
    vmask = head_masks((2, 3, 1))

    def inputs():
        return pltpu.make_async_copy(x_ref, xs, sems.at[chunks + 2])

    def keep(u, value, place):
        value = value.astype(bf16)
        dq_ref[u * BLK : (u + 1) * BLK, :] = value
        if last:
            dqs[pl.ds(pl.multiple_of(place + u * BLK, 64), BLK), :] = value

    @pl.when(step == 0)
    def _():
        if last:
            half = dqs.shape[0] // 2
            carry = pltpu.make_async_copy(in_ref, acc, sems.at[chunks])
            carry.start()
            first_half = pltpu.make_async_copy(
                before_ref.at[pl.ds(0, half)], dqs.at[pl.ds(0, half)], sems.at[chunks + 1]
            )
            first_half.start()
            inputs().start()
        else:
            acc[...] = jnp.zeros_like(acc)
        load_pieces(seq // chunks, starts_ref, pieces, kv, sems)
        if last:
            carry.wait()
            first_half.wait()

    def add_rows(start, n, wk, wv):
        rows = pl.ds(start, n)
        acc[rows, 0:128] += wk[:, 0:128]
        acc[rows, 128:256] += wk[:, 128:256] + wv[:, 0:128]
        acc[rows, 256:384] += wv[:, 128:256]

    def sparse(u):
        i = block0 + u
        near, rand = tile_starts(i, first + u, rand_ref, seq)
        tiles = gather_tiles(kv, near, rand)
        live = tile_live(i, near, rand, length)
        row = lax.broadcasted_iota(jnp.int32, (BLK, 192), 0)
        qs = spread(q_ref[u * BLK : (u + 1) * BLK, :], kmask)
        gs = spread(do_ref[u * BLK : (u + 1) * BLK, :], vmask)
        s = nt(tiles[:, 0:256], qs)
        s = jnp.concatenate(
            [jnp.where(row < live[j], s[j * BLK : (j + 1) * BLK], MASKED) for j in range(8)],
            axis=0,
        )
        top = jnp.max(s, axis=0, keepdims=True)
        p = jnp.exp(s - top)
        p = p * (1.0 / jnp.sum(p, axis=0, keepdims=True))
        dp = nt(tiles[:, 128:384], gs)
        inner = jnp.sum(p * dp, axis=0, keepdims=True)
        ds = (p * (dp - inner)).astype(bf16)
        wk = nn(ds, qs)
        wv = nn(p.astype(bf16), gs)
        add_rows(near, 192, wk[0:192], wv[0:192])
        for r in range(3):
            a = 192 + r * BLK
            add_rows(rand[r], BLK, wk[a : a + BLK], wv[a : a + BLK])
        add_rows(0, 128, wk[384:512], wv[384:512])
        dq = fold(tn(ds, tiles[:, 0:256]), kmask) * 0.125
        keep(u, dq, (step + steps) * PAIR * BLK)

    def dense():
        rows_g = jnp.where(meta_ref[6] == 0, own_ref[...].astype(f32), came_ref[...].astype(f32))
        qs, gs, inner = [], [], []
        for u in range(PAIR):
            rows = slice(u * BLK, (u + 1) * BLK)
            qs.append(spread(qd_ref[rows, :], kmask))
            gs.append(spread(rows_g[rows, :].astype(bf16), vmask))
            for m in vmask:
                part = rows_g[rows, :] * od_ref[rows, :].astype(f32) * m.astype(f32)
                inner.append(jnp.sum(part, axis=1, keepdims=True))
        qs, gs = jnp.concatenate(qs, axis=0), jnp.concatenate(gs, axis=0)
        inner = turned(jnp.concatenate(inner, axis=0))
        log_sum = log_ref[0:1, :]
        cols = qs.shape[0]
        row = lax.broadcasted_iota(jnp.int32, (CHUNK, cols), 0)

        def back(c, dq):
            start = pl.multiple_of(c * CHUNK, CHUNK)
            keys = kv[pl.ds(start, CHUNK), :]
            s = jnp.where(row < length - start, nt(keys[:, 0:256], qs), MASKED)
            p = jnp.exp(s - log_sum)
            ds = (p * (nt(keys[:, 128:384], gs) - inner)).astype(bf16)
            add_rows(start, CHUNK, nn(ds, qs), nn(p.astype(bf16), gs))
            return dq + tn(ds, keys[:, 0:256])

        dq = lax.fori_loop(0, seq // CHUNK, back, jnp.zeros((cols, 256), f32))
        half = cols // PAIR
        for u in range(PAIR):
            keep(u, fold(dq[u * half : (u + 1) * half], kmask) * 0.125, meta_ref[4] * PAIR * BLK)

    @pl.when((step < steps) & (block0 >= 2))
    def _():
        for u in range(PAIR):
            sparse(u)

    if last:

        @pl.when((step == steps) & (meta_ref[1] == 0))
        def _():
            dense()

    @pl.when(pl.program_id(0) == pl.num_programs(0) - 1)
    def _():
        if not last:
            pltpu.sync_copy(acc, out_ref)
        else:
            size = seq // chunks

            def emit(k):
                start = pl.multiple_of(starts_ref[chunks + k], 64)
                return acc[pl.ds(start, size), :].astype(bf16)

            for k in range(chunks):
                piece = emit(k)
                all_ref[k * size : (k + 1) * size, :] = piece
                if n_send and k >= chunks - 4:
                    j = k - chunks + 4
                    dst, at = sends[j // 2], j % 2
                    dst[at * size : (at + 1) * size, :] = piece
            inputs().wait()
            if n_send:
                part = 2 * size
                total = None
                for k in range(0, seq, part):
                    value = tn(all_ref[k : k + part, :], xs[k : k + part, :])
                    total = value if total is None else total + value
                dw_ref[256:640, :] = total
                dw_ref[0:256, :] = tn(dqs[...], xs[0 : dqs.shape[0], :])
                sums = [
                    jnp.sum(all_ref[:, 128:384].astype(f32), axis=0, keepdims=True),
                    jnp.sum(dqs[...].astype(f32), axis=0, keepdims=True),
                ]
                sums = jnp.concatenate(sums + [jnp.zeros((6, 256), f32)], axis=0)
                dw_ref[640:648, 0:256] = sums


def attend_back(meta, rand, starts, q, grad, pieces, seq, chunks, n_send, tokens, carried=None, dense=None, x=None):
    rows = tokens // 2
    steps = rows // (PAIR * BLK)
    count = len(pieces)
    last = carried is not None
    shape = (PAIR * BLK, 256)
    more = []
    if last:

        def dq_block(g, m, r, s):
            return (jnp.where((g == steps) & (m[1] == 0), m[4], jnp.minimum(g, steps - 1) + steps), 0)

        chosen = pl.BlockSpec(shape, lambda g, m, r, s: (m[5], 0))
        more = [
            chosen,
            chosen,
            pl.BlockSpec(shape, lambda g, m, r, s: (0, 0)),
            pl.BlockSpec((8, 3 * PAIR * BLK), lambda g, m, r, s: (0, 0)),
        ]
    else:
        dq_block = lambda g, m, r, s: (g, 0)
    out_specs = [pl.BlockSpec(shape, dq_block)]
    out_shape = [jax.ShapeDtypeStruct((tokens, 256), bf16)]
    if last:
        sizes = [seq] + [2 * seq // chunks] * n_send
        more = [ANY] + more
        outs = [(n, 384, bf16) for n in sizes]
        outs.insert(1, (648, x.shape[1], f32))
        out_specs += [
            pl.BlockSpec((n, w), lambda g, m, r, s: (0, 0), pipeline_mode=pl.Buffered(1)) for n, w, _ in outs
        ]
        out_shape += [jax.ShapeDtypeStruct((n, w), t) for n, w, t in outs]
    else:
        out_specs += [ANY]
        out_shape += [jax.ShapeDtypeStruct((seq, 384), f32)]
    grad_spec = pl.BlockSpec(shape, lambda g, m, r, s: (jnp.minimum(g, steps - 1), 0))
    return call(
        functools.partial(bwd_kernel, count, last, chunks, n_send),
        grid_spec=pltpu.PrefetchScalarGridSpec(
            num_scalar_prefetch=3,
            grid=(steps + (1 if last else 0),),
            in_specs=q_specs(steps, 0) + [grad_spec] + [ANY] * (count + (2 if last else 0)) + more,
            out_specs=out_specs,
            scratch_shapes=[
                pltpu.VMEM((seq, 384), bf16),
                pltpu.VMEM((seq, 384), f32),
                pltpu.SemaphoreType.DMA((chunks + 3,)),
            ]
            + ([pltpu.VMEM((tokens, 256), bf16), pltpu.VMEM(x.shape, bf16)] if last else []),
        ),
        out_shape=out_shape,
        input_output_aliases={3 + 3 + count + 1: 0} if last else {},
        compiler_params=pltpu.CompilerParams(
            vmem_limit_bytes=seq * 2304 + 10 * MIB + (seq * 1536 + x.size * 2 + 6 * MIB if last else 0)
        ),
        cost_estimate=LIGHT,
        name="attend_back",
    )(meta, rand, starts, q, q, grad, *pieces, *(carried or ()), *(() if x is None else (x,)), *(dense or ()))


def split_kernel(count, short, long, a_ref, wq_ref, wkv_ref, ship_ref, vec_ref):
    step = a_ref.shape[0] // count
    rows = step - 16
    parts = []
    for k in range(count):
        there, here = slice(k * step, k * step + rows), slice(k * rows, (k + 1) * rows)
        zero = jnp.zeros((rows, 64), bf16)
        wq_ref[here, 0:192] = a_ref[there, 0:192]
        wq_ref[here, 192:256] = zero
        wkv_ref[here, :] = a_ref[there, 192:576]
        ship_ref[here, 0:64] = zero
        ship_ref[here, 64:256] = a_ref[there, 576:768]
        parts.append(a_ref[k * step + rows : (k + 1) * step, :].astype(f32))
    width = vec_ref.shape[1]
    attn = jnp.concatenate([p[:, 0:short] for p in parts], axis=1)
    attn = jnp.concatenate([attn, jnp.zeros((16, width - attn.shape[1]), f32)], axis=1)
    dense = jnp.concatenate([p[:, 0:long] for p in parts], axis=1)
    vec = jnp.concatenate([attn[0:2], dense[2:16]], axis=0)
    vec_ref[...] = vec
    ship = jnp.concatenate([vec[2:3, k * 256 : (k + 1) * 256] for k in range(3)], axis=0)
    ship = jnp.concatenate([ship, jnp.zeros((13, 256), f32)], axis=0)
    ship_ref[count * rows : count * rows + 16, :] = ship.astype(bf16)


def split_call(count, short, long, gathered):
    rows = gathered.shape[0] - 16 * count
    outs = [
        jax.ShapeDtypeStruct((rows, 256), bf16),
        jax.ShapeDtypeStruct((rows, 384), bf16),
        jax.ShapeDtypeStruct((rows + 16, 256), bf16),
        jax.ShapeDtypeStruct((16, count * long), f32),
    ]
    return call(
        functools.partial(split_kernel, count, short, long),
        outs="-",
        grid=(1,),
        in_specs=[whole_block(gathered)],
        out_specs=[whole_block(v) for v in outs],
        out_shape=outs,
        compiler_params=pltpu.CompilerParams(vmem_limit_bytes=10 * MIB),
        cost_estimate=LIGHT,
        name="split",
    )(gathered)


TILE = 256


def proj_kernel(keep_ref, got_ref, wm_ref, wt_ref, peer_ref, own_ref):
    half, width = peer_ref.shape
    for k, out in enumerate((peer_ref, own_ref)):
        rows = slice(k * half, (k + 1) * half)
        value = nt(keep_ref[rows, :], wm_ref[0:width, :]) + nt(got_ref[rows, :], wt_ref[0:width, :])
        out[...] = value.astype(out.dtype)


def in_vmem(kernel, out_shape, limit, name, aliases=None, outs="v", ins="v"):
    def pick(text, values):
        return [VM if text[min(k, len(text) - 1)] == "v" else whole_block(v) for k, v in enumerate(values)]

    return lambda *args: call(
        kernel,
        ins=ins,
        outs=outs,
        grid=(1,),
        in_specs=pick(ins, args),
        out_specs=pick(outs, out_shape),
        out_shape=out_shape,
        input_output_aliases=aliases or {},
        compiler_params=pltpu.CompilerParams(vmem_limit_bytes=limit * MIB),
        cost_estimate=LIGHT,
        name=name,
    )(*args)


def project(keep, got, wm, wt):
    rows, width = keep.shape[0] // 2, wm.shape[0] - 16
    outs = [jax.ShapeDtypeStruct((rows, width), bf16)] * 2
    return in_vmem(proj_kernel, outs, 10, "project", outs="h", ins="-")(keep, got, wm, wt)


def stats(value):
    center = jnp.mean(value, axis=-1, keepdims=True)
    offset = value - center
    inverse = lax.rsqrt(jnp.mean(offset * offset, axis=-1, keepdims=True) + EPSILON)
    return offset * inverse, inverse


def fetch_two(slot_ref, src, dst, came, got, sems):
    start = pl.multiple_of(slot_ref[0] * dst.shape[0], 64)
    load_all([(src.at[pl.ds(start, dst.shape[0])], dst), (came, got)], sems)


def norm_one_kernel(
    slot_ref, x_ref, came_ref, part_ref, vec_ref, resid_ref, hidden_ref, low_ref, rows_ref, got_ref, sems
):
    fetch_two(slot_ref, x_ref, rows_ref, came_ref, got_ref, sems)
    for k in range(0, part_ref.shape[0], TILE):
        rows = slice(k, k + TILE)
        resid = rows_ref[rows, :].astype(f32) + (
            part_ref[rows, :].astype(f32) + got_ref[rows, :].astype(f32) + vec_ref[3:4, :]
        )
        resid_ref[rows, :] = resid
        normed, _ = stats(resid)
        hidden = normed * vec_ref[4:5, :] + vec_ref[5:6, :]
        hidden_ref[rows, :] = hidden
        low_ref[rows, :] = hidden.astype(bf16)


def norm_one(slot, x, part, got, vec):
    rows, width = part.shape
    return call(
        norm_one_kernel,
        ins="h-",
        outs="h",
        grid_spec=pltpu.PrefetchScalarGridSpec(
            num_scalar_prefetch=1,
            grid=(1,),
            in_specs=[HBM, ANY] + [whole_block(v) for v in (part, vec)],
            out_specs=[pl.BlockSpec((rows, width), lambda g, s: (0, 0))] * 3,
            scratch_shapes=[pltpu.VMEM((rows, width), bf16)] * 2 + [pltpu.SemaphoreType.DMA((2,))],
        ),
        out_shape=[jax.ShapeDtypeStruct((rows, width), t) for t in (f32, f32, bf16)],
        compiler_params=pltpu.CompilerParams(vmem_limit_bytes=14 * MIB),
        cost_estimate=LIGHT,
        name="norm_one",
    )(slot, x, got, part, vec)


def add_sums(total, low, error, normed):
    sums = [jnp.sum(v, axis=0, keepdims=True) for v in (low.astype(f32), error * normed, error)]
    return sums if total is None else [x + z for x, z in zip(total, sums)]


def ride(low_ref, sums_ref, total):
    sums = jnp.concatenate(total + [jnp.zeros((5, low_ref.shape[1]), f32)], axis=0)
    sums_ref[...] = sums
    rows = low_ref.shape[0] - 16
    low_ref[rows : rows + 16, :] = jnp.concatenate([sums, jnp.zeros_like(sums)], axis=0).astype(bf16)


def norm_two_kernel(
    slot_ref, cot_ref, came_ref, hidden_ref, part_ref, vec_ref,
    out_ref, low_ref, grad_ref, sums_ref, rows_ref, got_ref, sems,
):
    fetch_two(slot_ref, cot_ref, rows_ref, came_ref, got_ref, sems)
    gain = vec_ref[7:8, :]
    total = None
    for k in range(0, part_ref.shape[0], TILE):
        rows = slice(k, k + TILE)
        value = hidden_ref[rows, :] + (part_ref[rows, :].astype(f32) + got_ref[rows, :].astype(f32)) + vec_ref[6:7, :]
        normed, inverse = stats(value)
        position = slot_ref[1] + k + lax.broadcasted_iota(jnp.int32, (TILE, 1), 0)
        live = (position < slot_ref[2]).astype(f32)
        out_ref[rows, :] = ((normed * gain + vec_ref[8:9, :]) * live).astype(bf16)
        error = rows_ref[rows, :].astype(f32) * live
        inner = error * gain
        first = jnp.mean(inner, axis=-1, keepdims=True)
        second = jnp.mean(inner * normed, axis=-1, keepdims=True)
        grad = inverse * (inner - first - normed * second)
        grad_ref[rows, :] = grad
        low = grad.astype(bf16)
        low_ref[rows, :] = low
        total = add_sums(total, low, error, normed)
    ride(low_ref, sums_ref, total)


def norm_two(slot, cotangent, hidden, part, got, vec):
    rows, width = part.shape
    return call(
        norm_two_kernel,
        ins="h-",
        outs="h",
        grid_spec=pltpu.PrefetchScalarGridSpec(
            num_scalar_prefetch=1,
            grid=(1,),
            in_specs=[HBM, ANY] + [whole_block(v) for v in (hidden, part, vec)],
            out_specs=[
                pl.BlockSpec((n, width), lambda g, s: (0, 0)) for n in (rows, rows + 16, rows, 8)
            ],
            scratch_shapes=[pltpu.VMEM((rows, width), bf16)] * 2 + [pltpu.SemaphoreType.DMA((2,))],
        ),
        out_shape=[
            jax.ShapeDtypeStruct((rows, width), bf16),
            jax.ShapeDtypeStruct((rows + 16, width), bf16),
            jax.ShapeDtypeStruct((rows, width), f32),
            jax.ShapeDtypeStruct((8, width), f32),
        ],
        compiler_params=pltpu.CompilerParams(vmem_limit_bytes=14 * MIB),
        cost_estimate=LIGHT,
        name="norm_two",
    )(slot, cotangent, got, hidden, part, vec)


def norm_one_back_kernel(resid_ref, two_ref, part_ref, got_ref, vec_ref, grad_ref, low_ref, sums_ref):
    total = None
    for k in range(0, part_ref.shape[0], TILE):
        rows = slice(k, k + TILE)
        normed, inverse = stats(resid_ref[rows, :])
        error = two_ref[rows, :] + (part_ref[rows, :].astype(f32) + got_ref[rows, :].astype(f32))
        inner = error * vec_ref[4:5, :]
        first = jnp.mean(inner, axis=-1, keepdims=True)
        second = jnp.mean(inner * normed, axis=-1, keepdims=True)
        grad = inverse * (inner - first - normed * second)
        grad_ref[rows, :] = grad
        low = grad.astype(bf16)
        low_ref[rows, :] = low
        total = add_sums(total, low, error, normed)
    ride(low_ref, sums_ref, total)


def norm_one_back(resid, two, part, got, vec):
    rows, width = part.shape
    outs = [
        jax.ShapeDtypeStruct((rows, width), f32),
        jax.ShapeDtypeStruct((rows + 16, width), bf16),
        jax.ShapeDtypeStruct((8, width), f32),
    ]
    return in_vmem(norm_one_back_kernel, outs, 14, "norm_one_back", outs="h", ins="-")(resid, two, part, got, vec)


ERFC = (
    -1.26551223, 1.00002368, 0.37409196, 0.09678418, -0.18628806,
    0.27886807, -1.13520398, 1.48851587, -0.82215223, 0.17087277,
)


def gelu_pair(pre):
    z = jnp.abs(pre) * math.sqrt(0.5)
    t = 1.0 / (1.0 + 0.5 * z)
    poly = jnp.full_like(t, ERFC[-1])
    for coefficient in ERFC[-2::-1]:
        poly = poly * t + coefficient
    square = -z * z
    tail = 0.5 * t * jnp.exp(square + poly)
    cdf = jnp.where(pre < 0, tail, 1.0 - tail)
    density = jnp.exp(square) * (1.0 / math.sqrt(2.0 * math.pi))
    return (pre * cdf).astype(bf16), (cdf + pre * density).astype(bf16)


def up_kernel(base, hid_ref, wim_ref, wit_ref, vec_ref, ship_ref, *rest):
    act_ref, slope_ref, all_ref = rest[-3:]
    units, at = wim_ref.shape[1], ship_ref.shape[0] - 16
    shipped = ship_ref[at : at + 16, :].astype(f32)
    shipped = jnp.concatenate([shipped[k : k + 1, :] for k in range(3)], axis=1)
    for k in range(0, hid_ref.shape[0], TILE):
        rows, there = slice(k, k + TILE), slice(base + k, base + k + TILE)
        hid = hid_ref[rows, :]
        all_ref[there, :] = hid
        for j, (wi, b) in enumerate(((wim_ref, vec_ref[2:3, :]), (wit_ref, shipped))):
            act, slope = gelu_pair(nn(hid, wi[...]) + b)
            act_ref[there, j * units : (j + 1) * units] = act
            slope_ref[there, j * units : (j + 1) * units] = slope


def mlp_up(hid, wi_m, wi_t, vec, ship, earlier):
    rows, width = hid.shape
    units = wi_m.shape[1]
    big = jax.ShapeDtypeStruct((2 * rows, 2 * units), bf16)
    outs = [big, big, jax.ShapeDtypeStruct((2 * rows, width), bf16)]
    second = earlier is not None
    kernel = functools.partial(up_kernel, rows if second else 0)
    aliases = {5 + k: k for k in range(3)} if second else {}
    args = (hid, wi_m, wi_t, vec, ship) + (tuple(earlier) if second else ())
    return in_vmem(kernel, outs, 16, "mlp_up", aliases, ins="-----v")(*args)


def down_kernel(base, act_ref, wo_ref, part_ref):
    for k in range(0, part_ref.shape[0], TILE):
        there = slice(base + k, base + k + TILE)
        part_ref[k : k + TILE, :] = nt(act_ref[there, :], wo_ref[...]).astype(bf16)


def mlp_down(act, wo, second):
    rows = act.shape[0] // 2
    kernel = functools.partial(down_kernel, rows if second else 0)
    outs = [jax.ShapeDtypeStruct((rows, wo.shape[0]), bf16)]
    return in_vmem(kernel, outs, 10, "mlp_down", outs="h", ins="v-")(act, wo)[0]


def mlp_back_kernel(base, gm_ref, slope_ref, wim_ref, wit_ref, wo_ref, *rest):
    gp_ref, all_ref, part_ref, sums_ref = rest[-4:]
    units = wim_ref.shape[1]
    sums = [None, None]
    for k in range(0, part_ref.shape[0], TILE):
        rows, there = slice(k, k + TILE), slice(base + k, base + k + TILE)
        gm = gm_ref[rows, :]
        all_ref[there, :] = gm
        total = None
        for j, wi in enumerate((wim_ref, wit_ref)):
            cols = slice(j * units, (j + 1) * units)
            gp = (nn(gm, wo_ref[:, cols]) * slope_ref[there, cols].astype(f32)).astype(bf16)
            gp_ref[there, cols] = gp
            column = jnp.sum(gp.astype(f32), axis=0, keepdims=True)
            sums[j] = column if sums[j] is None else sums[j] + column
            value = nt(gp, wi[...])
            total = value if total is None else total + value
        part_ref[rows, :] = total.astype(bf16)
    sums_ref[...] = jnp.concatenate(sums + [jnp.zeros((6, units), f32)], axis=0)


def mlp_back(gm, slope, wi_m, wi_t, wo, earlier):
    rows, width = gm.shape[0] - 16, gm.shape[1]
    units = wi_m.shape[1]
    outs = [
        jax.ShapeDtypeStruct((2 * rows, 2 * units), bf16),
        jax.ShapeDtypeStruct((2 * rows, width), bf16),
        jax.ShapeDtypeStruct((rows, width), bf16),
        jax.ShapeDtypeStruct((8, units), f32),
    ]
    second = earlier is not None
    kernel = functools.partial(mlp_back_kernel, rows if second else 0)
    aliases = {5 + k: k for k in range(2)} if second else {}
    args = (gm, slope, wi_m, wi_t, wo) + (tuple(earlier) if second else ())
    return in_vmem(kernel, outs, 20, "mlp_back", aliases, outs="vvhh", ins="-v---v")(*args)


def heads_kernel(
    peer_ref, own_ref, wm_ref, wt_ref, two_ref, twop_ref, one_ref, dbi_a_ref, dbi_b_ref,
    send_ref, keep_ref, both_ref, vec_ref,
):
    half = peer_ref.shape[0] - 16
    for k, ref in enumerate((peer_ref, own_ref)):
        rows = slice(k * half, (k + 1) * half)
        grad = ref[0:half, :]
        both_ref[rows, :] = grad
        send_ref[rows, :] = nn(grad, wt_ref[0 : grad.shape[1], :]).astype(bf16)
        keep_ref[rows, :] = nn(grad, wm_ref[0 : grad.shape[1], :]).astype(bf16)
    two = two_ref[...] + twop_ref[half : half + 16, :].astype(f32)[0:8]
    one = one_ref[...] + peer_ref[half : half + 16, :].astype(f32)[0:8]
    dbi = dbi_a_ref[...] + dbi_b_ref[...]
    vec = jnp.concatenate([two[0:3], one[0:3], dbi[1:2], dbi[0:1]], axis=0)
    vec_ref[...] = vec
    width = vec.shape[1] // 3
    packed = jnp.concatenate([vec[:, k * width : (k + 1) * width] for k in range(3)], axis=0)
    packed = jnp.concatenate([packed, jnp.zeros((8, width), f32)], axis=0)
    send_ref[2 * half : 2 * half + 32, :] = packed.astype(bf16)


def heads_back(peer, own, wm, wt, two, gm_peer, one, dbi_a, dbi_b):
    rows, width = peer.shape[0] - 16, peer.shape[1]
    shapes = [(2 * rows + 32, 256), (2 * rows, 256), (2 * rows, width)]
    outs = [jax.ShapeDtypeStruct(v, bf16) for v in shapes] + [jax.ShapeDtypeStruct((8, width), f32)]
    return in_vmem(heads_kernel, outs, 12, "heads_back", outs="h", ins="-")(
        peer, own, wm, wt, two, gm_peer, one, dbi_a, dbi_b
    )


def input_kernel(count, dq_ref, mine_ref, *rest):
    got_ref = rest[0] if count else None
    wq_ref, wkv_ref = rest[count : count + 2]
    adds, out_ref = rest[count + 2 : -1], rest[-1]
    both = mine_ref[...]
    if count:
        both = (both.astype(f32) + got_ref[...].astype(f32)).astype(bf16)
    total = nt(dq_ref[...], wq_ref[...]) + nt(both, wkv_ref[...])
    for add in adds:
        total = total + add[...].astype(f32)
    out_ref[...] = total.astype(bf16)


def input_back(k, dq, mine, got, got_block, wq, wkv, adds):
    got = [] if got is None else [got]
    rows, width = dq.shape[0] // 4, wq.shape[0]
    out = jax.ShapeDtypeStruct((rows, width), bf16)
    return call(
        functools.partial(input_kernel, len(got)),
        ins="-",
        grid=(1,),
        in_specs=[
            pl.BlockSpec((rows, 256), lambda g: (k, 0)),
            pl.BlockSpec((rows, 384), lambda g: (k, 0)),
        ]
        + [pl.BlockSpec((rows, 384), lambda g: (got_block, 0)) for _ in got]
        + [whole_block(v) for v in [wq, wkv] + adds],
        out_specs=whole_block(out),
        out_shape=out,
        compiler_params=pltpu.CompilerParams(vmem_limit_bytes=8 * MIB),
        cost_estimate=LIGHT,
        name="input_back",
    )(dq, mine, *got, wq, wkv, *adds)


def table_kernel(dw_ref, dwp_ref, got_ref, vec_ref, peer_ref, table):
    count = (table.shape[0] - got_ref.shape[0]) // 16
    shard = got_ref.shape[0] // count
    dwq_t, dwkv_t = dw_ref[0:192, :], dw_ref[256:640, :]
    dbv, dbq = dw_ref[640:641, 0:256], dw_ref[641:642, 0:192]
    dbv = jnp.concatenate([dbv[:, 128:256], dbv[:, 64:128]], axis=1)
    came = peer_ref[...].astype(f32)
    came = jnp.concatenate([came[8 * k : 8 * k + 8, :] for k in range(3)], axis=1)
    vectors = [vec_ref[k : k + 1, :] + came[k : k + 1, :] for k in (0, 1, 2, 4, 5, 3)]
    vectors += [vec_ref[7:8, :] + came[6:7, :], dbq, dbv]
    dwq, dwkv = dwq_t.T, dwkv_t.T
    for j in range(count):
        rows = slice(j * shard, (j + 1) * shard)
        base = j * (shard + 16)
        main = slice(base, base + shard)
        table[main, 0:192] = dwq[rows, :].astype(bf16)
        table[main, 192:576] = dwkv[rows, :].astype(bf16)
        table[main, 576:768] = (
            dwp_ref[rows, 64:256].astype(f32) + got_ref[rows, 64:256].astype(f32)
        ).astype(bf16)
        parts = []
        for vector in vectors:
            n = vector.shape[1] // count
            parts.append(
                jnp.concatenate([vector[:, j * n : (j + 1) * n], jnp.zeros((1, 768 - n), f32)], axis=1)
            )
        parts.append(jnp.zeros((16 - len(parts), 768), f32))
        table[base + shard : base + shard + 16, :] = jnp.concatenate(parts, axis=0).astype(bf16)


def table_call(count, dw, dwp, got, vec, peer):
    out = jax.ShapeDtypeStruct((got.shape[0] + 16 * count, 768), bf16)
    args = [dw, dwp, got, vec, peer]
    specs = [whole_block(v) for v in args]
    specs[4] = pl.BlockSpec((32, 256), lambda g: (peer.shape[0] // 32 - 1, 0))
    return call(
        table_kernel,
        ins="h",
        outs="h",
        grid=(1,),
        in_specs=specs,
        out_specs=whole_block(out),
        out_shape=out,
        compiler_params=pltpu.CompilerParams(vmem_limit_bytes=14 * MIB),
        cost_estimate=LIGHT,
        name="table",
    )(*args)


def products_kernel(own, x_ref, xq_ref, dq_ref, dkv_ref, dw_ref):
    step = pl.program_id(0)

    @pl.when(step == 0)
    def _():
        dw_ref[...] = jnp.zeros_like(dw_ref)

    dw_ref[256:640, :] += tn(dkv_ref[...], x_ref[...])
    dw_ref[640:641, 0:256] += jnp.sum(dkv_ref[:, 128:384].astype(f32), axis=0, keepdims=True)

    @pl.when(step < own)
    def _():
        dw_ref[0:256, :] += tn(dq_ref[...], xq_ref[...])
        dw_ref[641:642, 0:256] += jnp.sum(dq_ref[...].astype(f32), axis=0, keepdims=True)


def products_call(x, xq, dq, dkv):
    rows, own, width = dq.shape[0] // 2, 2, x.shape[1]
    out = jax.ShapeDtypeStruct((648, width), f32)
    return call(
        functools.partial(products_kernel, own),
        ins="h",
        outs="h",
        grid=(x.shape[0] // rows,),
        in_specs=[
            pl.BlockSpec((rows, width), lambda g: (g, 0)),
            pl.BlockSpec((rows, width), lambda g: (jnp.minimum(g, own - 1), 0)),
            pl.BlockSpec((rows, 256), lambda g: (jnp.minimum(g, own - 1), 0)),
            pl.BlockSpec((rows, 384), lambda g: (g, 0)),
        ],
        out_specs=whole_block(out),
        out_shape=out,
        compiler_params=pltpu.CompilerParams(vmem_limit_bytes=24 * MIB),
        cost_estimate=LIGHT,
        name="products",
    )(x, xq, dq, dkv)


def last_kernel(mine_ref, came_ref, dwq_ref, dwk_ref, dwv_ref, dwp_ref, small_ref):
    both = mine_ref[...].astype(f32) + came_ref[...].astype(f32)
    shard = dwq_ref.shape[0]
    main = both[0:shard]
    dwq_ref[...] = main[:, 0:192]
    dwk_ref[...] = main[:, 192:384]
    dwv_ref[:, 0:128] = main[:, 448:576]
    dwv_ref[:, 128:192] = main[:, 384:448]
    down = main[:, 576:768].T
    dwp_ref[0:128, :] = down[64:192, :]
    dwp_ref[128:192, :] = down[0:64, :]
    small_ref[...] = both[shard : shard + 16, :]


def last_call(mine, came):
    shard = mine.shape[0] - 16
    shapes = [(shard, 192)] * 3 + [(192, shard), (16, 768)]
    outs = [jax.ShapeDtypeStruct(v, f32) for v in shapes]
    return in_vmem(last_kernel, outs, 8, "last", outs="h", ins="-")(mine, came)


def core_swap(value):
    return lax.ppermute(value, TP, [(0, 1), (1, 0), (2, 3), (3, 2)])


def y_swap(value):
    return lax.ppermute(value, TP, [(0, 2), (2, 0), (1, 3), (3, 1)])


def x_swap(value):
    return lax.ppermute(value, CTX, [(0, 1), (1, 0)])


def after(value, *others):
    return lax.optimization_barrier((value,) + others)[0]


def rows_at(array, start, count):
    return lax.dynamic_slice_in_dim(array, start, count, axis=0)


def on_device(
    layer_in,
    cotangent,
    lengths,
    rand_blocks,
    w_query,
    b_query,
    w_key,
    w_value,
    b_value,
    w_proj,
    b_proj,
    gain_one,
    shift_one,
    w_in,
    b_in,
    w_out,
    b_out,
    gain_two,
    shift_two,
):
    tokens, width = layer_in.shape
    ctx_count = lax.axis_size(CTX)
    fsdp_count = lax.axis_size(FSDP)
    ctx = lax.axis_index(CTX)
    tp = lax.axis_index(TP)
    y, c = tp // 2, tp % 2
    seq = tokens * ctx_count
    half, quarter = tokens // 2, tokens // 4
    shard = w_query.shape[0]
    units = w_in.shape[1]
    pair = ctx_count == 2
    order = [2 * y + 1 - c, 2 * y + c, 2 * (1 - y) + 1 - c, 2 * (1 - y) + c]
    own_rows, other_rows = ctx * tokens, (1 - ctx) * tokens

    n_long = b_in.shape[0]
    vecs = [b_query, b_value, b_in, b_proj, gain_one, shift_one, b_out, gain_two, shift_two]
    piece, x_send = open_call(
        layer_in, [order[1], order[3]], quarter, w_query, w_key, w_value, w_proj, vecs
    )
    x_got = x_swap(x_send) if pair else None
    gathered = lax.all_gather(piece, FSDP, axis=0, tiled=True)
    wi_m = lax.all_gather(after(w_in, piece), FSDP, axis=0, tiled=True)
    out_both = jnp.concatenate([w_out.T, y_swap(after(w_out.T, piece))], axis=1)
    wo = lax.all_gather(after(out_both, gathered), FSDP, axis=0, tiled=True)
    wq, wkv, wp_m, vec = split_call(fsdp_count, b_query.shape[0], n_long, gathered)
    bias = vec[:, 0:192]
    wp_t = y_swap(wp_m)
    wi_t = y_swap(wi_m)

    if pair:
        x_got = after(x_got, wkv)
        q_all, kv_own = qkv(layer_in, wq, wkv, bias, True)
        x_core = core_swap(x_got)
        kv_pieces = [kv_own] + [qkv(v, wq, wkv, bias, False)[0] for v in (x_got, x_core)]
        kv_starts = [own_rows + k * quarter for k in range(4)]
        kv_starts += [other_rows + order[k] * quarter for k in (1, 3, 0, 2)]
    else:
        q_all, _ = qkv(layer_in, wq, wkv, bias, True)
        x_all = lax.all_gather(layer_in, CTX, axis=0, tiled=True)
        kv_pieces = list(qkv(x_all, wq, wkv, bias, False))
        kv_starts = [k * quarter for k in range(seq // quarter)]
    blocks = tokens // BLK
    rand = rand_blocks.reshape(-1)
    live = lengths[0]

    def meta(half_index):
        values = [half_index * (blocks // 2), ctx * blocks, live, (1 - c) * (blocks // 4)]
        values += [(8 * y + 4 * (1 - c)) * blocks // 32, 4 * (1 - c) * blocks // 32, y]
        return jnp.stack(values).astype(jnp.int32)

    as_table = lambda values: jnp.stack([jnp.asarray(v, jnp.int32) for v in values])
    chunks = seq // quarter
    starts = as_table(kv_starts)
    kv_pieces[-1] = after(kv_pieces[-1], wp_t)
    o_send, dense_o, dense_log = attend(
        meta(1 - y), rand, starts, q_all, kv_pieces, seq, half, chunks
    )
    o_got = y_swap(o_send)
    (o_keep,) = attend(
        meta(y), rand, starts, after(q_all, o_send, wi_m), kv_pieces, seq, half, chunks, dense_o
    )
    o_keep, o_got = lax.optimization_barrier((o_keep, o_got))

    slot = jnp.stack([tp, ctx * tokens + tp * quarter, live]).astype(jnp.int32)
    part_peer, part_own = project(o_keep, o_got, wp_m, wp_t)
    resid, hidden, hid_own = norm_one(slot, layer_in, part_own, core_swap(part_peer), vec)
    hid_peer = core_swap(hid_own)

    x_order = collect(after(layer_in, o_keep), order, [x_core, x_got] if pair else [])
    outs = mlp_up(hid_peer, wi_m, wi_t, vec, wp_t, None)
    act, slope, hid = mlp_up(hid_own, wi_m, wi_t, vec, wp_t, outs)
    wo = after(wo, act, x_order)
    mlp_got = core_swap(mlp_down(act, wo, False))
    part_own = mlp_down(act, wo, True)
    out_own, gm_own, grad_two, sums_two = norm_two(slot, cotangent, hidden, part_own, mlp_got, vec)
    gm_peer = core_swap(gm_own)
    out_other = y_swap(out_own)
    outs = mlp_back(gm_peer, slope, wi_m, wi_t, wo, None)
    gh_got, dbi_peer = core_swap(outs[2]), outs[3]
    gp, gm, gh_own, dbi_own = mlp_back(gm_own, slope, wi_m, wi_t, wo, outs[0:2])
    grad_one, gb_own, sums_one = norm_one_back(resid, grad_two, gh_own, gh_got, vec)
    go_send, go_keep, gb, vec_sum = heads_back(
        core_swap(gb_own), gb_own, wp_m, wp_t, sums_two, gm_peer, sums_one, dbi_peer, dbi_own
    )
    go_got = y_swap(go_send)

    def z_sum(value):
        return lax.psum_scatter(value, FSDP, scatter_dimension=0, tiled=True)

    def x_sum(value):
        value = value.astype(bf16)
        return value.astype(f32) + x_swap(value).astype(f32) if pair else lax.psum(value, CTX).astype(f32)

    dwo = z_sum(tn(gm, act).astype(bf16))
    dwi = z_sum(tn(hid, gp).astype(bf16))
    dwp_t = tn(gb, o_got).astype(bf16)
    dwp = tn(gb, o_keep).astype(bf16)

    if pair:
        chunk_rows = [own_rows + k * quarter for k in order] + [other_rows + k * quarter for k in order]
    else:
        chunk_rows = [k * quarter for k in range(chunks)]
    starts = as_table(kv_starts + chunk_rows)
    n_send = 2 if pair else 0
    go_keep = after(go_keep, dwp_t, dwp)
    carried = attend_back(
        meta(y), rand, starts, q_all, go_keep, kv_pieces, seq, chunks, n_send, tokens
    )
    go_got, dwo, out_other, *carried = lax.optimization_barrier((go_got, dwo, out_other, *carried))
    dwo_got = y_swap(dwo[:, units:])
    dwp_got = y_swap(after(dwp_t, carried[1]))
    outs = attend_back(
        meta(1 - y), rand, starts, q_all, go_got, kv_pieces, seq, chunks, n_send, tokens,
        (carried[1], carried[0]), (go_keep, go_got, dense_o, dense_log), x_order if pair else x_order[0:8],
    )
    outs, dwo_got, dwp_got = lax.optimization_barrier((outs, dwo_got, dwp_got))
    dq, dkv, dw = outs[0:3]
    if not pair:
        dw = products_call(x_all, x_order, dq, dkv)

    gate = dkv
    table = table_call(fsdp_count, dw, dwp, dwp_got, vec_sum, go_got)
    dwo_sum = (dwo[:, 0:units].astype(f32) + dwo_got.astype(f32)).astype(bf16)
    dwi = after(dwi, table)
    dwi_sum = (dwi[:, 0:units].astype(f32) + y_swap(dwi[:, units:]).astype(f32)).astype(bf16)
    if pair:
        came = [x_swap(v) for v in outs[3:]]
        came[0] = after(came[0], dwi_sum, dwo_sum)
        gate = came[0]
        got = [came[0], came[0], came[1], came[1]]
        mine = dkv
    else:
        got = [None] * 4
        mine = collect(lax.psum_scatter(dkv, CTX, scatter_dimension=0, tiled=True), order, [])

    def back_of(k, *adds):
        return input_back(k, dq, mine, got[k], k % 2, wq, wkv, list(adds))

    sent = [core_swap(back_of(k)) for k in (0, 2)]
    lead = back_of(1, grad_one, sent[0])
    rear = back_of(3, sent[1])
    out_own, out_other = after(out_own, gate), after(out_other, gate)
    layer_out = place(
        [core_swap(out_own), out_own, core_swap(out_other), out_other],
        order,
        tokens,
    )
    both = z_sum(table)
    dwo = x_sum(dwo_sum)
    dwi = x_sum(dwi_sum)
    came_both = x_swap(both) if pair else lax.psum(both.astype(f32), CTX) - both.astype(f32)
    dwq, dwk, dwv, dwp, small = last_call(both, came_both)
    sizes = [shard] * 6 + [units // fsdp_count, 192 // fsdp_count, 192 // fsdp_count]
    db_out, dg2, ds2, dg1, ds1, db_proj, db_in, db_query, db_value = [
        small[k, 0:size] for k, size in enumerate(sizes)
    ]
    from_rear, from_lead = y_swap(rear), y_swap(lead)
    lead_sum = (lead.astype(f32) + from_rear.astype(f32)).astype(bf16)
    grad_input = place([core_swap(lead_sum), lead_sum], order[0:2], tokens)
    from_lead = after(from_lead, layer_out, dwi, dwo, dwq, small, grad_input)
    rear_sum = (rear.astype(f32) + from_lead.astype(f32)).astype(bf16)
    grad_input = place([core_swap(rear_sum), rear_sum], order[2:4], tokens, grad_input)
    return (
        layer_out,
        grad_input,
        dwq,
        db_query,
        dwk,
        dwv,
        db_value,
        dwp,
        db_proj,
        dg1,
        ds1,
        dwi,
        db_in,
        dwo.T,
        db_out,
        dg2,
        ds2,
    )


def solution(mesh):
    rows = P((FSDP, CTX), None)
    vector, unit = P(FSDP), P((TP, FSDP))
    column, row = P(FSDP, TP), P(TP, FSDP)
    return jax.shard_map(
        on_device,
        mesh=mesh,
        in_specs=(
            rows, rows, vector, P(FSDP, CTX, None), column, unit, column, column, unit, row,
            vector, vector, vector, column, unit, row, vector, vector, vector,
        ),
        out_specs=(
            rows, rows, column, unit, column, column, unit, row, vector, vector, vector,
            column, unit, row, vector, vector, vector,
        ),
        check_vma=False,
    )
```

```python
import functools
import math

import jax
import jax.numpy as jnp
from jax import lax
from jax.experimental import pallas as pl
from jax.experimental.pallas import tpu as pltpu
from jax.sharding import PartitionSpec as P

BLK = 64
PAIR = 2
MASKED = -1e30
CHUNK = 512
EPSILON = 1e-05
FSDP, CTX, TP = "fsdp", "ctx", "tp"
f32, bf16 = jnp.float32, jnp.bfloat16
ANY = pl.BlockSpec(memory_space=pl.ANY)


VM = pl.BlockSpec(memory_space=pltpu.VMEM)
HBM = pl.BlockSpec(memory_space=pltpu.HBM)
MIB = 1 << 20
LIGHT = pl.CostEstimate(flops=0, bytes_accessed=0, transcendentals=0)
SPACES = {"h": pltpu.HBM, "v": pltpu.VMEM}


def call(kernel, out_shape, ins="", outs="", **options):
    spec = options.get("grid_spec")
    tables = spec.num_scalar_prefetch if spec is not None else 0

    def letter(text, k):
        return text[min(k, len(text) - 1)] if text else "h"

    many = isinstance(out_shape, (list, tuple))
    shapes = list(out_shape) if many else [out_shape]
    shapes = [
        v if letter(outs, k) == "-" else SPACES[letter(outs, k)](v.shape, v.dtype)
        for k, v in enumerate(shapes)
    ]
    run = pl.pallas_call(kernel, out_shape=shapes if many else shapes[0], **options)

    def apply(*args):
        placed = [
            v if letter(ins, k) == "-" else pltpu.with_memory_space_constraint(v, SPACES[letter(ins, k)])
            for k, v in enumerate(args[tables:])
        ]
        return run(*args[0:tables], *placed)

    return apply


def nt(a, b):
    return lax.dot_general(a, b, (((1,), (1,)), ((), ())), preferred_element_type=f32)


def tn(a, b):
    return lax.dot_general(a, b, (((0,), (0,)), ((), ())), preferred_element_type=f32)


def nn(a, b):
    return jnp.dot(a, b, preferred_element_type=f32)


def place_kernel(count, slots_ref, *refs):
    for k in range(count):

        @pl.when(pl.program_id(0) == k)
        def _():
            refs[-1][...] = refs[k][...]


def place(pieces, slots, total, earlier=None):
    count = len(pieces)
    rows, width = pieces[0].shape
    more = [] if earlier is None else [earlier]
    return call(
        functools.partial(place_kernel, count),
        ins="-",
        outs="h",
        grid_spec=pltpu.PrefetchScalarGridSpec(
            num_scalar_prefetch=1,
            grid=(count,),
            in_specs=[whole_block(p) for p in pieces] + [ANY] * len(more),
            out_specs=pl.BlockSpec((rows, width), lambda g, s: (s[g], 0)),
        ),
        out_shape=jax.ShapeDtypeStruct((total, width), pieces[0].dtype),
        input_output_aliases={1 + count: 0} if more else {},
        compiler_params=pltpu.CompilerParams(vmem_limit_bytes=8 * MIB),
        cost_estimate=LIGHT,
        name="place",
    )(jnp.stack(slots).astype(jnp.int32), *pieces, *more)


def collect_kernel(count, slots_ref, x_ref, *refs):
    step = pl.program_id(0)

    @pl.when(step < 4)
    def _():
        refs[count][...] = x_ref[...]

    rows = x_ref.shape[0]
    parts = [(ref, at) for at in range(0, 2 * rows, rows) for ref in refs[:count]]
    for k, (ref, at) in enumerate(parts):

        @pl.when(step == 4 + k)
        def _():
            refs[count][...] = ref[at : at + rows, :]


def collect(x, slots, others):
    count = len(others)
    rows, width = x.shape[0] // 4, x.shape[1]
    steps = 4 + sum(v.shape[0] // rows for v in others)
    return call(
        functools.partial(collect_kernel, count),
        grid_spec=pltpu.PrefetchScalarGridSpec(
            num_scalar_prefetch=1,
            grid=(steps,),
            in_specs=[pl.BlockSpec((rows, width), lambda g, s: (s[jnp.minimum(g, 3)], 0))]
            + [whole_block(v) for v in others],
            out_specs=pl.BlockSpec((rows, width), lambda g, s: (g, 0)),
        ),
        out_shape=jax.ShapeDtypeStruct((steps * rows, width), x.dtype),
        compiler_params=pltpu.CompilerParams(vmem_limit_bytes=8 * MIB),
        cost_estimate=LIGHT,
        name="collect",
    )(jnp.stack(slots).astype(jnp.int32), x, *others)


def load_all(pairs, sems):
    copies = [pltpu.make_async_copy(src, dst, sems.at[k]) for k, (src, dst) in enumerate(pairs)]
    for copy in copies:
        copy.start()
    for copy in copies:
        copy.wait()


def open_kernel(count, slots_ref, x_ref, *refs):
    srcs, vecs = refs[0:4], refs[4:13]
    a_ref, half_ref, wq, wk, wv, wp, sems = refs[13:]
    size = half_ref.shape[0] // count
    pairs = []
    for k in range(count):
        start = pl.multiple_of(slots_ref[k] * size, 64)
        pairs.append((x_ref.at[pl.ds(start, size)], half_ref.at[pl.ds(k * size, size)]))
    load_all(list(zip(srcs, (wq, wk, wv, wp))) + pairs, sems)
    rows = wq.shape[0]
    a_ref[0:rows, 0:192] = wq[...]
    a_ref[0:rows, 192:384] = wk[...]
    a_ref[0:rows, 384:448] = wv[:, 128:192]
    a_ref[0:rows, 448:576] = wv[:, 0:128]
    turned_p = wp[...].T
    a_ref[0:rows, 576:640] = turned_p[:, 128:192]
    a_ref[0:rows, 640:768] = turned_p[:, 0:128]
    a_ref[rows : rows + 16, :] = jnp.zeros((16, 768), bf16)
    for k, vec in enumerate(vecs):
        n = vec.shape[0]
        a_ref[rows + k : rows + k + 1, 0:n] = vec[...].reshape(1, n)


def whole_block(value):
    zeros = (0,) * value.ndim
    return pl.BlockSpec(value.shape, lambda *_: zeros, pipeline_mode=pl.Buffered(1))


def open_call(x, slots, size, wq, wk, wv, wp, vecs):
    count = len(slots)
    rows, width = wq.shape[0], x.shape[1]
    srcs = [wq, wk, wv, wp]
    return call(
        functools.partial(open_kernel, count),
        grid_spec=pltpu.PrefetchScalarGridSpec(
            num_scalar_prefetch=1,
            grid=(1,),
            in_specs=[HBM] * 5 + [whole_block(v) for v in vecs],
            out_specs=[
                pl.BlockSpec((rows + 16, 768), lambda g, s: (0, 0)),
                pl.BlockSpec((count * size, width), lambda g, s: (0, 0)),
            ],
            scratch_shapes=[pltpu.VMEM(v.shape, bf16) for v in srcs]
            + [pltpu.SemaphoreType.DMA((4 + count,))],
        ),
        out_shape=[
            jax.ShapeDtypeStruct((rows + 16, 768), bf16),
            jax.ShapeDtypeStruct((count * size, width), bf16),
        ],
        compiler_params=pltpu.CompilerParams(vmem_limit_bytes=8 * MIB),
        cost_estimate=LIGHT,
        name="open",
    )(jnp.stack(slots).astype(jnp.int32), x, *srcs, *vecs)


def qkv_kernel(with_q, x_ref, wq_ref, wkv_ref, bias_ref, *outs):
    x = x_ref[...]
    zero = jnp.zeros((1, 64), f32)
    value_bias = bias_ref[1:2, :]
    bkv = jnp.concatenate([zero, zero, zero, value_bias[:, 128:192], value_bias[:, 0:128]], axis=1)
    outs[-1][...] = (nn(x, wkv_ref[...]) + bkv).astype(bf16)
    if with_q:
        bq = jnp.concatenate([bias_ref[0:1, :], zero], axis=1)
        outs[0][...] = (nn(x, wq_ref[...]) + bq).astype(bf16) * jnp.asarray(0.125, bf16)


def qkv(x, wq, wkv, bias, with_q):
    rows, width = x.shape
    tile = rows // 2 if rows <= 1024 else 512
    widths = [256, 384] if with_q else [384]
    return call(
        functools.partial(qkv_kernel, with_q),
        grid=(rows // tile,),
        in_specs=[pl.BlockSpec((tile, width), lambda g: (g, 0))]
        + [whole_block(v) for v in (wq, wkv, bias)],
        out_specs=[pl.BlockSpec((tile, w), lambda g: (g, 0)) for w in widths],
        out_shape=[jax.ShapeDtypeStruct((rows, w), bf16) for w in widths],
        compiler_params=pltpu.CompilerParams(vmem_limit_bytes=12 * MIB),
        cost_estimate=LIGHT,
        name="qkv",
    )(x, wq, wkv, bias)


def head_masks(places):
    group = lax.broadcasted_iota(jnp.int32, (1, 256), 1) // 64
    return [(group == place).astype(bf16) for place in places]


def spread(rows, masks):
    return jnp.concatenate([rows * m for m in masks], axis=0)


def fold(stacked, masks):
    n = stacked.shape[0] // 3
    out = stacked[0:n] * masks[0].astype(f32)
    for h in (1, 2):
        out = out + stacked[h * n : (h + 1) * n] * masks[h].astype(f32)
    return out


def tile_starts(i, b, rand_ref, seq):
    near = jnp.clip((i - 1) * BLK, 0, seq - 3 * BLK)
    near = pl.multiple_of(near, BLK)
    rand = [pl.multiple_of(rand_ref[3 * b + r] * BLK, BLK) for r in range(3)]
    return near, rand


def gather_tiles(kv, near, rand):
    parts = [kv[pl.ds(near, 3 * BLK), :]]
    parts += [kv[pl.ds(r, BLK), :] for r in rand]
    parts += [kv[0 : 2 * BLK, :]]
    return jnp.concatenate(parts, axis=0)


def tile_live(i, near, rand, length):
    out = []
    for j in range(3):
        blk = near // BLK + j
        out.append(jnp.where(jnp.abs(blk - i) <= 1, length - blk * BLK, 0))
    out += [length - r for r in rand]
    for g in range(2):
        out.append(jnp.where(jnp.abs(i - g) > 1, length - g * BLK, 0))
    return out


def load_pieces(size, starts_ref, pieces, kv, sems):
    copies = []
    for piece in pieces:
        for at in range(0, piece.shape[0], size):
            k = len(copies)
            start = pl.multiple_of(starts_ref[k], 64)
            copies.append(
                pltpu.make_async_copy(
                    piece.at[pl.ds(at, size)], kv.at[pl.ds(start, size)], sems.at[k]
                )
            )
    for copy in copies:
        copy.start()
    for copy in copies:
        copy.wait()


def step_block(meta_ref, step, steps):
    first = meta_ref[0] + PAIR * lax.rem(step + meta_ref[3] // PAIR, steps)
    return first, meta_ref[1] + first, meta_ref[2]


def turned(column):
    return jnp.broadcast_to(column, (column.shape[0], 128)).T[0:1, :]


def fwd_kernel(count, chunks, leads, meta_ref, rand_ref, starts_ref, q_ref, qd_ref, *rest):
    pieces, rest = rest[:count], rest[count:]
    if leads:
        o_ref, dense_ref, log_ref, kv, sems = rest
    else:
        dense_ref, o_ref, kv, sems = rest
    seq = kv.shape[0]
    step = pl.program_id(0) - (1 if leads else 0)
    steps = pl.num_programs(0) - (1 if leads else 0)
    first, block0, length = step_block(meta_ref, jnp.maximum(step, 0), steps)
    kmask = head_masks((0, 1, 2))
    vmask = head_masks((2, 3, 1))

    @pl.when(pl.program_id(0) == 0)
    def _():
        load_pieces(seq // chunks, starts_ref, pieces, kv, sems)

    def sparse(u):
        i = block0 + u
        near, rand = tile_starts(i, first + u, rand_ref, seq)
        tiles = gather_tiles(kv, near, rand)
        live = tile_live(i, near, rand, length)
        lane = lax.broadcasted_iota(jnp.int32, (1, BLK), 1)
        bias = jnp.concatenate([jnp.where(lane < n, 0.0, MASKED) for n in live], axis=1)
        qs = spread(q_ref[u * BLK : (u + 1) * BLK, :], kmask)
        s = nt(qs, tiles[:, 0:256]) + bias
        top = jnp.max(s, axis=1, keepdims=True)
        p = jnp.exp(s - top)
        total = jnp.sum(p, axis=1, keepdims=True)
        mixed = nn(p.astype(bf16), tiles[:, 128:384]) / total
        o_ref[u * BLK : (u + 1) * BLK, :] = fold(mixed, vmask).astype(bf16)

    def dense():
        qs = jnp.concatenate(
            [spread(qd_ref[u * BLK : (u + 1) * BLK, :], kmask) for u in range(PAIR)], axis=0
        )
        rows = qs.shape[0]
        lane = lax.broadcasted_iota(jnp.int32, (1, CHUNK), 1)

        def body(c, carry):
            top, total, mixed = carry
            start = pl.multiple_of(c * CHUNK, CHUNK)
            keys = kv[pl.ds(start, CHUNK), :]
            s = nt(qs, keys[:, 0:256]) + jnp.where(lane + start < length, 0.0, MASKED)
            new = jnp.maximum(top, jnp.max(s, axis=1, keepdims=True))
            scale = jnp.exp(top - new)
            p = jnp.exp(s - new)
            total = total * scale + jnp.sum(p, axis=1, keepdims=True)
            mixed = mixed * scale + nn(p.astype(bf16), keys[:, 128:384])
            return new, total, mixed

        init = (
            jnp.full((rows, 1), MASKED, f32),
            jnp.zeros((rows, 1), f32),
            jnp.zeros((rows, 256), f32),
        )
        top, total, mixed = lax.fori_loop(0, seq // CHUNK, body, init)
        mixed = mixed / total
        log_ref[...] = jnp.broadcast_to(turned(top + jnp.log(total)), log_ref.shape)
        half = rows // PAIR
        for u in range(PAIR):
            dense_ref[u * BLK : (u + 1) * BLK, :] = fold(
                mixed[u * half : (u + 1) * half], vmask
            ).astype(bf16)

    if leads:

        @pl.when((step < 0) & (meta_ref[1] == 0))
        def _():
            dense()

    @pl.when((step >= 0) & (block0 >= 2))
    def _():
        for u in range(PAIR):
            sparse(u)

    @pl.when((step >= 0) & (block0 < 2))
    def _():
        o_ref[...] = dense_ref[...]


def q_specs(steps, shift):
    def block(g, m, r, s):
        step = jnp.clip(g - shift, 0, steps - 1)
        return (m[0] // PAIR + lax.rem(step + m[3] // PAIR, steps), 0)

    fixed = pl.BlockSpec((PAIR * BLK, 256), lambda g, m, r, s: (0, 0))
    return [pl.BlockSpec((PAIR * BLK, 256), block), fixed]


def attend(meta, rand, starts, q, pieces, seq, rows, chunks, dense=None):
    steps = rows // (PAIR * BLK)
    count = len(pieces)
    leads = dense is None
    fixed = pl.BlockSpec((PAIR * BLK, 256), lambda g, m, r, s: (0, 0))
    out_specs = [
        pl.BlockSpec((PAIR * BLK, 256), lambda g, m, r, s: (jnp.maximum(g - (1 if leads else 0), 0), 0))
    ]
    out_shape = [jax.ShapeDtypeStruct((rows, 256), bf16)]
    if leads:
        out_specs += [fixed, pl.BlockSpec((8, 3 * PAIR * BLK), lambda g, m, r, s: (0, 0))]
        out_shape += [
            jax.ShapeDtypeStruct((PAIR * BLK, 256), bf16),
            jax.ShapeDtypeStruct((8, 3 * PAIR * BLK), f32),
        ]
    return call(
        functools.partial(fwd_kernel, count, chunks, leads),
        grid_spec=pltpu.PrefetchScalarGridSpec(
            num_scalar_prefetch=3,
            grid=(steps + (1 if leads else 0),),
            in_specs=q_specs(steps, 1 if leads else 0) + [ANY] * count + ([] if leads else [fixed]),
            out_specs=out_specs,
            scratch_shapes=[pltpu.VMEM((seq, 384), bf16), pltpu.SemaphoreType.DMA((chunks,))],
        ),
        out_shape=out_shape,
        compiler_params=pltpu.CompilerParams(vmem_limit_bytes=seq * 768 + 6 * MIB),
        cost_estimate=LIGHT,
        name="attend",
    )(meta, rand, starts, q, q, *pieces, *([] if leads else [dense]))


def bwd_kernel(count, last, chunks, n_send, meta_ref, rand_ref, starts_ref, q_ref, qd_ref, do_ref, *rest):
    pieces, rest = rest[:count], rest[count:]
    if last:
        in_ref, _, own_ref, came_ref, od_ref, log_ref, dq_ref, all_ref = rest[:8]
        sends, (kv, acc, sems) = rest[8 : 8 + n_send], rest[-3:]
    else:
        dq_ref, out_ref, kv, acc, sems = rest
    seq = kv.shape[0]
    step = pl.program_id(0)
    steps = pl.num_programs(0) - (1 if last else 0)
    first, block0, length = step_block(meta_ref, jnp.minimum(step, steps - 1), steps)
    kmask = head_masks((0, 1, 2))
    vmask = head_masks((2, 3, 1))

    @pl.when(step == 0)
    def _():
        if last:
            carry = pltpu.make_async_copy(in_ref, acc, sems.at[chunks])
            carry.start()
        else:
            acc[...] = jnp.zeros_like(acc)
        load_pieces(seq // chunks, starts_ref, pieces, kv, sems)
        if last:
            carry.wait()

    def add_rows(start, n, wk, wv):
        rows = pl.ds(start, n)
        acc[rows, 0:128] += wk[:, 0:128]
        acc[rows, 128:256] += wk[:, 128:256] + wv[:, 0:128]
        acc[rows, 256:384] += wv[:, 128:256]

    def sparse(u):
        i = block0 + u
        near, rand = tile_starts(i, first + u, rand_ref, seq)
        tiles = gather_tiles(kv, near, rand)
        live = tile_live(i, near, rand, length)
        row = lax.broadcasted_iota(jnp.int32, (BLK, 192), 0)
        qs = spread(q_ref[u * BLK : (u + 1) * BLK, :], kmask)
        gs = spread(do_ref[u * BLK : (u + 1) * BLK, :], vmask)
        s = nt(tiles[:, 0:256], qs)
        s = jnp.concatenate(
            [jnp.where(row < live[j], s[j * BLK : (j + 1) * BLK], MASKED) for j in range(8)],
            axis=0,
        )
        top = jnp.max(s, axis=0, keepdims=True)
        p = jnp.exp(s - top)
        p = p * (1.0 / jnp.sum(p, axis=0, keepdims=True))
        dp = nt(tiles[:, 128:384], gs)
        inner = jnp.sum(p * dp, axis=0, keepdims=True)
        ds = (p * (dp - inner)).astype(bf16)
        wk = nn(ds, qs)
        wv = nn(p.astype(bf16), gs)
        add_rows(near, 192, wk[0:192], wv[0:192])
        for r in range(3):
            a = 192 + r * BLK
            add_rows(rand[r], BLK, wk[a : a + BLK], wv[a : a + BLK])
        add_rows(0, 128, wk[384:512], wv[384:512])
        dq = fold(tn(ds, tiles[:, 0:256]), kmask) * 0.125
        dq_ref[u * BLK : (u + 1) * BLK, :] = dq.astype(bf16)

    def dense():
        rows_g = jnp.where(meta_ref[6] == 0, own_ref[...].astype(f32), came_ref[...].astype(f32))
        qs, gs, inner = [], [], []
        for u in range(PAIR):
            rows = slice(u * BLK, (u + 1) * BLK)
            qs.append(spread(qd_ref[rows, :], kmask))
            gs.append(spread(rows_g[rows, :].astype(bf16), vmask))
            for m in vmask:
                part = rows_g[rows, :] * od_ref[rows, :].astype(f32) * m.astype(f32)
                inner.append(jnp.sum(part, axis=1, keepdims=True))
        qs, gs = jnp.concatenate(qs, axis=0), jnp.concatenate(gs, axis=0)
        inner = turned(jnp.concatenate(inner, axis=0))
        log_sum = log_ref[0:1, :]
        cols = qs.shape[0]
        row = lax.broadcasted_iota(jnp.int32, (CHUNK, cols), 0)

        def back(c, dq):
            start = pl.multiple_of(c * CHUNK, CHUNK)
            keys = kv[pl.ds(start, CHUNK), :]
            s = jnp.where(row < length - start, nt(keys[:, 0:256], qs), MASKED)
            p = jnp.exp(s - log_sum)
            ds = (p * (nt(keys[:, 128:384], gs) - inner)).astype(bf16)
            add_rows(start, CHUNK, nn(ds, qs), nn(p.astype(bf16), gs))
            return dq + tn(ds, keys[:, 0:256])

        dq = lax.fori_loop(0, seq // CHUNK, back, jnp.zeros((cols, 256), f32))
        half = cols // PAIR
        for u in range(PAIR):
            dq_ref[u * BLK : (u + 1) * BLK, :] = (
                fold(dq[u * half : (u + 1) * half], kmask) * 0.125
            ).astype(bf16)

    @pl.when((step < steps) & (block0 >= 2))
    def _():
        for u in range(PAIR):
            sparse(u)

    if last:

        @pl.when((step == steps) & (meta_ref[1] == 0))
        def _():
            dense()

    @pl.when(pl.program_id(0) == pl.num_programs(0) - 1)
    def _():
        if not last:
            pltpu.sync_copy(acc, out_ref)
        else:
            size = seq // chunks

            def emit(k):
                start = pl.multiple_of(starts_ref[chunks + k], 64)
                return acc[pl.ds(start, size), :].astype(bf16)

            for k in range(chunks):
                piece = emit(k)
                all_ref[k * size : (k + 1) * size, :] = piece
                if n_send and k >= chunks - 4:
                    j = k - chunks + 4
                    dst, at = sends[j // 2], j % 2
                    dst[at * size : (at + 1) * size, :] = piece


def attend_back(meta, rand, starts, q, grad, pieces, seq, chunks, n_send, tokens, carried=None, dense=None):
    rows = tokens // 2
    steps = rows // (PAIR * BLK)
    count = len(pieces)
    last = carried is not None
    shape = (PAIR * BLK, 256)
    more = []
    if last:

        def dq_block(g, m, r, s):
            return (jnp.where((g == steps) & (m[1] == 0), m[4], jnp.minimum(g, steps - 1) + steps), 0)

        chosen = pl.BlockSpec(shape, lambda g, m, r, s: (m[5], 0))
        more = [
            chosen,
            chosen,
            pl.BlockSpec(shape, lambda g, m, r, s: (0, 0)),
            pl.BlockSpec((8, 3 * PAIR * BLK), lambda g, m, r, s: (0, 0)),
        ]
    else:
        dq_block = lambda g, m, r, s: (g, 0)
    out_specs = [pl.BlockSpec(shape, dq_block)]
    out_shape = [jax.ShapeDtypeStruct((tokens, 256), bf16)]
    if last:
        sizes = [seq] + [2 * seq // chunks] * n_send
        outs = [(n, 384, bf16) for n in sizes]
        out_specs += [
            pl.BlockSpec((n, w), lambda g, m, r, s: (0, 0), pipeline_mode=pl.Buffered(1)) for n, w, _ in outs
        ]
        out_shape += [jax.ShapeDtypeStruct((n, w), t) for n, w, t in outs]
    else:
        out_specs += [ANY]
        out_shape += [jax.ShapeDtypeStruct((seq, 384), f32)]
    grad_spec = pl.BlockSpec(shape, lambda g, m, r, s: (jnp.minimum(g, steps - 1), 0))
    return call(
        functools.partial(bwd_kernel, count, last, chunks, n_send),
        grid_spec=pltpu.PrefetchScalarGridSpec(
            num_scalar_prefetch=3,
            grid=(steps + (1 if last else 0),),
            in_specs=q_specs(steps, 0) + [grad_spec] + [ANY] * (count + (2 if last else 0)) + more,
            out_specs=out_specs,
            scratch_shapes=[
                pltpu.VMEM((seq, 384), bf16),
                pltpu.VMEM((seq, 384), f32),
                pltpu.SemaphoreType.DMA((chunks + 1,)),
            ],
        ),
        out_shape=out_shape,
        input_output_aliases={3 + 3 + count + 1: 0} if last else {},
        compiler_params=pltpu.CompilerParams(
            vmem_limit_bytes=seq * (3840 if last else 2304) + 7 * MIB
        ),
        cost_estimate=LIGHT,
        name="attend_back",
    )(meta, rand, starts, q, q, grad, *pieces, *(carried or ()), *(dense or ()))


def split_kernel(count, short, long, a_ref, wq_ref, wkv_ref, ship_ref, vec_ref):
    step = a_ref.shape[0] // count
    rows = step - 16
    parts = []
    for k in range(count):
        there, here = slice(k * step, k * step + rows), slice(k * rows, (k + 1) * rows)
        zero = jnp.zeros((rows, 64), bf16)
        wq_ref[here, 0:192] = a_ref[there, 0:192]
        wq_ref[here, 192:256] = zero
        wkv_ref[here, :] = a_ref[there, 192:576]
        ship_ref[here, 0:64] = zero
        ship_ref[here, 64:256] = a_ref[there, 576:768]
        parts.append(a_ref[k * step + rows : (k + 1) * step, :].astype(f32))
    width = vec_ref.shape[1]
    attn = jnp.concatenate([p[:, 0:short] for p in parts], axis=1)
    attn = jnp.concatenate([attn, jnp.zeros((16, width - attn.shape[1]), f32)], axis=1)
    dense = jnp.concatenate([p[:, 0:long] for p in parts], axis=1)
    vec = jnp.concatenate([attn[0:2], dense[2:16]], axis=0)
    vec_ref[...] = vec
    ship = jnp.concatenate([vec[2:3, k * 256 : (k + 1) * 256] for k in range(3)], axis=0)
    ship = jnp.concatenate([ship, jnp.zeros((13, 256), f32)], axis=0)
    ship_ref[count * rows : count * rows + 16, :] = ship.astype(bf16)


def split_call(count, short, long, gathered):
    rows = gathered.shape[0] - 16 * count
    outs = [
        jax.ShapeDtypeStruct((rows, 256), bf16),
        jax.ShapeDtypeStruct((rows, 384), bf16),
        jax.ShapeDtypeStruct((rows + 16, 256), bf16),
        jax.ShapeDtypeStruct((16, count * long), f32),
    ]
    return call(
        functools.partial(split_kernel, count, short, long),
        outs="-",
        grid=(1,),
        in_specs=[whole_block(gathered)],
        out_specs=[whole_block(v) for v in outs],
        out_shape=outs,
        compiler_params=pltpu.CompilerParams(vmem_limit_bytes=10 * MIB),
        cost_estimate=LIGHT,
        name="split",
    )(gathered)


TILE = 256


def proj_kernel(keep_ref, got_ref, wm_ref, wt_ref, peer_ref, own_ref):
    half, width = peer_ref.shape
    for k, out in enumerate((peer_ref, own_ref)):
        rows = slice(k * half, (k + 1) * half)
        value = nt(keep_ref[rows, :], wm_ref[0:width, :]) + nt(got_ref[rows, :], wt_ref[0:width, :])
        out[...] = value.astype(out.dtype)


def in_vmem(kernel, out_shape, limit, name, aliases=None, outs="v", ins="v"):
    def pick(text, values):
        return [VM if text[min(k, len(text) - 1)] == "v" else whole_block(v) for k, v in enumerate(values)]

    return lambda *args: call(
        kernel,
        ins=ins,
        outs=outs,
        grid=(1,),
        in_specs=pick(ins, args),
        out_specs=pick(outs, out_shape),
        out_shape=out_shape,
        input_output_aliases=aliases or {},
        compiler_params=pltpu.CompilerParams(vmem_limit_bytes=limit * MIB),
        cost_estimate=LIGHT,
        name=name,
    )(*args)


def project(keep, got, wm, wt):
    rows, width = keep.shape[0] // 2, wm.shape[0] - 16
    outs = [jax.ShapeDtypeStruct((rows, width), bf16)] * 2
    return in_vmem(proj_kernel, outs, 10, "project", outs="h", ins="-")(keep, got, wm, wt)


def stats(value):
    center = jnp.mean(value, axis=-1, keepdims=True)
    offset = value - center
    inverse = lax.rsqrt(jnp.mean(offset * offset, axis=-1, keepdims=True) + EPSILON)
    return offset * inverse, inverse


def fetch_two(slot_ref, src, dst, came, got, sems):
    start = pl.multiple_of(slot_ref[0] * dst.shape[0], 64)
    load_all([(src.at[pl.ds(start, dst.shape[0])], dst), (came, got)], sems)


def norm_one_kernel(
    slot_ref, x_ref, came_ref, part_ref, vec_ref, resid_ref, hidden_ref, low_ref, rows_ref, got_ref, sems
):
    fetch_two(slot_ref, x_ref, rows_ref, came_ref, got_ref, sems)
    for k in range(0, part_ref.shape[0], TILE):
        rows = slice(k, k + TILE)
        resid = rows_ref[rows, :].astype(f32) + (
            part_ref[rows, :].astype(f32) + got_ref[rows, :].astype(f32) + vec_ref[3:4, :]
        )
        resid_ref[rows, :] = resid
        normed, _ = stats(resid)
        hidden = normed * vec_ref[4:5, :] + vec_ref[5:6, :]
        hidden_ref[rows, :] = hidden
        low_ref[rows, :] = hidden.astype(bf16)


def norm_one(slot, x, part, got, vec):
    rows, width = part.shape
    return call(
        norm_one_kernel,
        ins="h-",
        outs="h",
        grid_spec=pltpu.PrefetchScalarGridSpec(
            num_scalar_prefetch=1,
            grid=(1,),
            in_specs=[HBM, ANY] + [whole_block(v) for v in (part, vec)],
            out_specs=[pl.BlockSpec((rows, width), lambda g, s: (0, 0))] * 3,
            scratch_shapes=[pltpu.VMEM((rows, width), bf16)] * 2 + [pltpu.SemaphoreType.DMA((2,))],
        ),
        out_shape=[jax.ShapeDtypeStruct((rows, width), t) for t in (f32, f32, bf16)],
        compiler_params=pltpu.CompilerParams(vmem_limit_bytes=14 * MIB),
        cost_estimate=LIGHT,
        name="norm_one",
    )(slot, x, got, part, vec)


def add_sums(total, low, error, normed):
    sums = [jnp.sum(v, axis=0, keepdims=True) for v in (low.astype(f32), error * normed, error)]
    return sums if total is None else [x + z for x, z in zip(total, sums)]


def ride(low_ref, sums_ref, total):
    sums = jnp.concatenate(total + [jnp.zeros((5, low_ref.shape[1]), f32)], axis=0)
    sums_ref[...] = sums
    rows = low_ref.shape[0] - 16
    low_ref[rows : rows + 16, :] = jnp.concatenate([sums, jnp.zeros_like(sums)], axis=0).astype(bf16)


def norm_two_kernel(
    slot_ref, cot_ref, came_ref, hidden_ref, part_ref, vec_ref,
    out_ref, low_ref, grad_ref, sums_ref, rows_ref, got_ref, sems,
):
    fetch_two(slot_ref, cot_ref, rows_ref, came_ref, got_ref, sems)
    gain = vec_ref[7:8, :]
    total = None
    for k in range(0, part_ref.shape[0], TILE):
        rows = slice(k, k + TILE)
        value = hidden_ref[rows, :] + (part_ref[rows, :].astype(f32) + got_ref[rows, :].astype(f32)) + vec_ref[6:7, :]
        normed, inverse = stats(value)
        position = slot_ref[1] + k + lax.broadcasted_iota(jnp.int32, (TILE, 1), 0)
        live = (position < slot_ref[2]).astype(f32)
        out_ref[rows, :] = ((normed * gain + vec_ref[8:9, :]) * live).astype(bf16)
        error = rows_ref[rows, :].astype(f32) * live
        inner = error * gain
        first = jnp.mean(inner, axis=-1, keepdims=True)
        second = jnp.mean(inner * normed, axis=-1, keepdims=True)
        grad = inverse * (inner - first - normed * second)
        grad_ref[rows, :] = grad
        low = grad.astype(bf16)
        low_ref[rows, :] = low
        total = add_sums(total, low, error, normed)
    ride(low_ref, sums_ref, total)


def norm_two(slot, cotangent, hidden, part, got, vec):
    rows, width = part.shape
    return call(
        norm_two_kernel,
        ins="h-",
        outs="h",
        grid_spec=pltpu.PrefetchScalarGridSpec(
            num_scalar_prefetch=1,
            grid=(1,),
            in_specs=[HBM, ANY] + [whole_block(v) for v in (hidden, part, vec)],
            out_specs=[
                pl.BlockSpec((n, width), lambda g, s: (0, 0)) for n in (rows, rows + 16, rows, 8)
            ],
            scratch_shapes=[pltpu.VMEM((rows, width), bf16)] * 2 + [pltpu.SemaphoreType.DMA((2,))],
        ),
        out_shape=[
            jax.ShapeDtypeStruct((rows, width), bf16),
            jax.ShapeDtypeStruct((rows + 16, width), bf16),
            jax.ShapeDtypeStruct((rows, width), f32),
            jax.ShapeDtypeStruct((8, width), f32),
        ],
        compiler_params=pltpu.CompilerParams(vmem_limit_bytes=14 * MIB),
        cost_estimate=LIGHT,
        name="norm_two",
    )(slot, cotangent, got, hidden, part, vec)


def norm_one_back_kernel(resid_ref, two_ref, part_ref, got_ref, vec_ref, grad_ref, low_ref, sums_ref):
    total = None
    for k in range(0, part_ref.shape[0], TILE):
        rows = slice(k, k + TILE)
        normed, inverse = stats(resid_ref[rows, :])
        error = two_ref[rows, :] + (part_ref[rows, :].astype(f32) + got_ref[rows, :].astype(f32))
        inner = error * vec_ref[4:5, :]
        first = jnp.mean(inner, axis=-1, keepdims=True)
        second = jnp.mean(inner * normed, axis=-1, keepdims=True)
        grad = inverse * (inner - first - normed * second)
        grad_ref[rows, :] = grad
        low = grad.astype(bf16)
        low_ref[rows, :] = low
        total = add_sums(total, low, error, normed)
    ride(low_ref, sums_ref, total)


def norm_one_back(resid, two, part, got, vec):
    rows, width = part.shape
    outs = [
        jax.ShapeDtypeStruct((rows, width), f32),
        jax.ShapeDtypeStruct((rows + 16, width), bf16),
        jax.ShapeDtypeStruct((8, width), f32),
    ]
    return in_vmem(norm_one_back_kernel, outs, 14, "norm_one_back", outs="h", ins="-")(resid, two, part, got, vec)


ERFC = (
    -1.26551223, 1.00002368, 0.37409196, 0.09678418, -0.18628806,
    0.27886807, -1.13520398, 1.48851587, -0.82215223, 0.17087277,
)


def gelu_pair(pre):
    z = jnp.abs(pre) * math.sqrt(0.5)
    t = 1.0 / (1.0 + 0.5 * z)
    poly = jnp.full_like(t, ERFC[-1])
    for coefficient in ERFC[-2::-1]:
        poly = poly * t + coefficient
    square = -z * z
    tail = 0.5 * t * jnp.exp(square + poly)
    cdf = jnp.where(pre < 0, tail, 1.0 - tail)
    density = jnp.exp(square) * (1.0 / math.sqrt(2.0 * math.pi))
    return (pre * cdf).astype(bf16), (cdf + pre * density).astype(bf16)


def up_kernel(base, hid_ref, wim_ref, wit_ref, vec_ref, ship_ref, *rest):
    act_ref, slope_ref, all_ref = rest[-3:]
    units, at = wim_ref.shape[1], ship_ref.shape[0] - 16
    shipped = ship_ref[at : at + 16, :].astype(f32)
    shipped = jnp.concatenate([shipped[k : k + 1, :] for k in range(3)], axis=1)
    for k in range(0, hid_ref.shape[0], TILE):
        rows, there = slice(k, k + TILE), slice(base + k, base + k + TILE)
        hid = hid_ref[rows, :]
        all_ref[there, :] = hid
        for j, (wi, b) in enumerate(((wim_ref, vec_ref[2:3, :]), (wit_ref, shipped))):
            act, slope = gelu_pair(nn(hid, wi[...]) + b)
            act_ref[there, j * units : (j + 1) * units] = act
            slope_ref[there, j * units : (j + 1) * units] = slope


def mlp_up(hid, wi_m, wi_t, vec, ship, earlier):
    rows, width = hid.shape
    units = wi_m.shape[1]
    big = jax.ShapeDtypeStruct((2 * rows, 2 * units), bf16)
    outs = [big, big, jax.ShapeDtypeStruct((2 * rows, width), bf16)]
    second = earlier is not None
    kernel = functools.partial(up_kernel, rows if second else 0)
    aliases = {5 + k: k for k in range(3)} if second else {}
    args = (hid, wi_m, wi_t, vec, ship) + (tuple(earlier) if second else ())
    return in_vmem(kernel, outs, 16, "mlp_up", aliases, ins="-----v")(*args)


def down_kernel(base, act_ref, wo_ref, part_ref):
    for k in range(0, part_ref.shape[0], TILE):
        there = slice(base + k, base + k + TILE)
        part_ref[k : k + TILE, :] = nt(act_ref[there, :], wo_ref[...]).astype(bf16)


def mlp_down(act, wo, second):
    rows = act.shape[0] // 2
    kernel = functools.partial(down_kernel, rows if second else 0)
    outs = [jax.ShapeDtypeStruct((rows, wo.shape[0]), bf16)]
    return in_vmem(kernel, outs, 10, "mlp_down", outs="h", ins="v-")(act, wo)[0]


def mlp_back_kernel(base, gm_ref, slope_ref, wim_ref, wit_ref, wo_ref, *rest):
    gp_ref, all_ref, part_ref, sums_ref = rest[-4:]
    units = wim_ref.shape[1]
    sums = [None, None]
    for k in range(0, part_ref.shape[0], TILE):
        rows, there = slice(k, k + TILE), slice(base + k, base + k + TILE)
        gm = gm_ref[rows, :]
        all_ref[there, :] = gm
        total = None
        for j, wi in enumerate((wim_ref, wit_ref)):
            cols = slice(j * units, (j + 1) * units)
            gp = (nn(gm, wo_ref[:, cols]) * slope_ref[there, cols].astype(f32)).astype(bf16)
            gp_ref[there, cols] = gp
            column = jnp.sum(gp.astype(f32), axis=0, keepdims=True)
            sums[j] = column if sums[j] is None else sums[j] + column
            value = nt(gp, wi[...])
            total = value if total is None else total + value
        part_ref[rows, :] = total.astype(bf16)
    sums_ref[...] = jnp.concatenate(sums + [jnp.zeros((6, units), f32)], axis=0)


def mlp_back(gm, slope, wi_m, wi_t, wo, earlier):
    rows, width = gm.shape[0] - 16, gm.shape[1]
    units = wi_m.shape[1]
    outs = [
        jax.ShapeDtypeStruct((2 * rows, 2 * units), bf16),
        jax.ShapeDtypeStruct((2 * rows, width), bf16),
        jax.ShapeDtypeStruct((rows, width), bf16),
        jax.ShapeDtypeStruct((8, units), f32),
    ]
    second = earlier is not None
    kernel = functools.partial(mlp_back_kernel, rows if second else 0)
    aliases = {5 + k: k for k in range(2)} if second else {}
    args = (gm, slope, wi_m, wi_t, wo) + (tuple(earlier) if second else ())
    return in_vmem(kernel, outs, 20, "mlp_back", aliases, outs="vvhh", ins="-v---v")(*args)


def heads_kernel(
    peer_ref, own_ref, wm_ref, wt_ref, two_ref, twop_ref, one_ref, dbi_a_ref, dbi_b_ref,
    send_ref, keep_ref, both_ref, vec_ref,
):
    half = peer_ref.shape[0] - 16
    for k, ref in enumerate((peer_ref, own_ref)):
        rows = slice(k * half, (k + 1) * half)
        grad = ref[0:half, :]
        both_ref[rows, :] = grad
        send_ref[rows, :] = nn(grad, wt_ref[0 : grad.shape[1], :]).astype(bf16)
        keep_ref[rows, :] = nn(grad, wm_ref[0 : grad.shape[1], :]).astype(bf16)
    two = two_ref[...] + twop_ref[half : half + 16, :].astype(f32)[0:8]
    one = one_ref[...] + peer_ref[half : half + 16, :].astype(f32)[0:8]
    dbi = dbi_a_ref[...] + dbi_b_ref[...]
    vec = jnp.concatenate([two[0:3], one[0:3], dbi[1:2], dbi[0:1]], axis=0)
    vec_ref[...] = vec
    width = vec.shape[1] // 3
    packed = jnp.concatenate([vec[:, k * width : (k + 1) * width] for k in range(3)], axis=0)
    packed = jnp.concatenate([packed, jnp.zeros((8, width), f32)], axis=0)
    send_ref[2 * half : 2 * half + 32, :] = packed.astype(bf16)


def heads_back(peer, own, wm, wt, two, gm_peer, one, dbi_a, dbi_b):
    rows, width = peer.shape[0] - 16, peer.shape[1]
    shapes = [(2 * rows + 32, 256), (2 * rows, 256), (2 * rows, width)]
    outs = [jax.ShapeDtypeStruct(v, bf16) for v in shapes] + [jax.ShapeDtypeStruct((8, width), f32)]
    return in_vmem(heads_kernel, outs, 12, "heads_back", outs="h", ins="-")(
        peer, own, wm, wt, two, gm_peer, one, dbi_a, dbi_b
    )


def input_kernel(count, dq_ref, mine_ref, *rest):
    got_ref = rest[0] if count else None
    wq_ref, wkv_ref = rest[count : count + 2]
    adds, out_ref = rest[count + 2 : -1], rest[-1]
    both = mine_ref[...]
    if count:
        both = (both.astype(f32) + got_ref[...].astype(f32)).astype(bf16)
    total = nt(dq_ref[...], wq_ref[...]) + nt(both, wkv_ref[...])
    for add in adds:
        total = total + add[...].astype(f32)
    out_ref[...] = total.astype(bf16)


def input_back(k, dq, mine, got, got_block, wq, wkv, adds):
    got = [] if got is None else [got]
    rows, width = dq.shape[0] // 4, wq.shape[0]
    out = jax.ShapeDtypeStruct((rows, width), bf16)
    return call(
        functools.partial(input_kernel, len(got)),
        ins="-",
        grid=(1,),
        in_specs=[
            pl.BlockSpec((rows, 256), lambda g: (k, 0)),
            pl.BlockSpec((rows, 384), lambda g: (k, 0)),
        ]
        + [pl.BlockSpec((rows, 384), lambda g: (got_block, 0)) for _ in got]
        + [whole_block(v) for v in [wq, wkv] + adds],
        out_specs=whole_block(out),
        out_shape=out,
        compiler_params=pltpu.CompilerParams(vmem_limit_bytes=8 * MIB),
        cost_estimate=pl.CostEstimate(flops=8 * 10**9, bytes_accessed=0, transcendentals=0),
        name="input_back",
    )(dq, mine, *got, wq, wkv, *adds)


def table_kernel(dw_ref, dwp_ref, got_ref, vec_ref, peer_ref, table):
    count = (table.shape[0] - got_ref.shape[0]) // 16
    shard = got_ref.shape[0] // count
    dwq_t, dwkv_t = dw_ref[0:192, :], dw_ref[256:640, :]
    dbv, dbq = dw_ref[640:641, 0:256], dw_ref[641:642, 0:192]
    dbv = jnp.concatenate([dbv[:, 128:256], dbv[:, 64:128]], axis=1)
    came = peer_ref[...].astype(f32)
    came = jnp.concatenate([came[8 * k : 8 * k + 8, :] for k in range(3)], axis=1)
    vectors = [vec_ref[k : k + 1, :] + came[k : k + 1, :] for k in (0, 1, 2, 4, 5, 3)]
    vectors += [vec_ref[7:8, :] + came[6:7, :], dbq, dbv]
    dwq, dwkv = dwq_t.T, dwkv_t.T
    for j in range(count):
        rows = slice(j * shard, (j + 1) * shard)
        base = j * (shard + 16)
        main = slice(base, base + shard)
        table[main, 0:192] = dwq[rows, :].astype(bf16)
        table[main, 192:576] = dwkv[rows, :].astype(bf16)
        table[main, 576:768] = (
            dwp_ref[rows, 64:256].astype(f32) + got_ref[rows, 64:256].astype(f32)
        ).astype(bf16)
        parts = []
        for vector in vectors:
            n = vector.shape[1] // count
            parts.append(
                jnp.concatenate([vector[:, j * n : (j + 1) * n], jnp.zeros((1, 768 - n), f32)], axis=1)
            )
        parts.append(jnp.zeros((16 - len(parts), 768), f32))
        table[base + shard : base + shard + 16, :] = jnp.concatenate(parts, axis=0).astype(bf16)


def table_call(count, dw, dwp, got, vec, peer):
    out = jax.ShapeDtypeStruct((got.shape[0] + 16 * count, 768), bf16)
    args = [dw, dwp, got, vec, peer]
    specs = [whole_block(v) for v in args]
    specs[4] = pl.BlockSpec((32, 256), lambda g: (peer.shape[0] // 32 - 1, 0))
    return call(
        table_kernel,
        ins="h",
        outs="h",
        grid=(1,),
        in_specs=specs,
        out_specs=whole_block(out),
        out_shape=out,
        compiler_params=pltpu.CompilerParams(vmem_limit_bytes=14 * MIB),
        cost_estimate=LIGHT,
        name="table",
    )(*args)


def products_kernel(own, x_ref, xq_ref, dq_ref, dkv_ref, dw_ref):
    step = pl.program_id(0)

    @pl.when(step == 0)
    def _():
        dw_ref[...] = jnp.zeros_like(dw_ref)

    dw_ref[256:640, :] += tn(dkv_ref[...], x_ref[...])
    dw_ref[640:641, 0:256] += jnp.sum(dkv_ref[:, 128:384].astype(f32), axis=0, keepdims=True)

    @pl.when(step < own)
    def _():
        dw_ref[0:256, :] += tn(dq_ref[...], xq_ref[...])
        dw_ref[641:642, 0:256] += jnp.sum(dq_ref[...].astype(f32), axis=0, keepdims=True)


def products_call(x, xq, dq, dkv):
    rows, own, width = dq.shape[0], 1, x.shape[1]
    out = jax.ShapeDtypeStruct((648, width), f32)
    return call(
        functools.partial(products_kernel, own),
        ins="h",
        outs="h",
        grid=(x.shape[0] // rows,),
        in_specs=[
            pl.BlockSpec((rows, width), lambda g: (g, 0)),
            pl.BlockSpec((rows, width), lambda g: (jnp.minimum(g, own - 1), 0)),
            pl.BlockSpec((rows, 256), lambda g: (jnp.minimum(g, own - 1), 0)),
            pl.BlockSpec((rows, 384), lambda g: (g, 0)),
        ],
        out_specs=whole_block(out),
        out_shape=out,
        compiler_params=pltpu.CompilerParams(vmem_limit_bytes=24 * MIB),
        cost_estimate=LIGHT,
        name="products",
    )(x, xq, dq, dkv)


def last_kernel(mine_ref, came_ref, dwq_ref, dwk_ref, dwv_ref, dwp_ref, small_ref):
    both = mine_ref[...].astype(f32) + came_ref[...].astype(f32)
    shard = dwq_ref.shape[0]
    main = both[0:shard]
    dwq_ref[...] = main[:, 0:192]
    dwk_ref[...] = main[:, 192:384]
    dwv_ref[:, 0:128] = main[:, 448:576]
    dwv_ref[:, 128:192] = main[:, 384:448]
    down = main[:, 576:768].T
    dwp_ref[0:128, :] = down[64:192, :]
    dwp_ref[128:192, :] = down[0:64, :]
    small_ref[...] = both[shard : shard + 16, :]


def last_call(mine, came):
    shard = mine.shape[0] - 16
    shapes = [(shard, 192)] * 3 + [(192, shard), (16, 768)]
    outs = [jax.ShapeDtypeStruct(v, f32) for v in shapes]
    return in_vmem(last_kernel, outs, 8, "last", outs="h", ins="-")(mine, came)


def core_swap(value):
    return lax.ppermute(value, TP, [(0, 1), (1, 0), (2, 3), (3, 2)])


def y_swap(value):
    return lax.ppermute(value, TP, [(0, 2), (2, 0), (1, 3), (3, 1)])


def x_swap(value):
    return lax.ppermute(value, CTX, [(0, 1), (1, 0)])


def after(value, *others):
    return lax.optimization_barrier((value,) + others)[0]


def rows_at(array, start, count):
    return lax.dynamic_slice_in_dim(array, start, count, axis=0)


def on_device(
    layer_in,
    cotangent,
    lengths,
    rand_blocks,
    w_query,
    b_query,
    w_key,
    w_value,
    b_value,
    w_proj,
    b_proj,
    gain_one,
    shift_one,
    w_in,
    b_in,
    w_out,
    b_out,
    gain_two,
    shift_two,
):
    tokens, width = layer_in.shape
    ctx_count = lax.axis_size(CTX)
    fsdp_count = lax.axis_size(FSDP)
    ctx = lax.axis_index(CTX)
    tp = lax.axis_index(TP)
    y, c = tp // 2, tp % 2
    seq = tokens * ctx_count
    half, quarter = tokens // 2, tokens // 4
    shard = w_query.shape[0]
    units = w_in.shape[1]
    pair = ctx_count == 2
    order = [2 * y + 1 - c, 2 * y + c, 2 * (1 - y) + 1 - c, 2 * (1 - y) + c]
    own_rows, other_rows = ctx * tokens, (1 - ctx) * tokens

    n_long = b_in.shape[0]
    vecs = [b_query, b_value, b_in, b_proj, gain_one, shift_one, b_out, gain_two, shift_two]
    piece, x_send = open_call(
        layer_in, [order[1], order[3]], quarter, w_query, w_key, w_value, w_proj, vecs
    )
    x_got = x_swap(x_send) if pair else None
    gathered = lax.all_gather(piece, FSDP, axis=0, tiled=True)
    wi_m = lax.all_gather(after(w_in, piece), FSDP, axis=0, tiled=True)
    out_both = jnp.concatenate([w_out.T, y_swap(after(w_out.T, piece))], axis=1)
    gathered = after(gathered, out_both)
    wo = lax.all_gather(after(out_both, gathered), FSDP, axis=0, tiled=True)
    wq, wkv, wp_m, vec = split_call(fsdp_count, b_query.shape[0], n_long, gathered)
    bias = vec[:, 0:192]
    wp_t = y_swap(wp_m)
    wi_t = y_swap(wi_m)

    if pair:
        x_got = after(x_got, wkv)
        q_all, kv_own = qkv(layer_in, wq, wkv, bias, True)
        x_core = core_swap(x_got)
        kv_pieces = [kv_own] + [qkv(v, wq, wkv, bias, False)[0] for v in (x_got, x_core)]
        kv_starts = [own_rows + k * quarter for k in range(4)]
        kv_starts += [other_rows + order[k] * quarter for k in (1, 3, 0, 2)]
    else:
        q_all, _ = qkv(layer_in, wq, wkv, bias, True)
        x_all = lax.all_gather(layer_in, CTX, axis=0, tiled=True)
        kv_pieces = list(qkv(x_all, wq, wkv, bias, False))
        kv_starts = [k * quarter for k in range(seq // quarter)]
    blocks = tokens // BLK
    rand = rand_blocks.reshape(-1)
    live = lengths[0]

    def meta(half_index):
        values = [half_index * (blocks // 2), ctx * blocks, live, (1 - c) * (blocks // 4)]
        values += [(8 * y + 4 * (1 - c)) * blocks // 32, 4 * (1 - c) * blocks // 32, y]
        return jnp.stack(values).astype(jnp.int32)

    as_table = lambda values: jnp.stack([jnp.asarray(v, jnp.int32) for v in values])
    chunks = seq // quarter
    starts = as_table(kv_starts)
    kv_pieces[-1] = after(kv_pieces[-1], wp_t)
    o_send, dense_o, dense_log = attend(
        meta(1 - y), rand, starts, q_all, kv_pieces, seq, half, chunks
    )
    o_got = y_swap(o_send)
    (o_keep,) = attend(
        meta(y), rand, starts, after(q_all, o_send, wi_m), kv_pieces, seq, half, chunks, dense_o
    )
    o_keep, o_got = lax.optimization_barrier((o_keep, o_got))

    slot = jnp.stack([tp, ctx * tokens + tp * quarter, live]).astype(jnp.int32)
    part_peer, part_own = project(o_keep, o_got, wp_m, wp_t)
    resid, hidden, hid_own = norm_one(slot, layer_in, part_own, core_swap(part_peer), vec)
    hid_peer = core_swap(hid_own)

    x_order = collect(after(layer_in, o_keep), order, [x_core, x_got] if pair else [])
    outs = mlp_up(hid_peer, wi_m, wi_t, vec, wp_t, None)
    act, slope, hid = mlp_up(hid_own, wi_m, wi_t, vec, wp_t, outs)
    wo = after(wo, act, x_order)
    mlp_got = core_swap(mlp_down(act, wo, False))
    part_own = mlp_down(act, wo, True)
    out_own, gm_own, grad_two, sums_two = norm_two(slot, cotangent, hidden, part_own, mlp_got, vec)
    gm_peer = core_swap(gm_own)
    out_other = y_swap(out_own)
    outs = mlp_back(gm_peer, slope, wi_m, wi_t, wo, None)
    gh_got, dbi_peer = core_swap(outs[2]), outs[3]
    gp, gm, gh_own, dbi_own = mlp_back(gm_own, slope, wi_m, wi_t, wo, outs[0:2])
    grad_one, gb_own, sums_one = norm_one_back(resid, grad_two, gh_own, gh_got, vec)
    go_send, go_keep, gb, vec_sum = heads_back(
        core_swap(gb_own), gb_own, wp_m, wp_t, sums_two, gm_peer, sums_one, dbi_peer, dbi_own
    )
    go_got = y_swap(go_send)

    def z_sum(value):
        return lax.psum_scatter(value, FSDP, scatter_dimension=0, tiled=True)

    def x_sum(value):
        value = value.astype(bf16)
        return value.astype(f32) + x_swap(value).astype(f32) if pair else lax.psum(value, CTX).astype(f32)

    dwo = z_sum(tn(gm, act).astype(bf16))
    dwi_full = tn(hid, gp).astype(bf16)
    dwi = z_sum(dwi_full)
    dwp_t = tn(gb, o_got).astype(bf16)
    dwp = tn(gb, o_keep).astype(bf16)

    if pair:
        chunk_rows = [own_rows + k * quarter for k in order] + [other_rows + k * quarter for k in order]
    else:
        chunk_rows = [k * quarter for k in range(chunks)]
    starts = as_table(kv_starts + chunk_rows)
    n_send = 2 if pair else 0
    go_keep = after(go_keep, dwp_t, dwp, dwi_full)
    carried = attend_back(
        meta(y), rand, starts, q_all, go_keep, kv_pieces, seq, chunks, n_send, tokens
    )
    go_got, dwo, out_other, *carried = lax.optimization_barrier((go_got, dwo, out_other, *carried))
    dwo_got = y_swap(dwo[:, units:])
    dwp_got = y_swap(after(dwp_t, carried[1]))
    outs = attend_back(
        meta(1 - y), rand, starts, q_all, go_got, kv_pieces, seq, chunks, n_send, tokens,
        (carried[1], carried[0]), (go_keep, go_got, dense_o, dense_log),
    )
    outs, dwo_got, dwp_got = lax.optimization_barrier((outs, dwo_got, dwp_got))
    dq, dkv = outs[0:2]
    dw = products_call(x_order if pair else x_all, x_order, dq, dkv)

    gate = dkv
    table = table_call(fsdp_count, dw, dwp, dwp_got, vec_sum, go_got)
    dwo_sum = (dwo[:, 0:units].astype(f32) + dwo_got.astype(f32)).astype(bf16)
    if pair:
        came = [x_swap(v) for v in outs[2:]]
        came[0] = after(came[0], dwi)
        gate = came[0]
        got = [came[0], came[0], came[1], came[1]]
        mine = dkv
    else:
        got = [None] * 4
        mine = collect(lax.psum_scatter(dkv, CTX, scatter_dimension=0, tiled=True), order, [])

    def back_of(k, *adds):
        return input_back(k, dq, mine, got[k], k % 2, wq, wkv, list(adds))

    sent = [core_swap(back_of(k)) for k in (0, 2)]
    lead = back_of(1, grad_one, sent[0])
    rear = back_of(3, sent[1])
    dwi = after(dwi, lead)
    dwi_sum = (dwi[:, 0:units].astype(f32) + y_swap(dwi[:, units:]).astype(f32)).astype(bf16)
    out_own, out_other = after(out_own, gate), after(out_other, gate)
    layer_out = place(
        [core_swap(out_own), out_own, core_swap(out_other), out_other],
        order,
        tokens,
    )
    both = z_sum(table)
    dwo = x_sum(dwo_sum)
    dwi = x_sum(dwi_sum)
    came_both = x_swap(both) if pair else lax.psum(both.astype(f32), CTX) - both.astype(f32)
    dwq, dwk, dwv, dwp, small = last_call(both, came_both)
    sizes = [shard] * 6 + [units // fsdp_count, 192 // fsdp_count, 192 // fsdp_count]
    db_out, dg2, ds2, dg1, ds1, db_proj, db_in, db_query, db_value = [
        small[k, 0:size] for k, size in enumerate(sizes)
    ]
    from_rear, from_lead = after(y_swap(rear), came_both), y_swap(lead)
    lead_sum = (lead.astype(f32) + from_rear.astype(f32)).astype(bf16)
    grad_input = place([core_swap(lead_sum), lead_sum], order[0:2], tokens)
    from_lead = after(from_lead, layer_out, dwi, dwo, dwq, small, grad_input)
    rear_sum = (rear.astype(f32) + from_lead.astype(f32)).astype(bf16)
    grad_input = place([core_swap(rear_sum), rear_sum], order[2:4], tokens, grad_input)
    return (
        layer_out,
        grad_input,
        dwq,
        db_query,
        dwk,
        dwv,
        db_value,
        dwp,
        db_proj,
        dg1,
        ds1,
        dwi,
        db_in,
        dwo.T,
        db_out,
        dg2,
        ds2,
    )


def solution(mesh):
    rows = P((FSDP, CTX), None)
    vector, unit = P(FSDP), P((TP, FSDP))
    column, row = P(FSDP, TP), P(TP, FSDP)
    return jax.shard_map(
        on_device,
        mesh=mesh,
        in_specs=(
            rows, rows, vector, P(FSDP, CTX, None), column, unit, column, column, unit, row,
            vector, vector, vector, column, unit, row, vector, vector, vector,
        ),
        out_specs=(
            rows, rows, column, unit, column, column, unit, row, vector, vector, vector,
            column, unit, row, vector, vector, vector,
        ),
        check_vma=False,
    )
```

```python
import functools
import math

import jax
import jax.numpy as jnp
from jax import lax
from jax.experimental import pallas as pl
from jax.experimental.pallas import tpu as pltpu
from jax.sharding import PartitionSpec as P

BLK = 64
PAIR = 2
MASKED = -1e30
CHUNK = 512
EPSILON = 1e-05
FSDP, CTX, TP = "fsdp", "ctx", "tp"
f32, bf16 = jnp.float32, jnp.bfloat16
ANY = pl.BlockSpec(memory_space=pl.ANY)


VM = pl.BlockSpec(memory_space=pltpu.VMEM)
HBM = pl.BlockSpec(memory_space=pltpu.HBM)
MIB = 1 << 20
LIGHT = pl.CostEstimate(flops=0, bytes_accessed=0, transcendentals=0)
SPACES = {"h": pltpu.HBM, "v": pltpu.VMEM}


def call(kernel, out_shape, ins="", outs="", **options):
    spec = options.get("grid_spec")
    tables = spec.num_scalar_prefetch if spec is not None else 0

    def letter(text, k):
        return text[min(k, len(text) - 1)] if text else "h"

    many = isinstance(out_shape, (list, tuple))
    shapes = list(out_shape) if many else [out_shape]
    shapes = [
        v if letter(outs, k) == "-" else SPACES[letter(outs, k)](v.shape, v.dtype)
        for k, v in enumerate(shapes)
    ]
    run = pl.pallas_call(kernel, out_shape=shapes if many else shapes[0], **options)

    def apply(*args):
        placed = [
            v if letter(ins, k) == "-" else pltpu.with_memory_space_constraint(v, SPACES[letter(ins, k)])
            for k, v in enumerate(args[tables:])
        ]
        return run(*args[0:tables], *placed)

    return apply


def nt(a, b):
    return lax.dot_general(a, b, (((1,), (1,)), ((), ())), preferred_element_type=f32)


def tn(a, b):
    return lax.dot_general(a, b, (((0,), (0,)), ((), ())), preferred_element_type=f32)


def nn(a, b):
    return jnp.dot(a, b, preferred_element_type=f32)


def place_kernel(count, slots_ref, *refs):
    rows = refs[-1].shape[0]
    parts = [(ref, at) for ref in refs[:count] for at in range(0, ref.shape[0], rows)]
    for k, (ref, at) in enumerate(parts):

        @pl.when(pl.program_id(0) == k)
        def _():
            refs[-1][...] = ref[at : at + rows, :]


def place(pieces, slots, total, earlier=None):
    count, steps = len(pieces), len(slots)
    rows, width = sum(p.shape[0] for p in pieces) // steps, pieces[0].shape[1]
    more = [] if earlier is None else [earlier]
    return call(
        functools.partial(place_kernel, count),
        ins="-",
        outs="h",
        grid_spec=pltpu.PrefetchScalarGridSpec(
            num_scalar_prefetch=1,
            grid=(steps,),
            in_specs=[whole_block(p) for p in pieces] + [ANY] * len(more),
            out_specs=pl.BlockSpec((rows, width), lambda g, s: (s[g], 0)),
        ),
        out_shape=jax.ShapeDtypeStruct((total, width), pieces[0].dtype),
        input_output_aliases={1 + count: 0} if more else {},
        compiler_params=pltpu.CompilerParams(vmem_limit_bytes=8 * MIB),
        cost_estimate=LIGHT,
        name="place",
    )(jnp.stack(slots).astype(jnp.int32), *pieces, *more)


def collect_kernel(count, slots_ref, x_ref, *refs):
    step = pl.program_id(0)

    @pl.when(step < 4)
    def _():
        refs[count][...] = x_ref[...]

    rows = x_ref.shape[0]
    parts = [(ref, at) for at in range(0, 2 * rows, rows) for ref in refs[:count]]
    for k, (ref, at) in enumerate(parts):

        @pl.when(step == 4 + k)
        def _():
            refs[count][...] = ref[at : at + rows, :]


def collect(x, slots, others):
    count = len(others)
    rows, width = x.shape[0] // 4, x.shape[1]
    steps = 4 + sum(v.shape[0] // rows for v in others)
    return call(
        functools.partial(collect_kernel, count),
        grid_spec=pltpu.PrefetchScalarGridSpec(
            num_scalar_prefetch=1,
            grid=(steps,),
            in_specs=[pl.BlockSpec((rows, width), lambda g, s: (s[jnp.minimum(g, 3)], 0))]
            + [whole_block(v) for v in others],
            out_specs=pl.BlockSpec((rows, width), lambda g, s: (g, 0)),
        ),
        out_shape=jax.ShapeDtypeStruct((steps * rows, width), x.dtype),
        compiler_params=pltpu.CompilerParams(vmem_limit_bytes=8 * MIB),
        cost_estimate=LIGHT,
        name="collect",
    )(jnp.stack(slots).astype(jnp.int32), x, *others)


def load_all(pairs, sems):
    copies = [pltpu.make_async_copy(src, dst, sems.at[k]) for k, (src, dst) in enumerate(pairs)]
    for copy in copies:
        copy.start()
    for copy in copies:
        copy.wait()


def open_kernel(count, slots_ref, x_ref, *refs):
    srcs, vecs = refs[0:4], refs[4:13]
    a_ref, half_ref, wq, wk, wv, wp, sems = refs[13:]
    size = half_ref.shape[0] // count
    pairs = []
    for k in range(count):
        start = pl.multiple_of(slots_ref[k] * size, 64)
        pairs.append((x_ref.at[pl.ds(start, size)], half_ref.at[pl.ds(k * size, size)]))
    load_all(list(zip(srcs, (wq, wk, wv, wp))) + pairs, sems)
    rows = wq.shape[0]
    a_ref[0:rows, 0:192] = wq[...]
    a_ref[0:rows, 192:384] = wk[...]
    a_ref[0:rows, 384:448] = wv[:, 128:192]
    a_ref[0:rows, 448:576] = wv[:, 0:128]
    turned_p = wp[...].T
    a_ref[0:rows, 576:640] = turned_p[:, 128:192]
    a_ref[0:rows, 640:768] = turned_p[:, 0:128]
    a_ref[rows : rows + 16, :] = jnp.zeros((16, 768), bf16)
    for k, vec in enumerate(vecs):
        n = vec.shape[0]
        a_ref[rows + k : rows + k + 1, 0:n] = vec[...].reshape(1, n)


def whole_block(value):
    zeros = (0,) * value.ndim
    return pl.BlockSpec(value.shape, lambda *_: zeros, pipeline_mode=pl.Buffered(1))


def open_call(x, slots, size, wq, wk, wv, wp, vecs):
    count = len(slots)
    rows, width = wq.shape[0], x.shape[1]
    srcs = [wq, wk, wv, wp]
    return call(
        functools.partial(open_kernel, count),
        grid_spec=pltpu.PrefetchScalarGridSpec(
            num_scalar_prefetch=1,
            grid=(1,),
            in_specs=[HBM] * 5 + [whole_block(v) for v in vecs],
            out_specs=[
                pl.BlockSpec((rows + 16, 768), lambda g, s: (0, 0)),
                pl.BlockSpec((count * size, width), lambda g, s: (0, 0)),
            ],
            scratch_shapes=[pltpu.VMEM(v.shape, bf16) for v in srcs]
            + [pltpu.SemaphoreType.DMA((4 + count,))],
        ),
        out_shape=[
            jax.ShapeDtypeStruct((rows + 16, 768), bf16),
            jax.ShapeDtypeStruct((count * size, width), bf16),
        ],
        compiler_params=pltpu.CompilerParams(vmem_limit_bytes=8 * MIB),
        cost_estimate=LIGHT,
        name="open",
    )(jnp.stack(slots).astype(jnp.int32), x, *srcs, *vecs)


def qkv_kernel(with_q, x_ref, wq_ref, wkv_ref, bias_ref, *outs):
    x = x_ref[...]
    zero = jnp.zeros((1, 64), f32)
    value_bias = bias_ref[1:2, :]
    bkv = jnp.concatenate([zero, zero, zero, value_bias[:, 128:192], value_bias[:, 0:128]], axis=1)
    outs[-1][...] = (nn(x, wkv_ref[...]) + bkv).astype(bf16)
    if with_q:
        bq = jnp.concatenate([bias_ref[0:1, :], zero], axis=1)
        outs[0][...] = (nn(x, wq_ref[...]) + bq).astype(bf16) * jnp.asarray(0.125, bf16)


def qkv(x, wq, wkv, bias, with_q):
    rows, width = x.shape
    tile = rows // 2 if rows <= 1024 else 512
    widths = [256, 384] if with_q else [384]
    return call(
        functools.partial(qkv_kernel, with_q),
        grid=(rows // tile,),
        in_specs=[pl.BlockSpec((tile, width), lambda g: (g, 0))]
        + [whole_block(v) for v in (wq, wkv, bias)],
        out_specs=[pl.BlockSpec((tile, w), lambda g: (g, 0)) for w in widths],
        out_shape=[jax.ShapeDtypeStruct((rows, w), bf16) for w in widths],
        compiler_params=pltpu.CompilerParams(vmem_limit_bytes=12 * MIB),
        cost_estimate=LIGHT,
        name="qkv",
    )(x, wq, wkv, bias)


def head_masks(places):
    group = lax.broadcasted_iota(jnp.int32, (1, 256), 1) // 64
    return [(group == place).astype(bf16) for place in places]


def spread(rows, masks):
    return jnp.concatenate([rows * m for m in masks], axis=0)


def fold(stacked, masks):
    n = stacked.shape[0] // 3
    out = stacked[0:n] * masks[0].astype(f32)
    for h in (1, 2):
        out = out + stacked[h * n : (h + 1) * n] * masks[h].astype(f32)
    return out


def tile_starts(i, b, rand_ref, seq):
    near = jnp.clip((i - 1) * BLK, 0, seq - 3 * BLK)
    near = pl.multiple_of(near, BLK)
    rand = [pl.multiple_of(rand_ref[3 * b + r] * BLK, BLK) for r in range(3)]
    return near, rand


def gather_tiles(kv, near, rand):
    parts = [kv[pl.ds(near, 3 * BLK), :]]
    parts += [kv[pl.ds(r, BLK), :] for r in rand]
    parts += [kv[0 : 2 * BLK, :]]
    return jnp.concatenate(parts, axis=0)


def tile_live(i, near, rand, length):
    out = []
    for j in range(3):
        blk = near // BLK + j
        out.append(jnp.where(jnp.abs(blk - i) <= 1, length - blk * BLK, 0))
    out += [length - r for r in rand]
    for g in range(2):
        out.append(jnp.where(jnp.abs(i - g) > 1, length - g * BLK, 0))
    return out


def load_pieces(size, starts_ref, pieces, kv, sems):
    copies = []
    for piece in pieces:
        for at in range(0, piece.shape[0], size):
            k = len(copies)
            start = pl.multiple_of(starts_ref[k], 64)
            copies.append(
                pltpu.make_async_copy(
                    piece.at[pl.ds(at, size)], kv.at[pl.ds(start, size)], sems.at[k]
                )
            )
    for copy in copies:
        copy.start()
    for copy in copies:
        copy.wait()


def step_block(meta_ref, step, steps):
    first = meta_ref[0] + PAIR * lax.rem(step + meta_ref[3] // PAIR, steps)
    return first, meta_ref[1] + first, meta_ref[2]


def turned(column):
    return jnp.broadcast_to(column, (column.shape[0], 128)).T[0:1, :]


def fwd_kernel(count, chunks, leads, meta_ref, rand_ref, starts_ref, q_ref, qd_ref, *rest):
    pieces, rest = rest[:count], rest[count:]
    if leads:
        o_ref, dense_ref, log_ref, kv, sems = rest
    else:
        dense_ref, o_ref, kv, sems = rest
    seq = kv.shape[0]
    step = pl.program_id(0) - (1 if leads else 0)
    steps = pl.num_programs(0) - (1 if leads else 0)
    first, block0, length = step_block(meta_ref, jnp.maximum(step, 0), steps)
    kmask = head_masks((0, 1, 2))
    vmask = head_masks((2, 3, 1))

    @pl.when(pl.program_id(0) == 0)
    def _():
        load_pieces(seq // chunks, starts_ref, pieces, kv, sems)

    def sparse(u):
        i = block0 + u
        near, rand = tile_starts(i, first + u, rand_ref, seq)
        tiles = gather_tiles(kv, near, rand)
        live = tile_live(i, near, rand, length)
        lane = lax.broadcasted_iota(jnp.int32, (1, BLK), 1)
        bias = jnp.concatenate([jnp.where(lane < n, 0.0, MASKED) for n in live], axis=1)
        qs = spread(q_ref[u * BLK : (u + 1) * BLK, :], kmask)
        s = nt(qs, tiles[:, 0:256]) + bias
        top = jnp.max(s, axis=1, keepdims=True)
        p = jnp.exp(s - top)
        total = jnp.sum(p, axis=1, keepdims=True)
        mixed = nn(p.astype(bf16), tiles[:, 128:384]) / total
        o_ref[u * BLK : (u + 1) * BLK, :] = fold(mixed, vmask).astype(bf16)

    def dense():
        qs = jnp.concatenate(
            [spread(qd_ref[u * BLK : (u + 1) * BLK, :], kmask) for u in range(PAIR)], axis=0
        )
        rows = qs.shape[0]
        lane = lax.broadcasted_iota(jnp.int32, (1, CHUNK), 1)

        def body(c, carry):
            top, total, mixed = carry
            start = pl.multiple_of(c * CHUNK, CHUNK)
            keys = kv[pl.ds(start, CHUNK), :]
            s = nt(qs, keys[:, 0:256]) + jnp.where(lane + start < length, 0.0, MASKED)
            new = jnp.maximum(top, jnp.max(s, axis=1, keepdims=True))
            scale = jnp.exp(top - new)
            p = jnp.exp(s - new)
            total = total * scale + jnp.sum(p, axis=1, keepdims=True)
            mixed = mixed * scale + nn(p.astype(bf16), keys[:, 128:384])
            return new, total, mixed

        init = (
            jnp.full((rows, 1), MASKED, f32),
            jnp.zeros((rows, 1), f32),
            jnp.zeros((rows, 256), f32),
        )
        top, total, mixed = lax.fori_loop(0, seq // CHUNK, body, init)
        mixed = mixed / total
        log_ref[...] = jnp.broadcast_to(turned(top + jnp.log(total)), log_ref.shape)
        half = rows // PAIR
        for u in range(PAIR):
            dense_ref[u * BLK : (u + 1) * BLK, :] = fold(
                mixed[u * half : (u + 1) * half], vmask
            ).astype(bf16)

    if leads:

        @pl.when((step < 0) & (meta_ref[1] == 0))
        def _():
            dense()

    @pl.when((step >= 0) & (block0 >= 2))
    def _():
        for u in range(PAIR):
            sparse(u)

    @pl.when((step >= 0) & (block0 < 2))
    def _():
        o_ref[...] = dense_ref[...]


def q_specs(steps, shift):
    def block(g, m, r, s):
        step = jnp.clip(g - shift, 0, steps - 1)
        return (m[0] // PAIR + lax.rem(step + m[3] // PAIR, steps), 0)

    fixed = pl.BlockSpec((PAIR * BLK, 256), lambda g, m, r, s: (0, 0))
    return [pl.BlockSpec((PAIR * BLK, 256), block), fixed]


def attend(meta, rand, starts, q, pieces, seq, rows, chunks, dense=None):
    steps = rows // (PAIR * BLK)
    count = len(pieces)
    leads = dense is None
    fixed = pl.BlockSpec((PAIR * BLK, 256), lambda g, m, r, s: (0, 0))
    out_specs = [
        pl.BlockSpec((PAIR * BLK, 256), lambda g, m, r, s: (jnp.maximum(g - (1 if leads else 0), 0), 0))
    ]
    out_shape = [jax.ShapeDtypeStruct((rows, 256), bf16)]
    if leads:
        out_specs += [fixed, pl.BlockSpec((8, 3 * PAIR * BLK), lambda g, m, r, s: (0, 0))]
        out_shape += [
            jax.ShapeDtypeStruct((PAIR * BLK, 256), bf16),
            jax.ShapeDtypeStruct((8, 3 * PAIR * BLK), f32),
        ]
    return call(
        functools.partial(fwd_kernel, count, chunks, leads),
        grid_spec=pltpu.PrefetchScalarGridSpec(
            num_scalar_prefetch=3,
            grid=(steps + (1 if leads else 0),),
            in_specs=q_specs(steps, 1 if leads else 0) + [ANY] * count + ([] if leads else [fixed]),
            out_specs=out_specs,
            scratch_shapes=[pltpu.VMEM((seq, 384), bf16), pltpu.SemaphoreType.DMA((chunks,))],
        ),
        out_shape=out_shape,
        compiler_params=pltpu.CompilerParams(vmem_limit_bytes=seq * 768 + 6 * MIB),
        cost_estimate=LIGHT,
        name="attend",
    )(meta, rand, starts, q, q, *pieces, *([] if leads else [dense]))


def bwd_kernel(count, last, chunks, n_send, meta_ref, rand_ref, starts_ref, q_ref, qd_ref, do_ref, *rest):
    pieces, rest = rest[:count], rest[count:]
    if last:
        in_ref, _, own_ref, came_ref, od_ref, log_ref, dq_ref, all_ref = rest[:8]
        sends, (kv, acc, sems) = rest[8 : 8 + n_send], rest[-3:]
    else:
        dq_ref, out_ref, kv, acc, sems = rest
    seq = kv.shape[0]
    step = pl.program_id(0)
    steps = pl.num_programs(0) - (1 if last else 0)
    first, block0, length = step_block(meta_ref, jnp.minimum(step, steps - 1), steps)
    kmask = head_masks((0, 1, 2))
    vmask = head_masks((2, 3, 1))

    @pl.when(step == 0)
    def _():
        if last:
            carry = pltpu.make_async_copy(in_ref, acc, sems.at[chunks])
            carry.start()
        else:
            acc[...] = jnp.zeros_like(acc)
        load_pieces(seq // chunks, starts_ref, pieces, kv, sems)
        if last:
            carry.wait()

    def add_rows(start, n, wk, wv):
        rows = pl.ds(start, n)
        acc[rows, 0:128] += wk[:, 0:128]
        acc[rows, 128:256] += wk[:, 128:256] + wv[:, 0:128]
        acc[rows, 256:384] += wv[:, 128:256]

    def sparse(u):
        i = block0 + u
        near, rand = tile_starts(i, first + u, rand_ref, seq)
        tiles = gather_tiles(kv, near, rand)
        live = tile_live(i, near, rand, length)
        row = lax.broadcasted_iota(jnp.int32, (BLK, 192), 0)
        qs = spread(q_ref[u * BLK : (u + 1) * BLK, :], kmask)
        gs = spread(do_ref[u * BLK : (u + 1) * BLK, :], vmask)
        s = nt(tiles[:, 0:256], qs)
        s = jnp.concatenate(
            [jnp.where(row < live[j], s[j * BLK : (j + 1) * BLK], MASKED) for j in range(8)],
            axis=0,
        )
        top = jnp.max(s, axis=0, keepdims=True)
        p = jnp.exp(s - top)
        p = p * (1.0 / jnp.sum(p, axis=0, keepdims=True))
        dp = nt(tiles[:, 128:384], gs)
        inner = jnp.sum(p * dp, axis=0, keepdims=True)
        ds = (p * (dp - inner)).astype(bf16)
        wk = nn(ds, qs)
        wv = nn(p.astype(bf16), gs)
        add_rows(near, 192, wk[0:192], wv[0:192])
        for r in range(3):
            a = 192 + r * BLK
            add_rows(rand[r], BLK, wk[a : a + BLK], wv[a : a + BLK])
        add_rows(0, 128, wk[384:512], wv[384:512])
        dq = fold(tn(ds, tiles[:, 0:256]), kmask) * 0.125
        dq_ref[u * BLK : (u + 1) * BLK, :] = dq.astype(bf16)

    def dense():
        rows_g = jnp.where(meta_ref[6] == 0, own_ref[...].astype(f32), came_ref[...].astype(f32))
        qs, gs, inner = [], [], []
        for u in range(PAIR):
            rows = slice(u * BLK, (u + 1) * BLK)
            qs.append(spread(qd_ref[rows, :], kmask))
            gs.append(spread(rows_g[rows, :].astype(bf16), vmask))
            for m in vmask:
                part = rows_g[rows, :] * od_ref[rows, :].astype(f32) * m.astype(f32)
                inner.append(jnp.sum(part, axis=1, keepdims=True))
        qs, gs = jnp.concatenate(qs, axis=0), jnp.concatenate(gs, axis=0)
        inner = turned(jnp.concatenate(inner, axis=0))
        log_sum = log_ref[0:1, :]
        cols = qs.shape[0]
        row = lax.broadcasted_iota(jnp.int32, (CHUNK, cols), 0)

        def back(c, dq):
            start = pl.multiple_of(c * CHUNK, CHUNK)
            keys = kv[pl.ds(start, CHUNK), :]
            s = jnp.where(row < length - start, nt(keys[:, 0:256], qs), MASKED)
            p = jnp.exp(s - log_sum)
            ds = (p * (nt(keys[:, 128:384], gs) - inner)).astype(bf16)
            add_rows(start, CHUNK, nn(ds, qs), nn(p.astype(bf16), gs))
            return dq + tn(ds, keys[:, 0:256])

        dq = lax.fori_loop(0, seq // CHUNK, back, jnp.zeros((cols, 256), f32))
        half = cols // PAIR
        for u in range(PAIR):
            dq_ref[u * BLK : (u + 1) * BLK, :] = (
                fold(dq[u * half : (u + 1) * half], kmask) * 0.125
            ).astype(bf16)

    @pl.when((step < steps) & (block0 >= 2))
    def _():
        for u in range(PAIR):
            sparse(u)

    if last:

        @pl.when((step == steps) & (meta_ref[1] == 0))
        def _():
            dense()

    @pl.when(pl.program_id(0) == pl.num_programs(0) - 1)
    def _():
        if not last:
            pltpu.sync_copy(acc, out_ref)
        else:
            size = seq // chunks

            def emit(k):
                start = pl.multiple_of(starts_ref[chunks + k], 64)
                return acc[pl.ds(start, size), :].astype(bf16)

            for k in range(chunks):
                piece = emit(k)
                all_ref[k * size : (k + 1) * size, :] = piece
                if n_send and k >= chunks - 4:
                    j = k - chunks + 4
                    dst, at = sends[j // 2], j % 2
                    dst[at * size : (at + 1) * size, :] = piece


def attend_back(meta, rand, starts, q, grad, pieces, seq, chunks, n_send, tokens, carried=None, dense=None):
    rows = tokens // 2
    steps = rows // (PAIR * BLK)
    count = len(pieces)
    last = carried is not None
    shape = (PAIR * BLK, 256)
    more = []
    if last:

        def dq_block(g, m, r, s):
            return (jnp.where((g == steps) & (m[1] == 0), m[4], jnp.minimum(g, steps - 1) + steps), 0)

        chosen = pl.BlockSpec(shape, lambda g, m, r, s: (m[5], 0))
        more = [
            chosen,
            chosen,
            pl.BlockSpec(shape, lambda g, m, r, s: (0, 0)),
            pl.BlockSpec((8, 3 * PAIR * BLK), lambda g, m, r, s: (0, 0)),
        ]
    else:
        dq_block = lambda g, m, r, s: (g, 0)
    out_specs = [pl.BlockSpec(shape, dq_block)]
    out_shape = [jax.ShapeDtypeStruct((tokens, 256), bf16)]
    if last:
        sizes = [seq] + [2 * seq // chunks] * n_send
        outs = [(n, 384, bf16) for n in sizes]
        out_specs += [
            pl.BlockSpec((n, w), lambda g, m, r, s: (0, 0), pipeline_mode=pl.Buffered(1)) for n, w, _ in outs
        ]
        out_shape += [jax.ShapeDtypeStruct((n, w), t) for n, w, t in outs]
    else:
        out_specs += [ANY]
        out_shape += [jax.ShapeDtypeStruct((seq, 384), f32)]
    grad_spec = pl.BlockSpec(shape, lambda g, m, r, s: (jnp.minimum(g, steps - 1), 0))
    return call(
        functools.partial(bwd_kernel, count, last, chunks, n_send),
        grid_spec=pltpu.PrefetchScalarGridSpec(
            num_scalar_prefetch=3,
            grid=(steps + (1 if last else 0),),
            in_specs=q_specs(steps, 0) + [grad_spec] + [ANY] * (count + (2 if last else 0)) + more,
            out_specs=out_specs,
            scratch_shapes=[
                pltpu.VMEM((seq, 384), bf16),
                pltpu.VMEM((seq, 384), f32),
                pltpu.SemaphoreType.DMA((chunks + 1,)),
            ],
        ),
        out_shape=out_shape,
        input_output_aliases={3 + 3 + count + 1: 0} if last else {},
        compiler_params=pltpu.CompilerParams(
            vmem_limit_bytes=seq * (3840 if last else 2304) + 7 * MIB
        ),
        cost_estimate=LIGHT,
        name="attend_back",
    )(meta, rand, starts, q, q, grad, *pieces, *(carried or ()), *(dense or ()))


def split_kernel(count, short, long, a_ref, wq_ref, wkv_ref, ship_ref, vec_ref):
    step = a_ref.shape[0] // count
    rows = step - 16
    parts = []
    for k in range(count):
        there, here = slice(k * step, k * step + rows), slice(k * rows, (k + 1) * rows)
        zero = jnp.zeros((rows, 64), bf16)
        wq_ref[here, 0:192] = a_ref[there, 0:192]
        wq_ref[here, 192:256] = zero
        wkv_ref[here, :] = a_ref[there, 192:576]
        ship_ref[here, 0:64] = zero
        ship_ref[here, 64:256] = a_ref[there, 576:768]
        parts.append(a_ref[k * step + rows : (k + 1) * step, :].astype(f32))
    width = vec_ref.shape[1]
    attn = jnp.concatenate([p[:, 0:short] for p in parts], axis=1)
    attn = jnp.concatenate([attn, jnp.zeros((16, width - attn.shape[1]), f32)], axis=1)
    dense = jnp.concatenate([p[:, 0:long] for p in parts], axis=1)
    vec = jnp.concatenate([attn[0:2], dense[2:16]], axis=0)
    vec_ref[...] = vec
    ship = jnp.concatenate([vec[2:3, k * 256 : (k + 1) * 256] for k in range(3)], axis=0)
    ship = jnp.concatenate([ship, jnp.zeros((13, 256), f32)], axis=0)
    ship_ref[count * rows : count * rows + 16, :] = ship.astype(bf16)


def split_call(count, short, long, gathered):
    rows = gathered.shape[0] - 16 * count
    outs = [
        jax.ShapeDtypeStruct((rows, 256), bf16),
        jax.ShapeDtypeStruct((rows, 384), bf16),
        jax.ShapeDtypeStruct((rows + 16, 256), bf16),
        jax.ShapeDtypeStruct((16, count * long), f32),
    ]
    return call(
        functools.partial(split_kernel, count, short, long),
        outs="-",
        grid=(1,),
        in_specs=[whole_block(gathered)],
        out_specs=[whole_block(v) for v in outs],
        out_shape=outs,
        compiler_params=pltpu.CompilerParams(vmem_limit_bytes=10 * MIB),
        cost_estimate=LIGHT,
        name="split",
    )(gathered)


TILE = 256


def proj_kernel(keep_ref, got_ref, wm_ref, wt_ref, peer_ref, own_ref):
    half, width = peer_ref.shape
    for k, out in enumerate((peer_ref, own_ref)):
        rows = slice(k * half, (k + 1) * half)
        value = nt(keep_ref[rows, :], wm_ref[0:width, :]) + nt(got_ref[rows, :], wt_ref[0:width, :])
        out[...] = value.astype(out.dtype)


def in_vmem(kernel, out_shape, limit, name, aliases=None, outs="v", ins="v"):
    def pick(text, values):
        return [VM if text[min(k, len(text) - 1)] == "v" else whole_block(v) for k, v in enumerate(values)]

    return lambda *args: call(
        kernel,
        ins=ins,
        outs=outs,
        grid=(1,),
        in_specs=pick(ins, args),
        out_specs=pick(outs, out_shape),
        out_shape=out_shape,
        input_output_aliases=aliases or {},
        compiler_params=pltpu.CompilerParams(vmem_limit_bytes=limit * MIB),
        cost_estimate=LIGHT,
        name=name,
    )(*args)


def project(keep, got, wm, wt):
    rows, width = keep.shape[0] // 2, wm.shape[0] - 16
    outs = [jax.ShapeDtypeStruct((rows, width), bf16)] * 2
    return in_vmem(proj_kernel, outs, 10, "project", outs="h", ins="-")(keep, got, wm, wt)


def stats(value):
    center = jnp.mean(value, axis=-1, keepdims=True)
    offset = value - center
    inverse = lax.rsqrt(jnp.mean(offset * offset, axis=-1, keepdims=True) + EPSILON)
    return offset * inverse, inverse


def fetch_two(slot_ref, src, dst, came, got, sems):
    start = pl.multiple_of(slot_ref[0] * dst.shape[0], 64)
    load_all([(src.at[pl.ds(start, dst.shape[0])], dst), (came, got)], sems)


def norm_one_kernel(
    slot_ref, x_ref, came_ref, part_ref, vec_ref, resid_ref, hidden_ref, low_ref, rows_ref, got_ref, sems
):
    fetch_two(slot_ref, x_ref, rows_ref, came_ref, got_ref, sems)
    for k in range(0, part_ref.shape[0], TILE):
        rows = slice(k, k + TILE)
        resid = rows_ref[rows, :].astype(f32) + (
            part_ref[rows, :].astype(f32) + got_ref[rows, :].astype(f32) + vec_ref[3:4, :]
        )
        resid_ref[rows, :] = resid
        normed, _ = stats(resid)
        hidden = normed * vec_ref[4:5, :] + vec_ref[5:6, :]
        hidden_ref[rows, :] = hidden
        low_ref[rows, :] = hidden.astype(bf16)


def norm_one(slot, x, part, got, vec):
    rows, width = part.shape
    return call(
        norm_one_kernel,
        ins="h-",
        outs="h",
        grid_spec=pltpu.PrefetchScalarGridSpec(
            num_scalar_prefetch=1,
            grid=(1,),
            in_specs=[HBM, ANY] + [whole_block(v) for v in (part, vec)],
            out_specs=[pl.BlockSpec((rows, width), lambda g, s: (0, 0))] * 3,
            scratch_shapes=[pltpu.VMEM((rows, width), bf16)] * 2 + [pltpu.SemaphoreType.DMA((2,))],
        ),
        out_shape=[jax.ShapeDtypeStruct((rows, width), t) for t in (f32, f32, bf16)],
        compiler_params=pltpu.CompilerParams(vmem_limit_bytes=14 * MIB),
        cost_estimate=LIGHT,
        name="norm_one",
    )(slot, x, got, part, vec)


def add_sums(total, low, error, normed):
    sums = [jnp.sum(v, axis=0, keepdims=True) for v in (low.astype(f32), error * normed, error)]
    return sums if total is None else [x + z for x, z in zip(total, sums)]


def ride(low_ref, sums_ref, total):
    sums = jnp.concatenate(total + [jnp.zeros((5, low_ref.shape[1]), f32)], axis=0)
    sums_ref[...] = sums
    rows = low_ref.shape[0] - 16
    low_ref[rows : rows + 16, :] = jnp.concatenate([sums, jnp.zeros_like(sums)], axis=0).astype(bf16)


def norm_two_kernel(
    slot_ref, cot_ref, came_ref, hidden_ref, part_ref, vec_ref,
    out_ref, low_ref, grad_ref, sums_ref, rows_ref, got_ref, sems,
):
    fetch_two(slot_ref, cot_ref, rows_ref, came_ref, got_ref, sems)
    gain = vec_ref[7:8, :]
    total = None
    for k in range(0, part_ref.shape[0], TILE):
        rows = slice(k, k + TILE)
        value = hidden_ref[rows, :] + (part_ref[rows, :].astype(f32) + got_ref[rows, :].astype(f32)) + vec_ref[6:7, :]
        normed, inverse = stats(value)
        position = slot_ref[1] + k + lax.broadcasted_iota(jnp.int32, (TILE, 1), 0)
        live = (position < slot_ref[2]).astype(f32)
        out_ref[rows, :] = ((normed * gain + vec_ref[8:9, :]) * live).astype(bf16)
        error = rows_ref[rows, :].astype(f32) * live
        inner = error * gain
        first = jnp.mean(inner, axis=-1, keepdims=True)
        second = jnp.mean(inner * normed, axis=-1, keepdims=True)
        grad = inverse * (inner - first - normed * second)
        grad_ref[rows, :] = grad
        low = grad.astype(bf16)
        low_ref[rows, :] = low
        total = add_sums(total, low, error, normed)
    ride(low_ref, sums_ref, total)


def norm_two(slot, cotangent, hidden, part, got, vec):
    rows, width = part.shape
    return call(
        norm_two_kernel,
        ins="h-",
        outs="h",
        grid_spec=pltpu.PrefetchScalarGridSpec(
            num_scalar_prefetch=1,
            grid=(1,),
            in_specs=[HBM, ANY] + [whole_block(v) for v in (hidden, part, vec)],
            out_specs=[
                pl.BlockSpec((n, width), lambda g, s: (0, 0)) for n in (rows, rows + 16, rows, 8)
            ],
            scratch_shapes=[pltpu.VMEM((rows, width), bf16)] * 2 + [pltpu.SemaphoreType.DMA((2,))],
        ),
        out_shape=[
            jax.ShapeDtypeStruct((rows, width), bf16),
            jax.ShapeDtypeStruct((rows + 16, width), bf16),
            jax.ShapeDtypeStruct((rows, width), f32),
            jax.ShapeDtypeStruct((8, width), f32),
        ],
        compiler_params=pltpu.CompilerParams(vmem_limit_bytes=14 * MIB),
        cost_estimate=LIGHT,
        name="norm_two",
    )(slot, cotangent, got, hidden, part, vec)


def norm_one_back_kernel(resid_ref, two_ref, part_ref, got_ref, vec_ref, grad_ref, low_ref, sums_ref):
    total = None
    for k in range(0, part_ref.shape[0], TILE):
        rows = slice(k, k + TILE)
        normed, inverse = stats(resid_ref[rows, :])
        error = two_ref[rows, :] + (part_ref[rows, :].astype(f32) + got_ref[rows, :].astype(f32))
        inner = error * vec_ref[4:5, :]
        first = jnp.mean(inner, axis=-1, keepdims=True)
        second = jnp.mean(inner * normed, axis=-1, keepdims=True)
        grad = inverse * (inner - first - normed * second)
        grad_ref[rows, :] = grad
        low = grad.astype(bf16)
        low_ref[rows, :] = low
        total = add_sums(total, low, error, normed)
    ride(low_ref, sums_ref, total)


def norm_one_back(resid, two, part, got, vec):
    rows, width = part.shape
    outs = [
        jax.ShapeDtypeStruct((rows, width), f32),
        jax.ShapeDtypeStruct((rows + 16, width), bf16),
        jax.ShapeDtypeStruct((8, width), f32),
    ]
    return in_vmem(norm_one_back_kernel, outs, 14, "norm_one_back", outs="h", ins="-")(resid, two, part, got, vec)


ERFC = (
    -1.26551223, 1.00002368, 0.37409196, 0.09678418, -0.18628806,
    0.27886807, -1.13520398, 1.48851587, -0.82215223, 0.17087277,
)


def gelu_pair(pre):
    z = jnp.abs(pre) * math.sqrt(0.5)
    t = 1.0 / (1.0 + 0.5 * z)
    poly = jnp.full_like(t, ERFC[-1])
    for coefficient in ERFC[-2::-1]:
        poly = poly * t + coefficient
    square = -z * z
    tail = 0.5 * t * jnp.exp(square + poly)
    cdf = jnp.where(pre < 0, tail, 1.0 - tail)
    density = jnp.exp(square) * (1.0 / math.sqrt(2.0 * math.pi))
    return (pre * cdf).astype(bf16), (cdf + pre * density).astype(bf16)


def up_kernel(base, hid_ref, wim_ref, wit_ref, vec_ref, ship_ref, *rest):
    act_ref, slope_ref, all_ref = rest[-3:]
    units, at = wim_ref.shape[1], ship_ref.shape[0] - 16
    shipped = ship_ref[at : at + 16, :].astype(f32)
    shipped = jnp.concatenate([shipped[k : k + 1, :] for k in range(3)], axis=1)
    for k in range(0, hid_ref.shape[0], TILE):
        rows, there = slice(k, k + TILE), slice(base + k, base + k + TILE)
        hid = hid_ref[rows, :]
        all_ref[there, :] = hid
        for j, (wi, b) in enumerate(((wim_ref, vec_ref[2:3, :]), (wit_ref, shipped))):
            act, slope = gelu_pair(nn(hid, wi[...]) + b)
            act_ref[there, j * units : (j + 1) * units] = act
            slope_ref[there, j * units : (j + 1) * units] = slope


def mlp_up(hid, wi_m, wi_t, vec, ship, earlier):
    rows, width = hid.shape
    units = wi_m.shape[1]
    big = jax.ShapeDtypeStruct((2 * rows, 2 * units), bf16)
    outs = [big, big, jax.ShapeDtypeStruct((2 * rows, width), bf16)]
    second = earlier is not None
    kernel = functools.partial(up_kernel, rows if second else 0)
    aliases = {5 + k: k for k in range(3)} if second else {}
    args = (hid, wi_m, wi_t, vec, ship) + (tuple(earlier) if second else ())
    return in_vmem(kernel, outs, 16, "mlp_up", aliases, ins="-----v")(*args)


def down_kernel(base, act_ref, wo_ref, part_ref):
    for k in range(0, part_ref.shape[0], TILE):
        there = slice(base + k, base + k + TILE)
        part_ref[k : k + TILE, :] = nt(act_ref[there, :], wo_ref[...]).astype(bf16)


def mlp_down(act, wo, second):
    rows = act.shape[0] // 2
    kernel = functools.partial(down_kernel, rows if second else 0)
    outs = [jax.ShapeDtypeStruct((rows, wo.shape[0]), bf16)]
    return in_vmem(kernel, outs, 10, "mlp_down", outs="h", ins="v-")(act, wo)[0]


def mlp_back_kernel(base, gm_ref, slope_ref, wim_ref, wit_ref, wo_ref, *rest):
    gp_ref, all_ref, part_ref, sums_ref = rest[-4:]
    units = wim_ref.shape[1]
    sums = [None, None]
    for k in range(0, part_ref.shape[0], TILE):
        rows, there = slice(k, k + TILE), slice(base + k, base + k + TILE)
        gm = gm_ref[rows, :]
        all_ref[there, :] = gm
        total = None
        for j, wi in enumerate((wim_ref, wit_ref)):
            cols = slice(j * units, (j + 1) * units)
            gp = (nn(gm, wo_ref[:, cols]) * slope_ref[there, cols].astype(f32)).astype(bf16)
            gp_ref[there, cols] = gp
            column = jnp.sum(gp.astype(f32), axis=0, keepdims=True)
            sums[j] = column if sums[j] is None else sums[j] + column
            value = nt(gp, wi[...])
            total = value if total is None else total + value
        part_ref[rows, :] = total.astype(bf16)
    sums_ref[...] = jnp.concatenate(sums + [jnp.zeros((6, units), f32)], axis=0)


def mlp_back(gm, slope, wi_m, wi_t, wo, earlier):
    rows, width = gm.shape[0] - 16, gm.shape[1]
    units = wi_m.shape[1]
    outs = [
        jax.ShapeDtypeStruct((2 * rows, 2 * units), bf16),
        jax.ShapeDtypeStruct((2 * rows, width), bf16),
        jax.ShapeDtypeStruct((rows, width), bf16),
        jax.ShapeDtypeStruct((8, units), f32),
    ]
    second = earlier is not None
    kernel = functools.partial(mlp_back_kernel, rows if second else 0)
    aliases = {5 + k: k for k in range(2)} if second else {}
    args = (gm, slope, wi_m, wi_t, wo) + (tuple(earlier) if second else ())
    return in_vmem(kernel, outs, 20, "mlp_back", aliases, outs="vvhh", ins="-v---v")(*args)


def heads_kernel(
    peer_ref, own_ref, wm_ref, wt_ref, two_ref, twop_ref, one_ref, dbi_a_ref, dbi_b_ref,
    send_ref, keep_ref, both_ref, vec_ref,
):
    half = peer_ref.shape[0] - 16
    for k, ref in enumerate((peer_ref, own_ref)):
        rows = slice(k * half, (k + 1) * half)
        grad = ref[0:half, :]
        both_ref[rows, :] = grad
        send_ref[rows, :] = nn(grad, wt_ref[0 : grad.shape[1], :]).astype(bf16)
        keep_ref[rows, :] = nn(grad, wm_ref[0 : grad.shape[1], :]).astype(bf16)
    two = two_ref[...] + twop_ref[half : half + 16, :].astype(f32)[0:8]
    one = one_ref[...] + peer_ref[half : half + 16, :].astype(f32)[0:8]
    dbi = dbi_a_ref[...] + dbi_b_ref[...]
    vec = jnp.concatenate([two[0:3], one[0:3], dbi[1:2], dbi[0:1]], axis=0)
    vec_ref[...] = vec
    width = vec.shape[1] // 3
    packed = jnp.concatenate([vec[:, k * width : (k + 1) * width] for k in range(3)], axis=0)
    packed = jnp.concatenate([packed, jnp.zeros((8, width), f32)], axis=0)
    send_ref[2 * half : 2 * half + 32, :] = packed.astype(bf16)


def heads_back(peer, own, wm, wt, two, gm_peer, one, dbi_a, dbi_b):
    rows, width = peer.shape[0] - 16, peer.shape[1]
    shapes = [(2 * rows + 32, 256), (2 * rows, 256), (2 * rows, width)]
    outs = [jax.ShapeDtypeStruct(v, bf16) for v in shapes] + [jax.ShapeDtypeStruct((8, width), f32)]
    return in_vmem(heads_kernel, outs, 12, "heads_back", outs="h", ins="-")(
        peer, own, wm, wt, two, gm_peer, one, dbi_a, dbi_b
    )


def input_kernel(count, dq_ref, mine_ref, *rest):
    got_ref = rest[0] if count else None
    wq_ref, wkv_ref = rest[count : count + 2]
    adds, out_ref = rest[count + 2 : -1], rest[-1]
    both = mine_ref[...]
    if count:
        both = (both.astype(f32) + got_ref[...].astype(f32)).astype(bf16)
    total = nt(dq_ref[...], wq_ref[...]) + nt(both, wkv_ref[...])
    for add in adds:
        total = total + add[...].astype(f32)
    out_ref[...] = total.astype(bf16)


def input_back(k, dq, mine, got, got_block, wq, wkv, adds):
    got = [] if got is None else [got]
    rows, width = dq.shape[0] // 4, wq.shape[0]
    out = jax.ShapeDtypeStruct((rows, width), bf16)
    return call(
        functools.partial(input_kernel, len(got)),
        ins="hh" + "-" * len(got) + "hh-",
        grid=(1,),
        in_specs=[
            pl.BlockSpec((rows, 256), lambda g: (k, 0)),
            pl.BlockSpec((rows, 384), lambda g: (k, 0)),
        ]
        + [pl.BlockSpec((rows, 384), lambda g: (got_block, 0)) for _ in got]
        + [whole_block(v) for v in [wq, wkv] + adds],
        out_specs=whole_block(out),
        out_shape=out,
        compiler_params=pltpu.CompilerParams(vmem_limit_bytes=8 * MIB),
        cost_estimate=pl.CostEstimate(flops=8 * 10**9, bytes_accessed=0, transcendentals=0),
        name="input_back",
    )(dq, mine, *got, wq, wkv, *adds)


def table_kernel(dw_ref, dwp_ref, got_ref, vec_ref, peer_ref, table):
    count = (table.shape[0] - got_ref.shape[0]) // 16
    shard = got_ref.shape[0] // count
    dwq_t, dwkv_t = dw_ref[0:192, :], dw_ref[256:640, :]
    dbv, dbq = dw_ref[640:641, 0:256], dw_ref[641:642, 0:192]
    dbv = jnp.concatenate([dbv[:, 128:256], dbv[:, 64:128]], axis=1)
    came = peer_ref[...].astype(f32)
    came = jnp.concatenate([came[8 * k : 8 * k + 8, :] for k in range(3)], axis=1)
    vectors = [vec_ref[k : k + 1, :] + came[k : k + 1, :] for k in (0, 1, 2, 4, 5, 3)]
    vectors += [vec_ref[7:8, :] + came[6:7, :], dbq, dbv]
    dwq, dwkv = dwq_t.T, dwkv_t.T
    for j in range(count):
        rows = slice(j * shard, (j + 1) * shard)
        base = j * (shard + 16)
        main = slice(base, base + shard)
        table[main, 0:192] = dwq[rows, :].astype(bf16)
        table[main, 192:576] = dwkv[rows, :].astype(bf16)
        table[main, 576:768] = (
            dwp_ref[rows, 64:256].astype(f32) + got_ref[rows, 64:256].astype(f32)
        ).astype(bf16)
        parts = []
        for vector in vectors:
            n = vector.shape[1] // count
            parts.append(
                jnp.concatenate([vector[:, j * n : (j + 1) * n], jnp.zeros((1, 768 - n), f32)], axis=1)
            )
        parts.append(jnp.zeros((16 - len(parts), 768), f32))
        table[base + shard : base + shard + 16, :] = jnp.concatenate(parts, axis=0).astype(bf16)


def table_call(count, dw, dwp, got, vec, peer):
    out = jax.ShapeDtypeStruct((got.shape[0] + 16 * count, 768), bf16)
    args = [dw, dwp, got, vec, peer]
    specs = [whole_block(v) for v in args]
    specs[4] = pl.BlockSpec((32, 256), lambda g: (peer.shape[0] // 32 - 1, 0))
    return call(
        table_kernel,
        ins="h",
        outs="h",
        grid=(1,),
        in_specs=specs,
        out_specs=whole_block(out),
        out_shape=out,
        compiler_params=pltpu.CompilerParams(vmem_limit_bytes=14 * MIB),
        cost_estimate=LIGHT,
        name="table",
    )(*args)


def products_kernel(own, x_ref, xq_ref, dq_ref, dkv_ref, dw_ref):
    step = pl.program_id(0)

    @pl.when(step == 0)
    def _():
        dw_ref[...] = jnp.zeros_like(dw_ref)

    dw_ref[256:640, :] += tn(dkv_ref[...], x_ref[...])
    dw_ref[640:641, 0:256] += jnp.sum(dkv_ref[:, 128:384].astype(f32), axis=0, keepdims=True)

    @pl.when(step < own)
    def _():
        dw_ref[0:256, :] += tn(dq_ref[...], xq_ref[...])
        dw_ref[641:642, 0:256] += jnp.sum(dq_ref[...].astype(f32), axis=0, keepdims=True)


def products_call(x, xq, dq, dkv):
    rows, own, width = dq.shape[0], 1, x.shape[1]
    out = jax.ShapeDtypeStruct((648, width), f32)
    return call(
        functools.partial(products_kernel, own),
        ins="h",
        outs="h",
        grid=(x.shape[0] // rows,),
        in_specs=[
            pl.BlockSpec((rows, width), lambda g: (g, 0)),
            pl.BlockSpec((rows, width), lambda g: (jnp.minimum(g, own - 1), 0)),
            pl.BlockSpec((rows, 256), lambda g: (jnp.minimum(g, own - 1), 0)),
            pl.BlockSpec((rows, 384), lambda g: (g, 0)),
        ],
        out_specs=whole_block(out),
        out_shape=out,
        compiler_params=pltpu.CompilerParams(vmem_limit_bytes=24 * MIB),
        cost_estimate=LIGHT,
        name="products",
    )(x, xq, dq, dkv)


def last_kernel(mine_ref, came_ref, dwq_ref, dwk_ref, dwv_ref, dwp_ref, small_ref):
    both = mine_ref[...].astype(f32) + came_ref[...].astype(f32)
    shard = dwq_ref.shape[0]
    main = both[0:shard]
    dwq_ref[...] = main[:, 0:192]
    dwk_ref[...] = main[:, 192:384]
    dwv_ref[:, 0:128] = main[:, 448:576]
    dwv_ref[:, 128:192] = main[:, 384:448]
    down = main[:, 576:768].T
    dwp_ref[0:128, :] = down[64:192, :]
    dwp_ref[128:192, :] = down[0:64, :]
    small_ref[...] = both[shard : shard + 16, :]


def last_call(mine, came):
    shard = mine.shape[0] - 16
    shapes = [(shard, 192)] * 3 + [(192, shard), (16, 768)]
    outs = [jax.ShapeDtypeStruct(v, f32) for v in shapes]
    return in_vmem(last_kernel, outs, 8, "last", outs="h", ins="-")(mine, came)


def core_swap(value):
    return lax.ppermute(value, TP, [(0, 1), (1, 0), (2, 3), (3, 2)])


def y_swap(value):
    return lax.ppermute(value, TP, [(0, 2), (2, 0), (1, 3), (3, 1)])


def x_swap(value):
    return lax.ppermute(value, CTX, [(0, 1), (1, 0)])


def after(value, *others):
    return lax.optimization_barrier((value,) + others)[0]


def rows_at(array, start, count):
    return lax.dynamic_slice_in_dim(array, start, count, axis=0)


def on_device(
    layer_in,
    cotangent,
    lengths,
    rand_blocks,
    w_query,
    b_query,
    w_key,
    w_value,
    b_value,
    w_proj,
    b_proj,
    gain_one,
    shift_one,
    w_in,
    b_in,
    w_out,
    b_out,
    gain_two,
    shift_two,
):
    tokens, width = layer_in.shape
    ctx_count = lax.axis_size(CTX)
    fsdp_count = lax.axis_size(FSDP)
    ctx = lax.axis_index(CTX)
    tp = lax.axis_index(TP)
    y, c = tp // 2, tp % 2
    seq = tokens * ctx_count
    half, quarter = tokens // 2, tokens // 4
    shard = w_query.shape[0]
    units = w_in.shape[1]
    pair = ctx_count == 2
    order = [2 * y + 1 - c, 2 * y + c, 2 * (1 - y) + 1 - c, 2 * (1 - y) + c]
    own_rows, other_rows = ctx * tokens, (1 - ctx) * tokens

    n_long = b_in.shape[0]
    vecs = [b_query, b_value, b_in, b_proj, gain_one, shift_one, b_out, gain_two, shift_two]
    piece, x_send = open_call(
        layer_in, [order[1], order[3]], quarter, w_query, w_key, w_value, w_proj, vecs
    )
    x_got = x_swap(x_send) if pair else None
    gathered = lax.all_gather(piece, FSDP, axis=0, tiled=True)
    wi_m = lax.all_gather(after(w_in, piece), FSDP, axis=0, tiled=True)
    out_both = jnp.concatenate([w_out.T, y_swap(after(w_out.T, piece))], axis=1)
    gathered = after(gathered, out_both)
    wo = lax.all_gather(after(out_both, gathered), FSDP, axis=0, tiled=True)
    wq, wkv, wp_m, vec = split_call(fsdp_count, b_query.shape[0], n_long, gathered)
    bias = vec[:, 0:192]
    wp_t = y_swap(wp_m)
    wi_t = y_swap(wi_m)

    if pair:
        x_got = after(x_got, wkv)
        q_all, kv_own = qkv(layer_in, wq, wkv, bias, True)
        x_core = core_swap(x_got)
        kv_pieces = [kv_own] + [qkv(v, wq, wkv, bias, False)[0] for v in (x_got, x_core)]
        kv_starts = [own_rows + k * quarter for k in range(4)]
        kv_starts += [other_rows + order[k] * quarter for k in (1, 3, 0, 2)]
    else:
        q_all, _ = qkv(layer_in, wq, wkv, bias, True)
        x_all = lax.all_gather(layer_in, CTX, axis=0, tiled=True)
        kv_pieces = list(qkv(x_all, wq, wkv, bias, False))
        kv_starts = [k * quarter for k in range(seq // quarter)]
    blocks = tokens // BLK
    rand = rand_blocks.reshape(-1)
    live = lengths[0]

    def meta(half_index):
        values = [half_index * (blocks // 2), ctx * blocks, live, (1 - c) * (blocks // 4)]
        values += [(8 * y + 4 * (1 - c)) * blocks // 32, 4 * (1 - c) * blocks // 32, y]
        return jnp.stack(values).astype(jnp.int32)

    as_table = lambda values: jnp.stack([jnp.asarray(v, jnp.int32) for v in values])
    chunks = seq // quarter
    starts = as_table(kv_starts)
    kv_pieces[-1] = after(kv_pieces[-1], wp_t)
    o_send, dense_o, dense_log = attend(
        meta(1 - y), rand, starts, q_all, kv_pieces, seq, half, chunks
    )
    o_got = y_swap(o_send)
    (o_keep,) = attend(
        meta(y), rand, starts, after(q_all, o_send, wi_m), kv_pieces, seq, half, chunks, dense_o
    )
    o_keep, o_got = lax.optimization_barrier((o_keep, o_got))

    slot = jnp.stack([tp, ctx * tokens + tp * quarter, live]).astype(jnp.int32)
    part_peer, part_own = project(o_keep, o_got, wp_m, wp_t)
    resid, hidden, hid_own = norm_one(slot, layer_in, part_own, core_swap(part_peer), vec)
    hid_peer = core_swap(hid_own)

    x_order = collect(after(layer_in, o_keep), order, [x_core, x_got] if pair else [])
    outs = mlp_up(hid_peer, wi_m, wi_t, vec, wp_t, None)
    act, slope, hid = mlp_up(hid_own, wi_m, wi_t, vec, wp_t, outs)
    wo = after(wo, act, x_order)
    mlp_got = core_swap(mlp_down(act, wo, False))
    part_own = mlp_down(act, wo, True)
    out_own, gm_own, grad_two, sums_two = norm_two(slot, cotangent, hidden, part_own, mlp_got, vec)
    gm_peer = core_swap(gm_own)
    out_other = y_swap(out_own)
    outs = mlp_back(gm_peer, slope, wi_m, wi_t, wo, None)
    gh_got, dbi_peer = core_swap(outs[2]), outs[3]
    gp, gm, gh_own, dbi_own = mlp_back(gm_own, slope, wi_m, wi_t, wo, outs[0:2])
    grad_one, gb_own, sums_one = norm_one_back(resid, grad_two, gh_own, gh_got, vec)
    go_send, go_keep, gb, vec_sum = heads_back(
        core_swap(gb_own), gb_own, wp_m, wp_t, sums_two, gm_peer, sums_one, dbi_peer, dbi_own
    )
    go_got = y_swap(go_send)

    def z_sum(value):
        return lax.psum_scatter(value, FSDP, scatter_dimension=0, tiled=True)

    def x_sum(value):
        value = value.astype(bf16)
        return value.astype(f32) + x_swap(value).astype(f32) if pair else lax.psum(value, CTX).astype(f32)

    dwo = z_sum(tn(gm, act).astype(bf16))
    dwi_full = tn(hid, gp).astype(bf16)
    dwi = z_sum(dwi_full)
    dwp_t = tn(gb, o_got).astype(bf16)
    dwp = tn(gb, o_keep).astype(bf16)

    if pair:
        chunk_rows = [own_rows + k * quarter for k in order] + [other_rows + k * quarter for k in order]
    else:
        chunk_rows = [k * quarter for k in range(chunks)]
    starts = as_table(kv_starts + chunk_rows)
    n_send = 2 if pair else 0
    go_keep = after(go_keep, dwp_t, dwp, dwi_full)
    carried = attend_back(
        meta(y), rand, starts, q_all, go_keep, kv_pieces, seq, chunks, n_send, tokens
    )
    go_got, dwo, out_other, *carried = lax.optimization_barrier((go_got, dwo, out_other, *carried))
    dwo_got = y_swap(dwo[:, units:])
    dwp_got = y_swap(after(dwp_t, carried[1]))
    outs = attend_back(
        meta(1 - y), rand, starts, q_all, go_got, kv_pieces, seq, chunks, n_send, tokens,
        (carried[1], carried[0]), (go_keep, go_got, dense_o, dense_log),
    )
    outs, dwo_got, dwp_got = lax.optimization_barrier((outs, dwo_got, dwp_got))
    dq, dkv = outs[0:2]
    dw = products_call(x_order if pair else x_all, x_order, dq, dkv)

    gate = dkv
    table = table_call(fsdp_count, dw, dwp, dwp_got, vec_sum, go_got)
    dwo_sum = (dwo[:, 0:units].astype(f32) + dwo_got.astype(f32)).astype(bf16)
    if pair:
        came = [x_swap(v) for v in outs[2:]]
        came[0] = after(came[0], dwi)
        gate = came[0]
        got = [came[0], came[0], came[1], came[1]]
        mine = dkv
    else:
        got = [None] * 4
        mine = collect(lax.psum_scatter(dkv, CTX, scatter_dimension=0, tiled=True), order, [])

    def back_of(k, *adds):
        return input_back(k, dq, mine, got[k], k % 2, wq, wkv, list(adds))

    sent = [core_swap(back_of(k)) for k in (0, 2)]
    lead = back_of(1, grad_one, sent[0])
    rear = back_of(3, sent[1])
    dwi = after(dwi, lead)
    dwi_sum = (dwi[:, 0:units].astype(f32) + y_swap(dwi[:, units:]).astype(f32)).astype(bf16)
    out_both = jnp.concatenate([out_own, after(out_other, gate)], axis=0)
    layer_out = place(
        [core_swap(out_both), out_both], [order[0], order[2], order[1], order[3]], tokens
    )

    both = z_sum(table)
    dwo = x_sum(dwo_sum)
    dwi = x_sum(dwi_sum)
    came_both = x_swap(both) if pair else lax.psum(both.astype(f32), CTX) - both.astype(f32)
    dwq, dwk, dwv, dwp, small = last_call(both, came_both)
    sizes = [shard] * 6 + [units // fsdp_count, 192 // fsdp_count, 192 // fsdp_count]
    db_out, dg2, ds2, dg1, ds1, db_proj, db_in, db_query, db_value = [
        small[k, 0:size] for k, size in enumerate(sizes)
    ]
    from_rear, from_lead = after(y_swap(rear), came_both), y_swap(lead)
    lead_sum = (lead.astype(f32) + from_rear.astype(f32)).astype(bf16)
    grad_input = place([core_swap(lead_sum), lead_sum], order[0:2], tokens)
    from_lead = after(from_lead, layer_out, dwi, dwo, dwq, small, grad_input)
    rear_sum = (rear.astype(f32) + from_lead.astype(f32)).astype(bf16)
    grad_input = place([core_swap(rear_sum), rear_sum], order[2:4], tokens, grad_input)
    return (
        layer_out,
        grad_input,
        dwq,
        db_query,
        dwk,
        dwv,
        db_value,
        dwp,
        db_proj,
        dg1,
        ds1,
        dwi,
        db_in,
        dwo.T,
        db_out,
        dg2,
        ds2,
    )


def solution(mesh):
    rows = P((FSDP, CTX), None)
    vector, unit = P(FSDP), P((TP, FSDP))
    column, row = P(FSDP, TP), P(TP, FSDP)
    return jax.shard_map(
        on_device,
        mesh=mesh,
        in_specs=(
            rows, rows, vector, P(FSDP, CTX, None), column, unit, column, column, unit, row,
            vector, vector, vector, column, unit, row, vector, vector, vector,
        ),
        out_specs=(
            rows, rows, column, unit, column, column, unit, row, vector, vector, vector,
            column, unit, row, vector, vector, vector,
        ),
        check_vma=False,
    )
```

```python
import functools
import math

import jax
import jax.numpy as jnp
from jax import lax
from jax.experimental import pallas as pl
from jax.experimental.pallas import tpu as pltpu
from jax.sharding import PartitionSpec as P

BLK = 64
PAIR = 2
MASKED = -1e30
CHUNK = 512
EPSILON = 1e-05
FSDP, CTX, TP = "fsdp", "ctx", "tp"
f32, bf16 = jnp.float32, jnp.bfloat16
ANY = pl.BlockSpec(memory_space=pl.ANY)


VM = pl.BlockSpec(memory_space=pltpu.VMEM)
HBM = pl.BlockSpec(memory_space=pltpu.HBM)
MIB = 1 << 20
LIGHT = pl.CostEstimate(flops=0, bytes_accessed=0, transcendentals=0)
SPACES = {"h": pltpu.HBM, "v": pltpu.VMEM}


def call(kernel, out_shape, ins="", outs="", **options):
    spec = options.get("grid_spec")
    tables = spec.num_scalar_prefetch if spec is not None else 0

    def letter(text, k):
        return text[min(k, len(text) - 1)] if text else "h"

    many = isinstance(out_shape, (list, tuple))
    shapes = list(out_shape) if many else [out_shape]
    shapes = [
        v if letter(outs, k) == "-" else SPACES[letter(outs, k)](v.shape, v.dtype)
        for k, v in enumerate(shapes)
    ]
    run = pl.pallas_call(kernel, out_shape=shapes if many else shapes[0], **options)

    def apply(*args):
        placed = [
            v if letter(ins, k) == "-" else pltpu.with_memory_space_constraint(v, SPACES[letter(ins, k)])
            for k, v in enumerate(args[tables:])
        ]
        return run(*args[0:tables], *placed)

    return apply


def nt(a, b):
    return lax.dot_general(a, b, (((1,), (1,)), ((), ())), preferred_element_type=f32)


def tn(a, b):
    return lax.dot_general(a, b, (((0,), (0,)), ((), ())), preferred_element_type=f32)


def nn(a, b):
    return jnp.dot(a, b, preferred_element_type=f32)


def place_kernel(count, slots_ref, *refs):
    rows = refs[-1].shape[0]
    parts = [(ref, at) for ref in refs[:count] for at in range(0, ref.shape[0], rows)]
    for k, (ref, at) in enumerate(parts):

        @pl.when(pl.program_id(0) == k)
        def _():
            refs[-1][...] = ref[at : at + rows, :]


def place(pieces, slots, total, earlier=None):
    count, steps = len(pieces), len(slots)
    rows, width = sum(p.shape[0] for p in pieces) // steps, pieces[0].shape[1]
    more = [] if earlier is None else [earlier]
    return call(
        functools.partial(place_kernel, count),
        ins="-",
        outs="h",
        grid_spec=pltpu.PrefetchScalarGridSpec(
            num_scalar_prefetch=1,
            grid=(steps,),
            in_specs=[whole_block(p) for p in pieces] + [ANY] * len(more),
            out_specs=pl.BlockSpec((rows, width), lambda g, s: (s[g], 0)),
        ),
        out_shape=jax.ShapeDtypeStruct((total, width), pieces[0].dtype),
        input_output_aliases={1 + count: 0} if more else {},
        compiler_params=pltpu.CompilerParams(vmem_limit_bytes=8 * MIB),
        cost_estimate=LIGHT,
        name="place",
    )(jnp.stack(slots).astype(jnp.int32), *pieces, *more)


def collect_kernel(count, slots_ref, x_ref, *refs):
    step = pl.program_id(0)

    @pl.when(step < 4)
    def _():
        refs[count][...] = x_ref[...]

    rows = x_ref.shape[0]
    parts = [(ref, at) for at in range(0, 2 * rows, rows) for ref in refs[:count]]
    for k, (ref, at) in enumerate(parts):

        @pl.when(step == 4 + k)
        def _():
            refs[count][...] = ref[at : at + rows, :]


def collect(x, slots, others):
    count = len(others)
    rows, width = x.shape[0] // 4, x.shape[1]
    steps = 4 + sum(v.shape[0] // rows for v in others)
    return call(
        functools.partial(collect_kernel, count),
        grid_spec=pltpu.PrefetchScalarGridSpec(
            num_scalar_prefetch=1,
            grid=(steps,),
            in_specs=[pl.BlockSpec((rows, width), lambda g, s: (s[jnp.minimum(g, 3)], 0))]
            + [whole_block(v) for v in others],
            out_specs=pl.BlockSpec((rows, width), lambda g, s: (g, 0)),
        ),
        out_shape=jax.ShapeDtypeStruct((steps * rows, width), x.dtype),
        compiler_params=pltpu.CompilerParams(vmem_limit_bytes=8 * MIB),
        cost_estimate=LIGHT,
        name="collect",
    )(jnp.stack(slots).astype(jnp.int32), x, *others)


def load_all(pairs, sems):
    copies = [pltpu.make_async_copy(src, dst, sems.at[k]) for k, (src, dst) in enumerate(pairs)]
    for copy in copies:
        copy.start()
    for copy in copies:
        copy.wait()


def open_kernel(count, slots_ref, x_ref, *refs):
    srcs, vecs = refs[0:4], refs[4:13]
    a_ref, half_ref, wq, wk, wv, wp, sems = refs[13:]
    size = half_ref.shape[0] // count
    pairs = []
    for k in range(count):
        start = pl.multiple_of(slots_ref[k] * size, 64)
        pairs.append((x_ref.at[pl.ds(start, size)], half_ref.at[pl.ds(k * size, size)]))
    load_all(list(zip(srcs, (wq, wk, wv, wp))) + pairs, sems)
    rows = wq.shape[0]
    a_ref[0:rows, 0:192] = wq[...]
    a_ref[0:rows, 192:384] = wk[...]
    a_ref[0:rows, 384:448] = wv[:, 128:192]
    a_ref[0:rows, 448:576] = wv[:, 0:128]
    turned_p = wp[...].T
    a_ref[0:rows, 576:640] = turned_p[:, 128:192]
    a_ref[0:rows, 640:768] = turned_p[:, 0:128]
    a_ref[rows : rows + 16, :] = jnp.zeros((16, 768), bf16)
    for k, vec in enumerate(vecs):
        n = vec.shape[0]
        a_ref[rows + k : rows + k + 1, 0:n] = vec[...].reshape(1, n)


def whole_block(value):
    zeros = (0,) * value.ndim
    return pl.BlockSpec(value.shape, lambda *_: zeros, pipeline_mode=pl.Buffered(1))


def open_call(x, slots, size, wq, wk, wv, wp, vecs):
    count = len(slots)
    rows, width = wq.shape[0], x.shape[1]
    srcs = [wq, wk, wv, wp]
    return call(
        functools.partial(open_kernel, count),
        grid_spec=pltpu.PrefetchScalarGridSpec(
            num_scalar_prefetch=1,
            grid=(1,),
            in_specs=[HBM] * 5 + [whole_block(v) for v in vecs],
            out_specs=[
                pl.BlockSpec((rows + 16, 768), lambda g, s: (0, 0)),
                pl.BlockSpec((count * size, width), lambda g, s: (0, 0)),
            ],
            scratch_shapes=[pltpu.VMEM(v.shape, bf16) for v in srcs]
            + [pltpu.SemaphoreType.DMA((4 + count,))],
        ),
        out_shape=[
            jax.ShapeDtypeStruct((rows + 16, 768), bf16),
            jax.ShapeDtypeStruct((count * size, width), bf16),
        ],
        compiler_params=pltpu.CompilerParams(vmem_limit_bytes=8 * MIB),
        cost_estimate=LIGHT,
        name="open",
    )(jnp.stack(slots).astype(jnp.int32), x, *srcs, *vecs)


def qkv_kernel(with_q, x_ref, wq_ref, wkv_ref, bias_ref, *outs):
    x = x_ref[...]
    zero = jnp.zeros((1, 64), f32)
    value_bias = bias_ref[1:2, :]
    bkv = jnp.concatenate([zero, zero, zero, value_bias[:, 128:192], value_bias[:, 0:128]], axis=1)
    outs[-1][...] = (nn(x, wkv_ref[...]) + bkv).astype(bf16)
    if with_q:
        bq = jnp.concatenate([bias_ref[0:1, :], zero], axis=1)
        outs[0][...] = (nn(x, wq_ref[...]) + bq).astype(bf16) * jnp.asarray(0.125, bf16)


def qkv(x, wq, wkv, bias, with_q):
    rows, width = x.shape
    tile = rows // 2 if rows <= 1024 else 512
    widths = [256, 384] if with_q else [384]
    return call(
        functools.partial(qkv_kernel, with_q),
        grid=(rows // tile,),
        in_specs=[pl.BlockSpec((tile, width), lambda g: (g, 0))]
        + [whole_block(v) for v in (wq, wkv, bias)],
        out_specs=[pl.BlockSpec((tile, w), lambda g: (g, 0)) for w in widths],
        out_shape=[jax.ShapeDtypeStruct((rows, w), bf16) for w in widths],
        compiler_params=pltpu.CompilerParams(vmem_limit_bytes=12 * MIB),
        cost_estimate=LIGHT,
        name="qkv",
    )(x, wq, wkv, bias)


def head_masks(places):
    group = lax.broadcasted_iota(jnp.int32, (1, 256), 1) // 64
    return [(group == place).astype(bf16) for place in places]


def spread(rows, masks):
    return jnp.concatenate([rows * m for m in masks], axis=0)


def fold(stacked, masks):
    n = stacked.shape[0] // 3
    out = stacked[0:n] * masks[0].astype(f32)
    for h in (1, 2):
        out = out + stacked[h * n : (h + 1) * n] * masks[h].astype(f32)
    return out


def tile_starts(i, b, rand_ref, seq):
    near = jnp.clip((i - 1) * BLK, 0, seq - 3 * BLK)
    near = pl.multiple_of(near, BLK)
    rand = [pl.multiple_of(rand_ref[3 * b + r] * BLK, BLK) for r in range(3)]
    return near, rand


def gather_tiles(kv, near, rand):
    parts = [kv[pl.ds(near, 3 * BLK), :]]
    parts += [kv[pl.ds(r, BLK), :] for r in rand]
    parts += [kv[0 : 2 * BLK, :]]
    return jnp.concatenate(parts, axis=0)


def tile_live(i, near, rand, length):
    out = []
    for j in range(3):
        blk = near // BLK + j
        out.append(jnp.where(jnp.abs(blk - i) <= 1, length - blk * BLK, 0))
    out += [length - r for r in rand]
    for g in range(2):
        out.append(jnp.where(jnp.abs(i - g) > 1, length - g * BLK, 0))
    return out


def load_pieces(size, starts_ref, pieces, kv, sems):
    copies = []
    for piece in pieces:
        for at in range(0, piece.shape[0], size):
            k = len(copies)
            start = pl.multiple_of(starts_ref[k], 64)
            copies.append(
                pltpu.make_async_copy(
                    piece.at[pl.ds(at, size)], kv.at[pl.ds(start, size)], sems.at[k]
                )
            )
    for copy in copies:
        copy.start()
    for copy in copies:
        copy.wait()


def step_block(meta_ref, step, steps):
    first = meta_ref[0] + PAIR * lax.rem(step + meta_ref[3] // PAIR, steps)
    return first, meta_ref[1] + first, meta_ref[2]


def turned(column):
    return jnp.broadcast_to(column, (column.shape[0], 128)).T[0:1, :]


def fwd_kernel(count, chunks, leads, meta_ref, rand_ref, starts_ref, q_ref, qd_ref, *rest):
    pieces, rest = rest[:count], rest[count:]
    if leads:
        o_ref, dense_ref, log_ref, kv, sems = rest
    else:
        dense_ref, o_ref, kv, sems = rest
    seq = kv.shape[0]
    step = pl.program_id(0) - (1 if leads else 0)
    steps = pl.num_programs(0) - (1 if leads else 0)
    first, block0, length = step_block(meta_ref, jnp.maximum(step, 0), steps)
    kmask = head_masks((0, 1, 2))
    vmask = head_masks((2, 3, 1))

    @pl.when(pl.program_id(0) == 0)
    def _():
        load_pieces(seq // chunks, starts_ref, pieces, kv, sems)

    def sparse(u):
        i = block0 + u
        near, rand = tile_starts(i, first + u, rand_ref, seq)
        tiles = gather_tiles(kv, near, rand)
        live = tile_live(i, near, rand, length)
        lane = lax.broadcasted_iota(jnp.int32, (1, BLK), 1)
        bias = jnp.concatenate([jnp.where(lane < n, 0.0, MASKED) for n in live], axis=1)
        qs = spread(q_ref[u * BLK : (u + 1) * BLK, :], kmask)
        s = nt(qs, tiles[:, 0:256]) + bias
        top = jnp.max(s, axis=1, keepdims=True)
        p = jnp.exp(s - top)
        total = jnp.sum(p, axis=1, keepdims=True)
        mixed = nn(p.astype(bf16), tiles[:, 128:384]) / total
        o_ref[u * BLK : (u + 1) * BLK, :] = fold(mixed, vmask).astype(bf16)

    def dense():
        qs = jnp.concatenate(
            [spread(qd_ref[u * BLK : (u + 1) * BLK, :], kmask) for u in range(PAIR)], axis=0
        )
        rows = qs.shape[0]
        lane = lax.broadcasted_iota(jnp.int32, (1, CHUNK), 1)

        def body(c, carry):
            top, total, mixed = carry
            start = pl.multiple_of(c * CHUNK, CHUNK)
            keys = kv[pl.ds(start, CHUNK), :]
            s = nt(qs, keys[:, 0:256]) + jnp.where(lane + start < length, 0.0, MASKED)
            new = jnp.maximum(top, jnp.max(s, axis=1, keepdims=True))
            scale = jnp.exp(top - new)
            p = jnp.exp(s - new)
            total = total * scale + jnp.sum(p, axis=1, keepdims=True)
            mixed = mixed * scale + nn(p.astype(bf16), keys[:, 128:384])
            return new, total, mixed

        init = (
            jnp.full((rows, 1), MASKED, f32),
            jnp.zeros((rows, 1), f32),
            jnp.zeros((rows, 256), f32),
        )
        top, total, mixed = lax.fori_loop(0, seq // CHUNK, body, init)
        mixed = mixed / total
        log_ref[...] = jnp.broadcast_to(turned(top + jnp.log(total)), log_ref.shape)
        half = rows // PAIR
        for u in range(PAIR):
            dense_ref[u * BLK : (u + 1) * BLK, :] = fold(
                mixed[u * half : (u + 1) * half], vmask
            ).astype(bf16)

    if leads:

        @pl.when((step < 0) & (meta_ref[1] == 0))
        def _():
            dense()

    @pl.when((step >= 0) & (block0 >= 2))
    def _():
        for u in range(PAIR):
            sparse(u)

    @pl.when((step >= 0) & (block0 < 2))
    def _():
        o_ref[...] = dense_ref[...]


def q_specs(steps, shift):
    def block(g, m, r, s):
        step = jnp.clip(g - shift, 0, steps - 1)
        return (m[0] // PAIR + lax.rem(step + m[3] // PAIR, steps), 0)

    fixed = pl.BlockSpec((PAIR * BLK, 256), lambda g, m, r, s: (0, 0))
    return [pl.BlockSpec((PAIR * BLK, 256), block), fixed]


def attend(meta, rand, starts, q, pieces, seq, rows, chunks, dense=None):
    steps = rows // (PAIR * BLK)
    count = len(pieces)
    leads = dense is None
    fixed = pl.BlockSpec((PAIR * BLK, 256), lambda g, m, r, s: (0, 0))
    out_specs = [
        pl.BlockSpec((PAIR * BLK, 256), lambda g, m, r, s: (jnp.maximum(g - (1 if leads else 0), 0), 0))
    ]
    out_shape = [jax.ShapeDtypeStruct((rows, 256), bf16)]
    if leads:
        out_specs += [fixed, pl.BlockSpec((8, 3 * PAIR * BLK), lambda g, m, r, s: (0, 0))]
        out_shape += [
            jax.ShapeDtypeStruct((PAIR * BLK, 256), bf16),
            jax.ShapeDtypeStruct((8, 3 * PAIR * BLK), f32),
        ]
    return call(
        functools.partial(fwd_kernel, count, chunks, leads),
        grid_spec=pltpu.PrefetchScalarGridSpec(
            num_scalar_prefetch=3,
            grid=(steps + (1 if leads else 0),),
            in_specs=q_specs(steps, 1 if leads else 0) + [ANY] * count + ([] if leads else [fixed]),
            out_specs=out_specs,
            scratch_shapes=[pltpu.VMEM((seq, 384), bf16), pltpu.SemaphoreType.DMA((chunks,))],
        ),
        out_shape=out_shape,
        compiler_params=pltpu.CompilerParams(vmem_limit_bytes=seq * 768 + 6 * MIB),
        cost_estimate=LIGHT,
        name="attend",
    )(meta, rand, starts, q, q, *pieces, *([] if leads else [dense]))


def bwd_kernel(count, last, chunks, n_send, meta_ref, rand_ref, starts_ref, q_ref, qd_ref, do_ref, *rest):
    pieces, rest = rest[:count], rest[count:]
    if last:
        in_ref, _, own_ref, came_ref, od_ref, log_ref, dq_ref, all_ref = rest[:8]
        sends, (kv, acc, sems) = rest[8 : 8 + n_send], rest[-3:]
    else:
        dq_ref, out_ref, kv, acc, sems = rest
    seq = kv.shape[0]
    step = pl.program_id(0)
    steps = pl.num_programs(0) - (1 if last else 0)
    first, block0, length = step_block(meta_ref, jnp.minimum(step, steps - 1), steps)
    kmask = head_masks((0, 1, 2))
    vmask = head_masks((2, 3, 1))

    @pl.when(step == 0)
    def _():
        if last:
            carry = pltpu.make_async_copy(in_ref, acc, sems.at[chunks])
            carry.start()
        else:
            acc[...] = jnp.zeros_like(acc)
        load_pieces(seq // chunks, starts_ref, pieces, kv, sems)
        if last:
            carry.wait()

    def add_rows(start, n, wk, wv):
        rows = pl.ds(start, n)
        acc[rows, 0:128] += wk[:, 0:128]
        acc[rows, 128:256] += wk[:, 128:256] + wv[:, 0:128]
        acc[rows, 256:384] += wv[:, 128:256]

    def sparse(u):
        i = block0 + u
        near, rand = tile_starts(i, first + u, rand_ref, seq)
        tiles = gather_tiles(kv, near, rand)
        live = tile_live(i, near, rand, length)
        row = lax.broadcasted_iota(jnp.int32, (BLK, 192), 0)
        qs = spread(q_ref[u * BLK : (u + 1) * BLK, :], kmask)
        gs = spread(do_ref[u * BLK : (u + 1) * BLK, :], vmask)
        s = nt(tiles[:, 0:256], qs)
        s = jnp.concatenate(
            [jnp.where(row < live[j], s[j * BLK : (j + 1) * BLK], MASKED) for j in range(8)],
            axis=0,
        )
        top = jnp.max(s, axis=0, keepdims=True)
        p = jnp.exp(s - top)
        p = p * (1.0 / jnp.sum(p, axis=0, keepdims=True))
        dp = nt(tiles[:, 128:384], gs)
        inner = jnp.sum(p * dp, axis=0, keepdims=True)
        ds = (p * (dp - inner)).astype(bf16)
        wk = nn(ds, qs)
        wv = nn(p.astype(bf16), gs)
        add_rows(near, 192, wk[0:192], wv[0:192])
        for r in range(3):
            a = 192 + r * BLK
            add_rows(rand[r], BLK, wk[a : a + BLK], wv[a : a + BLK])
        add_rows(0, 128, wk[384:512], wv[384:512])
        dq = fold(tn(ds, tiles[:, 0:256]), kmask) * 0.125
        dq_ref[u * BLK : (u + 1) * BLK, :] = dq.astype(bf16)

    def dense():
        rows_g = jnp.where(meta_ref[6] == 0, own_ref[...].astype(f32), came_ref[...].astype(f32))
        qs, gs, inner = [], [], []
        for u in range(PAIR):
            rows = slice(u * BLK, (u + 1) * BLK)
            qs.append(spread(qd_ref[rows, :], kmask))
            gs.append(spread(rows_g[rows, :].astype(bf16), vmask))
            for m in vmask:
                part = rows_g[rows, :] * od_ref[rows, :].astype(f32) * m.astype(f32)
                inner.append(jnp.sum(part, axis=1, keepdims=True))
        qs, gs = jnp.concatenate(qs, axis=0), jnp.concatenate(gs, axis=0)
        inner = turned(jnp.concatenate(inner, axis=0))
        log_sum = log_ref[0:1, :]
        cols = qs.shape[0]
        row = lax.broadcasted_iota(jnp.int32, (CHUNK, cols), 0)

        def back(c, dq):
            start = pl.multiple_of(c * CHUNK, CHUNK)
            keys = kv[pl.ds(start, CHUNK), :]
            s = jnp.where(row < length - start, nt(keys[:, 0:256], qs), MASKED)
            p = jnp.exp(s - log_sum)
            ds = (p * (nt(keys[:, 128:384], gs) - inner)).astype(bf16)
            add_rows(start, CHUNK, nn(ds, qs), nn(p.astype(bf16), gs))
            return dq + tn(ds, keys[:, 0:256])

        dq = lax.fori_loop(0, seq // CHUNK, back, jnp.zeros((cols, 256), f32))
        half = cols // PAIR
        for u in range(PAIR):
            dq_ref[u * BLK : (u + 1) * BLK, :] = (
                fold(dq[u * half : (u + 1) * half], kmask) * 0.125
            ).astype(bf16)

    @pl.when((step < steps) & (block0 >= 2))
    def _():
        for u in range(PAIR):
            sparse(u)

    if last:

        @pl.when((step == steps) & (meta_ref[1] == 0))
        def _():
            dense()

    @pl.when(pl.program_id(0) == pl.num_programs(0) - 1)
    def _():
        if not last:
            pltpu.sync_copy(acc, out_ref)
        else:
            size = seq // chunks

            def emit(k):
                start = pl.multiple_of(starts_ref[chunks + k], 64)
                return acc[pl.ds(start, size), :].astype(bf16)

            for k in range(chunks):
                piece = emit(k)
                all_ref[k * size : (k + 1) * size, :] = piece
                if n_send and k >= chunks - 4:
                    j = k - chunks + 4
                    dst, at = sends[j // 2], j % 2
                    dst[at * size : (at + 1) * size, :] = piece


def attend_back(meta, rand, starts, q, grad, pieces, seq, chunks, n_send, tokens, carried=None, dense=None):
    rows = tokens // 2
    steps = rows // (PAIR * BLK)
    count = len(pieces)
    last = carried is not None
    shape = (PAIR * BLK, 256)
    more = []
    if last:

        def dq_block(g, m, r, s):
            return (jnp.where((g == steps) & (m[1] == 0), m[4], jnp.minimum(g, steps - 1) + steps), 0)

        chosen = pl.BlockSpec(shape, lambda g, m, r, s: (m[5], 0))
        more = [
            chosen,
            chosen,
            pl.BlockSpec(shape, lambda g, m, r, s: (0, 0)),
            pl.BlockSpec((8, 3 * PAIR * BLK), lambda g, m, r, s: (0, 0)),
        ]
    else:
        dq_block = lambda g, m, r, s: (g, 0)
    out_specs = [pl.BlockSpec(shape, dq_block)]
    out_shape = [jax.ShapeDtypeStruct((tokens, 256), bf16)]
    if last:
        sizes = [seq] + [2 * seq // chunks] * n_send
        outs = [(n, 384, bf16) for n in sizes]
        out_specs += [
            pl.BlockSpec((n, w), lambda g, m, r, s: (0, 0), pipeline_mode=pl.Buffered(1)) for n, w, _ in outs
        ]
        out_shape += [jax.ShapeDtypeStruct((n, w), t) for n, w, t in outs]
    else:
        out_specs += [ANY]
        out_shape += [jax.ShapeDtypeStruct((seq, 384), f32)]
    grad_spec = pl.BlockSpec(shape, lambda g, m, r, s: (jnp.minimum(g, steps - 1), 0))
    return call(
        functools.partial(bwd_kernel, count, last, chunks, n_send),
        grid_spec=pltpu.PrefetchScalarGridSpec(
            num_scalar_prefetch=3,
            grid=(steps + (1 if last else 0),),
            in_specs=q_specs(steps, 0) + [grad_spec] + [ANY] * (count + (2 if last else 0)) + more,
            out_specs=out_specs,
            scratch_shapes=[
                pltpu.VMEM((seq, 384), bf16),
                pltpu.VMEM((seq, 384), f32),
                pltpu.SemaphoreType.DMA((chunks + 1,)),
            ],
        ),
        out_shape=out_shape,
        input_output_aliases={3 + 3 + count + 1: 0} if last else {},
        compiler_params=pltpu.CompilerParams(
            vmem_limit_bytes=seq * (3840 if last else 2304) + 7 * MIB
        ),
        cost_estimate=LIGHT,
        name="attend_back",
    )(meta, rand, starts, q, q, grad, *pieces, *(carried or ()), *(dense or ()))


def split_kernel(count, short, long, a_ref, wq_ref, wkv_ref, ship_ref, vec_ref):
    step = a_ref.shape[0] // count
    rows = step - 16
    parts = []
    for k in range(count):
        there, here = slice(k * step, k * step + rows), slice(k * rows, (k + 1) * rows)
        zero = jnp.zeros((rows, 64), bf16)
        wq_ref[here, 0:192] = a_ref[there, 0:192]
        wq_ref[here, 192:256] = zero
        wkv_ref[here, :] = a_ref[there, 192:576]
        ship_ref[here, 0:64] = zero
        ship_ref[here, 64:256] = a_ref[there, 576:768]
        parts.append(a_ref[k * step + rows : (k + 1) * step, :].astype(f32))
    width = vec_ref.shape[1]
    attn = jnp.concatenate([p[:, 0:short] for p in parts], axis=1)
    attn = jnp.concatenate([attn, jnp.zeros((16, width - attn.shape[1]), f32)], axis=1)
    dense = jnp.concatenate([p[:, 0:long] for p in parts], axis=1)
    vec = jnp.concatenate([attn[0:2], dense[2:16]], axis=0)
    vec_ref[...] = vec
    ship = jnp.concatenate([vec[2:3, k * 256 : (k + 1) * 256] for k in range(3)], axis=0)
    ship = jnp.concatenate([ship, jnp.zeros((13, 256), f32)], axis=0)
    ship_ref[count * rows : count * rows + 16, :] = ship.astype(bf16)


def split_call(count, short, long, gathered):
    rows = gathered.shape[0] - 16 * count
    outs = [
        jax.ShapeDtypeStruct((rows, 256), bf16),
        jax.ShapeDtypeStruct((rows, 384), bf16),
        jax.ShapeDtypeStruct((rows + 16, 256), bf16),
        jax.ShapeDtypeStruct((16, count * long), f32),
    ]
    return call(
        functools.partial(split_kernel, count, short, long),
        outs="-",
        grid=(1,),
        in_specs=[whole_block(gathered)],
        out_specs=[whole_block(v) for v in outs],
        out_shape=outs,
        compiler_params=pltpu.CompilerParams(vmem_limit_bytes=10 * MIB),
        cost_estimate=LIGHT,
        name="split",
    )(gathered)


TILE = 256


def proj_kernel(keep_ref, got_ref, wm_ref, wt_ref, peer_ref, own_ref):
    half, width = peer_ref.shape
    for k, out in enumerate((peer_ref, own_ref)):
        rows = slice(k * half, (k + 1) * half)
        value = nt(keep_ref[rows, :], wm_ref[0:width, :]) + nt(got_ref[rows, :], wt_ref[0:width, :])
        out[...] = value.astype(out.dtype)


def in_vmem(kernel, out_shape, limit, name, aliases=None, outs="v", ins="v"):
    def pick(text, values):
        return [VM if text[min(k, len(text) - 1)] == "v" else whole_block(v) for k, v in enumerate(values)]

    return lambda *args: call(
        kernel,
        ins=ins,
        outs=outs,
        grid=(1,),
        in_specs=pick(ins, args),
        out_specs=pick(outs, out_shape),
        out_shape=out_shape,
        input_output_aliases=aliases or {},
        compiler_params=pltpu.CompilerParams(vmem_limit_bytes=limit * MIB),
        cost_estimate=LIGHT,
        name=name,
    )(*args)


def project(keep, got, wm, wt):
    rows, width = keep.shape[0] // 2, wm.shape[0] - 16
    outs = [jax.ShapeDtypeStruct((rows, width), bf16)] * 2
    return in_vmem(proj_kernel, outs, 10, "project", outs="h", ins="-")(keep, got, wm, wt)


def stats(value):
    center = jnp.mean(value, axis=-1, keepdims=True)
    offset = value - center
    inverse = lax.rsqrt(jnp.mean(offset * offset, axis=-1, keepdims=True) + EPSILON)
    return offset * inverse, inverse


def fetch_two(slot_ref, src, dst, came, got, sems):
    start = pl.multiple_of(slot_ref[0] * dst.shape[0], 64)
    load_all([(src.at[pl.ds(start, dst.shape[0])], dst), (came, got)], sems)


def norm_one_kernel(
    slot_ref, x_ref, came_ref, part_ref, vec_ref, resid_ref, hidden_ref, low_ref, rows_ref, got_ref, sems
):
    fetch_two(slot_ref, x_ref, rows_ref, came_ref, got_ref, sems)
    for k in range(0, part_ref.shape[0], TILE):
        rows = slice(k, k + TILE)
        resid = rows_ref[rows, :].astype(f32) + (
            part_ref[rows, :].astype(f32) + got_ref[rows, :].astype(f32) + vec_ref[3:4, :]
        )
        resid_ref[rows, :] = resid
        normed, _ = stats(resid)
        hidden = normed * vec_ref[4:5, :] + vec_ref[5:6, :]
        hidden_ref[rows, :] = hidden
        low_ref[rows, :] = hidden.astype(bf16)


def norm_one(slot, x, part, got, vec):
    rows, width = part.shape
    return call(
        norm_one_kernel,
        ins="h-",
        outs="h",
        grid_spec=pltpu.PrefetchScalarGridSpec(
            num_scalar_prefetch=1,
            grid=(1,),
            in_specs=[HBM, ANY] + [whole_block(v) for v in (part, vec)],
            out_specs=[pl.BlockSpec((rows, width), lambda g, s: (0, 0))] * 3,
            scratch_shapes=[pltpu.VMEM((rows, width), bf16)] * 2 + [pltpu.SemaphoreType.DMA((2,))],
        ),
        out_shape=[jax.ShapeDtypeStruct((rows, width), t) for t in (f32, f32, bf16)],
        compiler_params=pltpu.CompilerParams(vmem_limit_bytes=14 * MIB),
        cost_estimate=LIGHT,
        name="norm_one",
    )(slot, x, got, part, vec)


def add_sums(total, low, error, normed):
    sums = [jnp.sum(v, axis=0, keepdims=True) for v in (low.astype(f32), error * normed, error)]
    return sums if total is None else [x + z for x, z in zip(total, sums)]


def ride(low_ref, sums_ref, total):
    sums = jnp.concatenate(total + [jnp.zeros((5, low_ref.shape[1]), f32)], axis=0)
    sums_ref[...] = sums
    rows = low_ref.shape[0] - 16
    low_ref[rows : rows + 16, :] = jnp.concatenate([sums, jnp.zeros_like(sums)], axis=0).astype(bf16)


def norm_two_kernel(
    slot_ref, cot_ref, came_ref, hidden_ref, part_ref, vec_ref,
    out_ref, low_ref, grad_ref, sums_ref, rows_ref, got_ref, sems,
):
    fetch_two(slot_ref, cot_ref, rows_ref, came_ref, got_ref, sems)
    gain = vec_ref[7:8, :]
    total = None
    for k in range(0, part_ref.shape[0], TILE):
        rows = slice(k, k + TILE)
        value = hidden_ref[rows, :] + (part_ref[rows, :].astype(f32) + got_ref[rows, :].astype(f32)) + vec_ref[6:7, :]
        normed, inverse = stats(value)
        position = slot_ref[1] + k + lax.broadcasted_iota(jnp.int32, (TILE, 1), 0)
        live = (position < slot_ref[2]).astype(f32)
        out_ref[rows, :] = ((normed * gain + vec_ref[8:9, :]) * live).astype(bf16)
        error = rows_ref[rows, :].astype(f32) * live
        inner = error * gain
        first = jnp.mean(inner, axis=-1, keepdims=True)
        second = jnp.mean(inner * normed, axis=-1, keepdims=True)
        grad = inverse * (inner - first - normed * second)
        grad_ref[rows, :] = grad
        low = grad.astype(bf16)
        low_ref[rows, :] = low
        total = add_sums(total, low, error, normed)
    ride(low_ref, sums_ref, total)


def norm_two(slot, cotangent, hidden, part, got, vec):
    rows, width = part.shape
    return call(
        norm_two_kernel,
        ins="h-",
        outs="h",
        grid_spec=pltpu.PrefetchScalarGridSpec(
            num_scalar_prefetch=1,
            grid=(1,),
            in_specs=[HBM, ANY] + [whole_block(v) for v in (hidden, part, vec)],
            out_specs=[
                pl.BlockSpec((n, width), lambda g, s: (0, 0)) for n in (rows, rows + 16, rows, 8)
            ],
            scratch_shapes=[pltpu.VMEM((rows, width), bf16)] * 2 + [pltpu.SemaphoreType.DMA((2,))],
        ),
        out_shape=[
            jax.ShapeDtypeStruct((rows, width), bf16),
            jax.ShapeDtypeStruct((rows + 16, width), bf16),
            jax.ShapeDtypeStruct((rows, width), f32),
            jax.ShapeDtypeStruct((8, width), f32),
        ],
        compiler_params=pltpu.CompilerParams(vmem_limit_bytes=14 * MIB),
        cost_estimate=LIGHT,
        name="norm_two",
    )(slot, cotangent, got, hidden, part, vec)


def norm_one_back_kernel(resid_ref, two_ref, part_ref, got_ref, vec_ref, grad_ref, low_ref, sums_ref):
    total = None
    for k in range(0, part_ref.shape[0], TILE):
        rows = slice(k, k + TILE)
        normed, inverse = stats(resid_ref[rows, :])
        error = two_ref[rows, :] + (part_ref[rows, :].astype(f32) + got_ref[rows, :].astype(f32))
        inner = error * vec_ref[4:5, :]
        first = jnp.mean(inner, axis=-1, keepdims=True)
        second = jnp.mean(inner * normed, axis=-1, keepdims=True)
        grad = inverse * (inner - first - normed * second)
        grad_ref[rows, :] = grad
        low = grad.astype(bf16)
        low_ref[rows, :] = low
        total = add_sums(total, low, error, normed)
    ride(low_ref, sums_ref, total)


def norm_one_back(resid, two, part, got, vec):
    rows, width = part.shape
    outs = [
        jax.ShapeDtypeStruct((rows, width), f32),
        jax.ShapeDtypeStruct((rows + 16, width), bf16),
        jax.ShapeDtypeStruct((8, width), f32),
    ]
    return in_vmem(norm_one_back_kernel, outs, 14, "norm_one_back", outs="h", ins="-")(resid, two, part, got, vec)


ERFC = (
    -1.26551223, 1.00002368, 0.37409196, 0.09678418, -0.18628806,
    0.27886807, -1.13520398, 1.48851587, -0.82215223, 0.17087277,
)


def gelu_pair(pre):
    z = jnp.abs(pre) * math.sqrt(0.5)
    t = 1.0 / (1.0 + 0.5 * z)
    poly = jnp.full_like(t, ERFC[-1])
    for coefficient in ERFC[-2::-1]:
        poly = poly * t + coefficient
    square = -z * z
    tail = 0.5 * t * jnp.exp(square + poly)
    cdf = jnp.where(pre < 0, tail, 1.0 - tail)
    density = jnp.exp(square) * (1.0 / math.sqrt(2.0 * math.pi))
    return (pre * cdf).astype(bf16), (cdf + pre * density).astype(bf16)


def up_kernel(base, hid_ref, wim_ref, wit_ref, vec_ref, ship_ref, *rest):
    act_ref, slope_ref, all_ref = rest[-3:]
    units, at = wim_ref.shape[1], ship_ref.shape[0] - 16
    shipped = ship_ref[at : at + 16, :].astype(f32)
    shipped = jnp.concatenate([shipped[k : k + 1, :] for k in range(3)], axis=1)
    for k in range(0, hid_ref.shape[0], TILE):
        rows, there = slice(k, k + TILE), slice(base + k, base + k + TILE)
        hid = hid_ref[rows, :]
        all_ref[there, :] = hid
        for j, (wi, b) in enumerate(((wim_ref, vec_ref[2:3, :]), (wit_ref, shipped))):
            act, slope = gelu_pair(nn(hid, wi[...]) + b)
            act_ref[there, j * units : (j + 1) * units] = act
            slope_ref[there, j * units : (j + 1) * units] = slope


def mlp_up(hid, wi_m, wi_t, vec, ship, earlier):
    rows, width = hid.shape
    units = wi_m.shape[1]
    big = jax.ShapeDtypeStruct((2 * rows, 2 * units), bf16)
    outs = [big, big, jax.ShapeDtypeStruct((2 * rows, width), bf16)]
    second = earlier is not None
    kernel = functools.partial(up_kernel, rows if second else 0)
    aliases = {5 + k: k for k in range(3)} if second else {}
    args = (hid, wi_m, wi_t, vec, ship) + (tuple(earlier) if second else ())
    return in_vmem(kernel, outs, 16, "mlp_up", aliases, ins="-----v")(*args)


def down_kernel(base, act_ref, wo_ref, part_ref):
    for k in range(0, part_ref.shape[0], TILE):
        there = slice(base + k, base + k + TILE)
        part_ref[k : k + TILE, :] = nt(act_ref[there, :], wo_ref[...]).astype(bf16)


def mlp_down(act, wo, second):
    rows = act.shape[0] // 2
    kernel = functools.partial(down_kernel, rows if second else 0)
    outs = [jax.ShapeDtypeStruct((rows, wo.shape[0]), bf16)]
    return in_vmem(kernel, outs, 10, "mlp_down", outs="h", ins="v-")(act, wo)[0]


def mlp_back_kernel(base, gm_ref, slope_ref, wim_ref, wit_ref, wo_ref, *rest):
    gp_ref, all_ref, part_ref, sums_ref = rest[-4:]
    units = wim_ref.shape[1]
    sums = [None, None]
    for k in range(0, part_ref.shape[0], TILE):
        rows, there = slice(k, k + TILE), slice(base + k, base + k + TILE)
        gm = gm_ref[rows, :]
        all_ref[there, :] = gm
        total = None
        for j, wi in enumerate((wim_ref, wit_ref)):
            cols = slice(j * units, (j + 1) * units)
            gp = (nn(gm, wo_ref[:, cols]) * slope_ref[there, cols].astype(f32)).astype(bf16)
            gp_ref[there, cols] = gp
            column = jnp.sum(gp.astype(f32), axis=0, keepdims=True)
            sums[j] = column if sums[j] is None else sums[j] + column
            value = nt(gp, wi[...])
            total = value if total is None else total + value
        part_ref[rows, :] = total.astype(bf16)
    sums_ref[...] = jnp.concatenate(sums + [jnp.zeros((6, units), f32)], axis=0)


def mlp_back(gm, slope, wi_m, wi_t, wo, earlier):
    rows, width = gm.shape[0] - 16, gm.shape[1]
    units = wi_m.shape[1]
    outs = [
        jax.ShapeDtypeStruct((2 * rows, 2 * units), bf16),
        jax.ShapeDtypeStruct((2 * rows, width), bf16),
        jax.ShapeDtypeStruct((rows, width), bf16),
        jax.ShapeDtypeStruct((8, units), f32),
    ]
    second = earlier is not None
    kernel = functools.partial(mlp_back_kernel, rows if second else 0)
    aliases = {5 + k: k for k in range(2)} if second else {}
    args = (gm, slope, wi_m, wi_t, wo) + (tuple(earlier) if second else ())
    return in_vmem(kernel, outs, 20, "mlp_back", aliases, outs="vvhh", ins="-v---v")(*args)


def heads_kernel(
    peer_ref, own_ref, wm_ref, wt_ref, two_ref, twop_ref, one_ref, dbi_a_ref, dbi_b_ref,
    send_ref, keep_ref, both_ref, vec_ref,
):
    half = peer_ref.shape[0] - 16
    for k, ref in enumerate((peer_ref, own_ref)):
        rows = slice(k * half, (k + 1) * half)
        grad = ref[0:half, :]
        both_ref[rows, :] = grad
        send_ref[rows, :] = nn(grad, wt_ref[0 : grad.shape[1], :]).astype(bf16)
        keep_ref[rows, :] = nn(grad, wm_ref[0 : grad.shape[1], :]).astype(bf16)
    two = two_ref[...] + twop_ref[half : half + 16, :].astype(f32)[0:8]
    one = one_ref[...] + peer_ref[half : half + 16, :].astype(f32)[0:8]
    dbi = dbi_a_ref[...] + dbi_b_ref[...]
    vec = jnp.concatenate([two[0:3], one[0:3], dbi[1:2], dbi[0:1]], axis=0)
    vec_ref[...] = vec
    width = vec.shape[1] // 3
    packed = jnp.concatenate([vec[:, k * width : (k + 1) * width] for k in range(3)], axis=0)
    packed = jnp.concatenate([packed, jnp.zeros((8, width), f32)], axis=0)
    send_ref[2 * half : 2 * half + 32, :] = packed.astype(bf16)


def heads_back(peer, own, wm, wt, two, gm_peer, one, dbi_a, dbi_b):
    rows, width = peer.shape[0] - 16, peer.shape[1]
    shapes = [(2 * rows + 32, 256), (2 * rows, 256), (2 * rows, width)]
    outs = [jax.ShapeDtypeStruct(v, bf16) for v in shapes] + [jax.ShapeDtypeStruct((8, width), f32)]
    return in_vmem(heads_kernel, outs, 12, "heads_back", outs="h", ins="-")(
        peer, own, wm, wt, two, gm_peer, one, dbi_a, dbi_b
    )


def input_kernel(count, dq_ref, mine_ref, *rest):
    got_ref = rest[0] if count else None
    wq_ref, wkv_ref = rest[count : count + 2]
    adds, out_ref = rest[count + 2 : -1], rest[-1]
    both = mine_ref[...]
    if count:
        both = (both.astype(f32) + got_ref[...].astype(f32)).astype(bf16)
    total = nt(dq_ref[...], wq_ref[...]) + nt(both, wkv_ref[...])
    for add in adds:
        total = total + add[...].astype(f32)
    out_ref[...] = total.astype(bf16)


def input_back(k, dq, mine, got, got_block, wq, wkv, adds):
    got = [] if got is None else [got]
    rows, width = dq.shape[0] // 4, wq.shape[0]
    out = jax.ShapeDtypeStruct((rows, width), bf16)
    return call(
        functools.partial(input_kernel, len(got)),
        ins="hh" + "-" * len(got) + "hh-",
        grid=(1,),
        in_specs=[
            pl.BlockSpec((rows, 256), lambda g: (k, 0)),
            pl.BlockSpec((rows, 384), lambda g: (k, 0)),
        ]
        + [pl.BlockSpec((rows, 384), lambda g: (got_block, 0)) for _ in got]
        + [whole_block(v) for v in [wq, wkv] + adds],
        out_specs=whole_block(out),
        out_shape=out,
        compiler_params=pltpu.CompilerParams(vmem_limit_bytes=8 * MIB),
        cost_estimate=pl.CostEstimate(flops=8 * 10**9, bytes_accessed=0, transcendentals=0),
        name="input_back",
    )(dq, mine, *got, wq, wkv, *adds)


def table_kernel(dw_ref, dwp_ref, got_ref, vec_ref, peer_ref, table):
    count = (table.shape[0] - got_ref.shape[0]) // 16
    shard = got_ref.shape[0] // count
    dwq_t, dwkv_t = dw_ref[0:192, :], dw_ref[256:640, :]
    dbv, dbq = dw_ref[640:641, 0:256], dw_ref[641:642, 0:192]
    dbv = jnp.concatenate([dbv[:, 128:256], dbv[:, 64:128]], axis=1)
    came = peer_ref[...].astype(f32)
    came = jnp.concatenate([came[8 * k : 8 * k + 8, :] for k in range(3)], axis=1)
    vectors = [vec_ref[k : k + 1, :] + came[k : k + 1, :] for k in (0, 1, 2, 4, 5, 3)]
    vectors += [vec_ref[7:8, :] + came[6:7, :], dbq, dbv]
    dwq, dwkv = dwq_t.T, dwkv_t.T
    for j in range(count):
        rows = slice(j * shard, (j + 1) * shard)
        base = j * (shard + 16)
        main = slice(base, base + shard)
        table[main, 0:192] = dwq[rows, :].astype(bf16)
        table[main, 192:576] = dwkv[rows, :].astype(bf16)
        table[main, 576:768] = (
            dwp_ref[rows, 64:256].astype(f32) + got_ref[rows, 64:256].astype(f32)
        ).astype(bf16)
        parts = []
        for vector in vectors:
            n = vector.shape[1] // count
            parts.append(
                jnp.concatenate([vector[:, j * n : (j + 1) * n], jnp.zeros((1, 768 - n), f32)], axis=1)
            )
        parts.append(jnp.zeros((16 - len(parts), 768), f32))
        table[base + shard : base + shard + 16, :] = jnp.concatenate(parts, axis=0).astype(bf16)


def table_call(count, dw, dwp, got, vec, peer):
    out = jax.ShapeDtypeStruct((got.shape[0] + 16 * count, 768), bf16)
    args = [dw, dwp, got, vec, peer]
    specs = [whole_block(v) for v in args]
    specs[4] = pl.BlockSpec((32, 256), lambda g: (peer.shape[0] // 32 - 1, 0))
    return call(
        table_kernel,
        ins="h",
        outs="h",
        grid=(1,),
        in_specs=specs,
        out_specs=whole_block(out),
        out_shape=out,
        compiler_params=pltpu.CompilerParams(vmem_limit_bytes=14 * MIB),
        cost_estimate=LIGHT,
        name="table",
    )(*args)


def products_kernel(own, x_ref, xq_ref, dq_ref, dkv_ref, dw_ref):
    step = pl.program_id(0)

    @pl.when(step == 0)
    def _():
        dw_ref[...] = jnp.zeros_like(dw_ref)

    dw_ref[256:640, :] += tn(dkv_ref[...], x_ref[...])
    dw_ref[640:641, 0:256] += jnp.sum(dkv_ref[:, 128:384].astype(f32), axis=0, keepdims=True)

    @pl.when(step < own)
    def _():
        dw_ref[0:256, :] += tn(dq_ref[...], xq_ref[...])
        dw_ref[641:642, 0:256] += jnp.sum(dq_ref[...].astype(f32), axis=0, keepdims=True)


def products_call(x, xq, dq, dkv):
    rows, own, width = dq.shape[0], 1, x.shape[1]
    out = jax.ShapeDtypeStruct((648, width), f32)
    return call(
        functools.partial(products_kernel, own),
        ins="h",
        outs="h",
        grid=(x.shape[0] // rows,),
        in_specs=[
            pl.BlockSpec((rows, width), lambda g: (g, 0)),
            pl.BlockSpec((rows, width), lambda g: (jnp.minimum(g, own - 1), 0)),
            pl.BlockSpec((rows, 256), lambda g: (jnp.minimum(g, own - 1), 0)),
            pl.BlockSpec((rows, 384), lambda g: (g, 0)),
        ],
        out_specs=whole_block(out),
        out_shape=out,
        compiler_params=pltpu.CompilerParams(vmem_limit_bytes=24 * MIB),
        cost_estimate=LIGHT,
        name="products",
    )(x, xq, dq, dkv)


def last_kernel(mine_ref, came_ref, dwq_ref, dwk_ref, dwv_ref, dwp_ref, small_ref):
    both = mine_ref[...].astype(f32) + came_ref[...].astype(f32)
    shard = dwq_ref.shape[0]
    main = both[0:shard]
    dwq_ref[...] = main[:, 0:192]
    dwk_ref[...] = main[:, 192:384]
    dwv_ref[:, 0:128] = main[:, 448:576]
    dwv_ref[:, 128:192] = main[:, 384:448]
    down = main[:, 576:768].T
    dwp_ref[0:128, :] = down[64:192, :]
    dwp_ref[128:192, :] = down[0:64, :]
    small_ref[...] = both[shard : shard + 16, :]


def last_call(mine, came):
    shard = mine.shape[0] - 16
    shapes = [(shard, 192)] * 3 + [(192, shard), (16, 768)]
    outs = [jax.ShapeDtypeStruct(v, f32) for v in shapes]
    return in_vmem(last_kernel, outs, 8, "last", outs="h", ins="-")(mine, came)


def core_swap(value):
    return lax.ppermute(value, TP, [(0, 1), (1, 0), (2, 3), (3, 2)])


def y_swap(value):
    return lax.ppermute(value, TP, [(0, 2), (2, 0), (1, 3), (3, 1)])


def x_swap(value):
    return lax.ppermute(value, CTX, [(0, 1), (1, 0)])


def after(value, *others):
    return lax.optimization_barrier((value,) + others)[0]


def rows_at(array, start, count):
    return lax.dynamic_slice_in_dim(array, start, count, axis=0)


def on_device(
    layer_in,
    cotangent,
    lengths,
    rand_blocks,
    w_query,
    b_query,
    w_key,
    w_value,
    b_value,
    w_proj,
    b_proj,
    gain_one,
    shift_one,
    w_in,
    b_in,
    w_out,
    b_out,
    gain_two,
    shift_two,
):
    tokens, width = layer_in.shape
    ctx_count = lax.axis_size(CTX)
    fsdp_count = lax.axis_size(FSDP)
    ctx = lax.axis_index(CTX)
    tp = lax.axis_index(TP)
    y, c = tp // 2, tp % 2
    seq = tokens * ctx_count
    half, quarter = tokens // 2, tokens // 4
    shard = w_query.shape[0]
    units = w_in.shape[1]
    pair = ctx_count == 2
    order = [2 * y + 1 - c, 2 * y + c, 2 * (1 - y) + 1 - c, 2 * (1 - y) + c]
    own_rows, other_rows = ctx * tokens, (1 - ctx) * tokens

    n_long = b_in.shape[0]
    vecs = [b_query, b_value, b_in, b_proj, gain_one, shift_one, b_out, gain_two, shift_two]
    piece, x_send = open_call(
        layer_in, [order[1], order[3]], quarter, w_query, w_key, w_value, w_proj, vecs
    )
    x_got = x_swap(x_send) if pair else None
    gathered = lax.all_gather(piece, FSDP, axis=0, tiled=True)
    wi_m = lax.all_gather(after(w_in, piece), FSDP, axis=0, tiled=True)
    out_both = jnp.concatenate([w_out.T, y_swap(after(w_out.T, piece))], axis=1)
    gathered = after(gathered, out_both)
    wo = lax.all_gather(after(out_both, gathered), FSDP, axis=0, tiled=True)
    wq, wkv, wp_m, vec = split_call(fsdp_count, b_query.shape[0], n_long, gathered)
    bias = vec[:, 0:192]
    wp_t = y_swap(wp_m)
    wi_t = y_swap(wi_m)

    if pair:
        x_got = after(x_got, wkv)
        q_all, kv_own = qkv(layer_in, wq, wkv, bias, True)
        x_core = core_swap(x_got)
        kv_pieces = [kv_own] + [qkv(v, wq, wkv, bias, False)[0] for v in (x_got, x_core)]
        kv_starts = [own_rows + k * quarter for k in range(4)]
        kv_starts += [other_rows + order[k] * quarter for k in (1, 3, 0, 2)]
    else:
        q_all, _ = qkv(layer_in, wq, wkv, bias, True)
        x_all = lax.all_gather(layer_in, CTX, axis=0, tiled=True)
        kv_pieces = list(qkv(x_all, wq, wkv, bias, False))
        kv_starts = [k * quarter for k in range(seq // quarter)]
    blocks = tokens // BLK
    rand = rand_blocks.reshape(-1)
    live = lengths[0]

    def meta(half_index):
        values = [half_index * (blocks // 2), ctx * blocks, live, (1 - c) * (blocks // 4)]
        values += [(8 * y + 4 * (1 - c)) * blocks // 32, 4 * (1 - c) * blocks // 32, y]
        return jnp.stack(values).astype(jnp.int32)

    as_table = lambda values: jnp.stack([jnp.asarray(v, jnp.int32) for v in values])
    chunks = seq // quarter
    starts = as_table(kv_starts)
    kv_pieces[-1] = after(kv_pieces[-1], wp_t)
    o_send, dense_o, dense_log = attend(
        meta(1 - y), rand, starts, q_all, kv_pieces, seq, half, chunks
    )
    o_got = y_swap(o_send)
    (o_keep,) = attend(
        meta(y), rand, starts, after(q_all, o_send, wi_m), kv_pieces, seq, half, chunks, dense_o
    )
    o_keep, o_got = lax.optimization_barrier((o_keep, o_got))

    slot = jnp.stack([tp, ctx * tokens + tp * quarter, live]).astype(jnp.int32)
    part_peer, part_own = project(o_keep, o_got, wp_m, wp_t)
    resid, hidden, hid_own = norm_one(slot, layer_in, part_own, core_swap(part_peer), vec)
    hid_peer = core_swap(hid_own)

    x_order = collect(after(layer_in, o_keep), order, [x_core, x_got] if pair else [])
    outs = mlp_up(hid_peer, wi_m, wi_t, vec, wp_t, None)
    act, slope, hid = mlp_up(hid_own, wi_m, wi_t, vec, wp_t, outs)
    wo = after(wo, act, x_order)
    mlp_got = core_swap(mlp_down(act, wo, False))
    part_own = mlp_down(act, wo, True)
    out_own, gm_own, grad_two, sums_two = norm_two(slot, cotangent, hidden, part_own, mlp_got, vec)
    gm_peer = core_swap(gm_own)
    out_other = y_swap(out_own)
    outs = mlp_back(gm_peer, slope, wi_m, wi_t, wo, None)
    gh_got, dbi_peer = core_swap(outs[2]), outs[3]
    gp, gm, gh_own, dbi_own = mlp_back(gm_own, slope, wi_m, wi_t, wo, outs[0:2])
    grad_one, gb_own, sums_one = norm_one_back(resid, grad_two, gh_own, gh_got, vec)
    go_send, go_keep, gb, vec_sum = heads_back(
        core_swap(gb_own), gb_own, wp_m, wp_t, sums_two, gm_peer, sums_one, dbi_peer, dbi_own
    )
    go_got = y_swap(go_send)

    def z_sum(value):
        return lax.psum_scatter(value, FSDP, scatter_dimension=0, tiled=True)

    def x_sum(value):
        value = value.astype(bf16)
        return value.astype(f32) + x_swap(value).astype(f32) if pair else lax.psum(value, CTX).astype(f32)

    dwo = z_sum(tn(gm, act).astype(bf16))
    dwi_full = tn(hid, gp).astype(bf16)
    dwi = z_sum(dwi_full)
    dwp_t = tn(gb, o_got).astype(bf16)
    dwp = tn(gb, o_keep).astype(bf16)

    if pair:
        chunk_rows = [own_rows + k * quarter for k in order] + [other_rows + k * quarter for k in order]
    else:
        chunk_rows = [k * quarter for k in range(chunks)]
    starts = as_table(kv_starts + chunk_rows)
    n_send = 2 if pair else 0
    go_keep = after(go_keep, dwp_t, dwp, dwi_full)
    carried = attend_back(
        meta(y), rand, starts, q_all, go_keep, kv_pieces, seq, chunks, n_send, tokens
    )
    go_got, dwo, out_other, *carried = lax.optimization_barrier((go_got, dwo, out_other, *carried))
    dwo_got = y_swap(dwo[:, units:])
    dwp_got = y_swap(after(dwp_t, carried[1]))
    outs = attend_back(
        meta(1 - y), rand, starts, q_all, go_got, kv_pieces, seq, chunks, n_send, tokens,
        (carried[1], carried[0]), (go_keep, go_got, dense_o, dense_log),
    )
    outs, dwo_got, dwp_got = lax.optimization_barrier((outs, dwo_got, dwp_got))
    dq, dkv = outs[0:2]
    dw = products_call(x_order if pair else x_all, x_order, dq, dkv)

    gate = dkv
    table = table_call(fsdp_count, dw, dwp, dwp_got, vec_sum, go_got)
    dwo_sum = (dwo[:, 0:units].astype(f32) + dwo_got.astype(f32)).astype(bf16)
    if pair:
        came = [x_swap(v) for v in outs[2:]]
        came[0] = after(came[0], dwi)
        gate = came[0]
        got = [came[0], came[0], came[1], came[1]]
        mine = dkv
    else:
        got = [None] * 4
        mine = collect(lax.psum_scatter(dkv, CTX, scatter_dimension=0, tiled=True), order, [])

    def back_of(k, *adds):
        return input_back(k, dq, mine, got[k], k % 2, wq, wkv, list(adds))

    sent = [core_swap(back_of(k)) for k in (0, 2)]
    lead = back_of(1, grad_one, sent[0])
    rear = back_of(3, sent[1])
    dwi = after(dwi, lead)
    dwi_sum = (dwi[:, 0:units].astype(f32) + y_swap(dwi[:, units:]).astype(f32)).astype(bf16)
    out_both = jnp.concatenate([out_own, after(out_other, gate)], axis=0)
    layer_out = place(
        [core_swap(out_both), out_both], [order[0], order[2], order[1], order[3]], tokens
    )

    both = z_sum(table)
    dwo = x_sum(dwo_sum)
    dwi = x_sum(dwi_sum)
    came_both = x_swap(both) if pair else lax.psum(both.astype(f32), CTX) - both.astype(f32)
    dwq, dwk, dwv, dwp, small = last_call(both, came_both)
    sizes = [shard] * 6 + [units // fsdp_count, 192 // fsdp_count, 192 // fsdp_count]
    db_out, dg2, ds2, dg1, ds1, db_proj, db_in, db_query, db_value = [
        small[k, 0:size] for k, size in enumerate(sizes)
    ]
    from_rear, from_lead = after(y_swap(rear), came_both), y_swap(lead)
    lead_sum = (lead.astype(f32) + from_rear.astype(f32)).astype(bf16)
    grad_input = place([core_swap(lead_sum), lead_sum], order[0:2], tokens)
    from_lead = after(from_lead, layer_out, dwi, dwo.T, dwq, db_out, dg2, ds2, dg1, ds1, db_proj, db_in, db_query, db_value, grad_input)
    rear_sum = (rear.astype(f32) + from_lead.astype(f32)).astype(bf16)
    grad_input = place([core_swap(rear_sum), rear_sum], order[2:4], tokens, grad_input)
    return (
        layer_out,
        grad_input,
        dwq,
        db_query,
        dwk,
        dwv,
        db_value,
        dwp,
        db_proj,
        dg1,
        ds1,
        dwi,
        db_in,
        dwo.T,
        db_out,
        dg2,
        ds2,
    )


def solution(mesh):
    rows = P((FSDP, CTX), None)
    vector, unit = P(FSDP), P((TP, FSDP))
    column, row = P(FSDP, TP), P(TP, FSDP)
    return jax.shard_map(
        on_device,
        mesh=mesh,
        in_specs=(
            rows, rows, vector, P(FSDP, CTX, None), column, unit, column, column, unit, row,
            vector, vector, vector, column, unit, row, vector, vector, vector,
        ),
        out_specs=(
            rows, rows, column, unit, column, column, unit, row, vector, vector, vector,
            column, unit, row, vector, vector, vector,
        ),
        check_vma=False,
    )
```
